32 devices in a mesh: clip: 2 (over x), tm: 2 (over core), space: 8 (over z, y).
Axes of the slice: x: 2, y: 2, z: 4, core: 2. Of those that a mesh axis runs over, the one named last changes fastest.
Arguments:
- queue_latents: float32 [16, 2, 16, 128], P(('clip', 'tm'), None, None, 'space'), parts along dimension 0, may hold values from -6 to 6
- fresh_noise: float32 [6, 2, 16, 128], P('clip', None, None, 'space'), parts along dimension 0, may hold values from -6 to 6
- slot_levels: int32 [16], P('clip'), parts along dimension 0, may hold values from 1 to 15, as said below
- level_table: float32 [16, 8, 1152], replicated, may hold values from -2.5 to 2.5
- embed_weight: float32 [16, 1152], replicated, may hold values from -1.5 to 1.5
- spatial_in: bfloat16 [1152, 1728], replicated, may hold values from -0.1875 to 0.1875
- spatial_out: bfloat16 [576, 1152], replicated, may hold values from -0.25 to 0.25
- temporal_in: bfloat16 [1152, 1728], replicated, may hold values from -0.1875 to 0.1875
- temporal_out: bfloat16 [576, 1152], replicated, may hold values from -0.25 to 0.25
- norm_gains: float32 [4, 72], replicated, may hold values from 0.1 to 1.9
- final_weight: float32 [1152, 16], replicated, may hold values from -0.1875 to 0.1875
Outputs:
- next_queue: float32 [16, 2, 16, 128], P(('clip', 'tm'), None, None, 'space'), parts along dimension 0
- denoised: float32 [16, 2, 16, 128], P(('clip', 'tm'), None, None, 'space'), parts along dimension 0
The draws below stay inside these ranges and needn't reach their ends.
There are 2 independent parts, one for each index of `clip`. The reference program is written for one: setup_inputs(seed, part) draws one part's arguments, and reference() takes and returns one part's arrays. A program takes and returns all parts, laid end to end along the dimension named above; an argument that names none is the same for every part. Nothing has to cross between parts.
Inputs may be any that keep to these rules, and one draw needn't show every extreme that they name: `slot_levels`: strictly rising along the queue; neighbouring slots differ by 1 or 2; the last slot holds 15.
All inputs are finite; a program needn't handle non-finite values.
Results may differ from the reference program's by a relative error of at most 0.0023.
Values may be sent and summed in bfloat16 or wider, within the bound.
A program may use at most 128 MiB of HBM per device.

```python
import math
import jax
import jax.numpy as jnp
from jax import lax

D = 1152
HEADS = 8
HD = 72
CH = 16
QUEUE = 8
FRAMES = 2
STEPS = 3
LEVELS = 16
SPACE_TOK = 128


def draw_slot_levels(key, part):
    gap_key = jax.random.fold_in(key, 11)
    gaps = jax.random.randint(gap_key, (QUEUE - 1,), 1, 3).astype(jnp.int32)
    above = jnp.cumsum(gaps[::-1])[::-1]
    top = jnp.full((1,), LEVELS - 1, jnp.int32)
    return jnp.concatenate([LEVELS - 1 - above, top]).astype(jnp.int32)


def steps_of(rng, extent, cuts, smallest, high):
    factor_of, own = 1.0, jax.random.fold_in(rng, 6)
    for position, blocks in cuts:
        draws = jnp.exp(jax.random.uniform(jax.random.fold_in(own, position), (blocks,), jnp.float32, smallest / len(cuts), high / len(cuts)))
        factor_of = factor_of * jnp.repeat(draws, extent[position] // blocks).reshape([-1 if axis == position else 1 for axis in range(len(extent))])
    return factor_of


def bell_draw(rng, dims, deviation, most, cuts=(), kind=jnp.bfloat16):
    values = jax.random.normal(rng, dims, jnp.float32) * deviation
    if len(cuts) > 0:
        values = steps_of(rng, dims, cuts, -0.22, 0.18) * values
    return jnp.clip(values, min=-most, max=most).astype(kind)


def setup_inputs(seed: int = 0, part: int = 0) -> dict:
    key_list = jax.random.split(jax.random.key(seed), 12)
    part_splits = jax.random.split(jax.random.fold_in(key_list[11], part), 12)
    queue_latents = bell_draw(part_splits[0], (QUEUE, FRAMES, CH, SPACE_TOK), 1.0, 6.0, ((0, 2), (3, 8)), jnp.float32)
    fresh_noise = bell_draw(part_splits[1], (STEPS, FRAMES, CH, SPACE_TOK), 1.0, 6.0, ((3, 8),), jnp.float32)
    slot_levels = draw_slot_levels(jax.random.fold_in(jax.random.fold_in(key_list[11], part), 71), part)
    level_table = bell_draw(key_list[3], (LEVELS, 8, D), 0.5, 2.5, (), jnp.float32)
    embed_weight = bell_draw(key_list[4], (CH, D), CH ** -0.5, 1.5, (), jnp.float32)
    spatial_in = bell_draw(key_list[5], (D, 3 * HEADS * HD), D ** -0.5, 0.1875)
    spatial_out = bell_draw(key_list[6], (HEADS * HD, D), (HEADS * HD) ** -0.5, 0.25)
    temporal_in = bell_draw(key_list[7], (D, 3 * HEADS * HD), D ** -0.5, 0.1875)
    temporal_out = bell_draw(key_list[8], (HEADS * HD, D), (HEADS * HD) ** -0.5, 0.25)
    norm_gains = jnp.clip(1.0 + 0.18 * jax.random.normal(key_list[9], (4, HD), jnp.float32), 0.1, 1.9)
    final_weight = bell_draw(key_list[10], (D, CH), D ** -0.5, 0.1875, (), jnp.float32)
    return dict(queue_latents=queue_latents, fresh_noise=fresh_noise, slot_levels=slot_levels, level_table=level_table, embed_weight=embed_weight, spatial_in=spatial_in, spatial_out=spatial_out, temporal_in=temporal_in, temporal_out=temporal_out, norm_gains=norm_gains, final_weight=final_weight)


epsilon = 1e-06
highest = lax.Precision.HIGHEST

def sincos(positions, width):
    half = width // 2
    rates = jnp.exp(-jnp.log(10000.0) * jnp.arange(half).astype(jnp.float32) / half)
    angles = positions.astype(jnp.float32)[:, None] * rates[None, :]
    return jnp.concatenate([jnp.sin(angles), jnp.cos(angles)], axis=-1)

def stored(values):
    return lax.optimization_barrier(values.astype(jnp.bfloat16))

def layer_norm(values):
    centered = values - lax.optimization_barrier(jnp.mean(values, axis=-1, keepdims=True))
    return centered * lax.rsqrt(lax.optimization_barrier(jnp.mean(centered * centered, axis=-1, keepdims=True)) + epsilon)

def modulate(hidden, table, shift_row, scale_row):
    shift = table[:, shift_row][:, None, None, :]
    scale = table[:, scale_row][:, None, None, :]
    return layer_norm(hidden) * (1.0 + scale) + shift

def head_norm(values, gain):
    values = values.astype(jnp.float32)
    scaled = values * lax.rsqrt(lax.optimization_barrier(jnp.mean(values * values, axis=-1, keepdims=True)) + epsilon)
    return stored(scaled * gain)

def project_heads(normed, weight, gains, first):
    projected = stored(jnp.dot(normed.reshape(-1, D), weight, preferred_element_type=jnp.float32))
    projected = projected.reshape(QUEUE * FRAMES, SPACE_TOK, 3, HEADS, HD)
    queries = head_norm(projected[:, :, 0], gains[first])
    keys = head_norm(projected[:, :, 1], gains[first + 1])
    return (queries, keys, projected[:, :, 2])

def spatial_frame(pieces):
    queries, keys, values = pieces
    scores = jnp.einsum('the,rhe->htr', queries.astype(jnp.float32), keys.astype(jnp.float32)) / math.sqrt(HD)
    weights = jnp.exp(scores)
    totals = lax.optimization_barrier(jnp.sum(weights, axis=-1))
    rounded = stored(weights).astype(jnp.float32)
    mixed = jnp.einsum('htr,rhe->the', rounded, values.astype(jnp.float32))
    return stored(mixed / jnp.transpose(totals)[:, :, None])

def temporal_mix(queries, keys, values):
    scores = jnp.einsum('fthe,gthe->thfg', queries.astype(jnp.float32), keys.astype(jnp.float32)) / math.sqrt(HD)
    weights = jnp.exp(scores)
    totals = jnp.transpose(lax.optimization_barrier(jnp.sum(weights, axis=-1)), (2, 0, 1))
    rounded = stored(weights).astype(jnp.float32)
    mixed = jnp.einsum('thfg,gthe->fthe', rounded, values.astype(jnp.float32))
    return stored(mixed / totals[..., None])

def denoise(latents, table, token_pos, frame_pos, embed_weight, spatial_in, spatial_out, temporal_in, temporal_out, norm_gains, final_weight):
    hidden = jnp.einsum('qfcp,cd->qfpd', latents, embed_weight, precision=highest) + token_pos
    normed = stored(modulate(hidden, table, 0, 1))
    queries, keys, values = project_heads(normed, spatial_in, norm_gains, 0)
    mixed = lax.map(spatial_frame, (queries, keys, values))
    branch = jnp.dot(mixed.reshape(-1, HEADS * HD), spatial_out, preferred_element_type=jnp.float32)
    hidden = hidden + table[:, 2][:, None, None, :] * branch.reshape(hidden.shape) + frame_pos
    normed = stored(modulate(hidden, table, 3, 4))
    queries, keys, values = project_heads(normed, temporal_in, norm_gains, 2)
    mixed = temporal_mix(queries, keys, values)
    branch = jnp.dot(mixed.reshape(-1, HEADS * HD), temporal_out, preferred_element_type=jnp.float32)
    hidden = hidden + table[:, 5][:, None, None, :] * branch.reshape(hidden.shape)
    final = modulate(hidden, table, 6, 7)
    return jnp.einsum('qfpd,dc->qfcp', final, final_weight, precision=highest)

def reference(queue_latents, fresh_noise, slot_levels, level_table, embed_weight, spatial_in, spatial_out, temporal_in, temporal_out, norm_gains, final_weight):
    times = (slot_levels.astype(jnp.float32) + 1.0) / LEVELS
    before = jnp.concatenate([jnp.zeros((1,), jnp.float32), times[:-1]])
    stride = times - before
    table = level_table[slot_levels]
    token_pos = sincos(jnp.arange(SPACE_TOK), D)
    frame_pos = sincos(jnp.arange(QUEUE * FRAMES), D).reshape(QUEUE, FRAMES, 1, D)
    latents = queue_latents
    denoised = latents
    for step in range(STEPS):
        velocity = denoise(latents, table, token_pos, frame_pos, embed_weight, spatial_in, spatial_out, temporal_in, temporal_out, norm_gains, final_weight)
        denoised = latents - times[:, None, None, None] * velocity
        moved = latents - stride[:, None, None, None] * velocity
        latents = jnp.concatenate([moved[1:], fresh_noise[step][None]], axis=0)
    return (latents, denoised)
```

```python
import functools
import math

import jax
import jax.numpy as jnp
import numpy as np
from jax import lax
from jax.experimental import pallas as pl
from jax.experimental.pallas import tpu as pltpu
from jax.sharding import PartitionSpec as P

LEVELS = 16
epsilon = 1e-06
f32 = jnp.float32
bf16 = jnp.bfloat16


def sincos(count, width):
    half = width // 2
    rates = np.exp(-np.log(np.float32(10000.0)) * np.arange(half, dtype=np.float32) / np.float32(half))
    angles = np.arange(count, dtype=np.float32)[:, None] * rates[None, :].astype(np.float32)
    return np.concatenate([np.sin(angles), np.cos(angles)], axis=-1).astype(np.float32)


def layer_norm(values):
    centered = values - jnp.mean(values, axis=-1, keepdims=True)
    return centered * lax.rsqrt(jnp.mean(centered * centered, axis=-1, keepdims=True) + epsilon)


def split(values):
    high = values.astype(bf16)
    return high, (values - high.astype(f32)).astype(bf16)


def attend(projected, mixed, gains, heads, size, rows, piece, masked):
    inner = heads * size

    def head_normed(at, gain):
        values = projected[at : at + size, 0:rows].astype(f32)
        mean = jnp.sum(values * values, axis=0, keepdims=True) * (1.0 / size)
        return (values * lax.rsqrt(mean + epsilon) * gains[gain, :, 0:rows]).astype(bf16)

    if masked:
        row = lax.rem(lax.broadcasted_iota(jnp.int32, (piece, rows), 0), piece)
        own = row == lax.rem(lax.broadcasted_iota(jnp.int32, (piece, rows), 1), piece)
        keep = jnp.concatenate([jnp.where(own, 1.0, 0.0)] * (rows // piece), axis=0).astype(bf16)
    for at in range(0, inner, size):
        queries = head_normed(at, 0)
        keys = head_normed(inner + at, 1)
        values = projected[2 * inner + at : 2 * inner + at + size, 0:rows]
        scores = lax.dot_general(
            keys, queries, (((0,), (0,)), ((), ())), preferred_element_type=f32
        )
        weights = jnp.exp2(scores)
        rounded = weights.astype(bf16)
        if masked:
            totals = jnp.sum(weights.reshape(rows // piece, piece, rows), axis=0)
            totals = jnp.sum(jnp.where(own, totals, 0.0), axis=0, keepdims=True)
            rounded = rounded * keep
        else:
            totals = jnp.sum(weights, axis=0, keepdims=True)
        total = jnp.dot(values, rounded, preferred_element_type=f32)
        mixed[at : at + size, 0:rows] = (total * (1.0 / totals)).astype(bf16)


def nt_dot(left, right):
    return lax.dot_general(left, right, (((1,), (1,)), ((), ())), preferred_element_type=f32)


def kernel(
    cfg,
    levels,
    queue_latents,
    fresh_noise,
    embed,
    final_weight,
    gains,
    level_table_hbm,
    pos_hbm,
    spatial_in_hbm,
    spatial_out_hbm,
    temporal_in_hbm,
    temporal_out_hbm,
    out,
    start,
    noise,
    level_table,
    pos,
    gain_columns,
    frame_latents,
    token_latents,
    mix_send,
    mix_recv,
    table,
    hidden,
    normed,
    finals,
    embed_halves,
    final_halves,
    ends,
    landed,
    spatial_in,
    spatial_out,
    temporal_in,
    temporal_out,
    spatial_turned,
    temporal_turned,
    projected,
    mixed,
    weight_sem,
    start_send,
    start_recv,
    half_send,
    half_recv,
    mix_send_sem,
    mix_recv_sem,
    lat_send_sem,
    lat_recv_sem,
    end_send,
    end_recv,
):
    sections, shards, repeat = cfg["sections"], cfg["shards"], cfg["repeat"]
    slots, frames, steps = cfg["slots"], cfg["frames"], cfg["steps"]
    heads, size, piece = cfg["heads"], cfg["size"], cfg["piece"]
    channels, width = embed.shape
    lanes = piece * channels
    group = sections * shards
    own_frames = slots * frames // sections
    rows = slots * frames * piece
    slab = frames * piece
    tokens = group * piece
    most = max(rows, tokens)
    part_heads = heads // repeat
    part_width = part_heads * size
    section, shard = lax.axis_index("tm"), lax.axis_index("space")
    item = section * shards + shard
    frame = item // repeat
    own_slot = frame // frames

    weight_copies = [
        pltpu.make_async_copy(src, dst, weight_sem.at[n])
        for n, (src, dst) in enumerate(
            (
                (level_table_hbm, level_table),
                (pos_hbm, pos),
                (spatial_in_hbm, spatial_in),
                (spatial_out_hbm, spatial_out),
                (temporal_in_hbm, temporal_in),
                (temporal_out_hbm, temporal_out),
            )
        )
    ]
    for copy in weight_copies:
        copy.start()

    barrier = pltpu.get_barrier_semaphore()

    def greet(n, carry):
        other = lax.rem(item + n, group)
        pl.semaphore_signal(
            barrier,
            inc=1,
            device_id={"tm": other // shards, "space": lax.rem(other, shards)},
            device_id_type=pl.DeviceIdType.MESH,
        )
        return carry

    lax.fori_loop(1, group, greet, 0)

    def packed(latents, count):
        own_tokens = latents.shape[1]
        wide = sections * lanes
        token = lax.broadcasted_iota(jnp.int32, (own_tokens, wide), 0)
        lane = lax.broadcasted_iota(jnp.int32, (own_tokens, wide), 1)
        spread = jnp.dot(
            latents,
            jnp.where(token == lane // channels, 1.0, 0.0),
            precision=lax.Precision.HIGHEST,
            preferred_element_type=f32,
        )
        channel = lax.broadcasted_iota(jnp.int32, (channels, wide), 0)
        own = channel == lax.rem(lax.broadcasted_iota(jnp.int32, (channels, wide), 1), channels)
        return [
            jnp.sum(
                jnp.where(own, spread[n * channels : (n + 1) * channels], 0.0),
                axis=0,
                keepdims=True,
            )
            for n in range(count)
        ]

    own_tokens = sections * piece
    lines = packed(queue_latents[...].reshape(own_frames * channels, own_tokens), own_frames)
    for n, line in enumerate(lines):
        for t in range(sections):
            start[n, t] = line[:, t * lanes : (t + 1) * lanes]
    pl.semaphore_wait(barrier, group - 1)

    def remote(src, dst, send, recv, to_section, to_shard):
        return pltpu.make_async_remote_copy(
            src_ref=src,
            dst_ref=dst,
            send_sem=send,
            recv_sem=recv,
            device_id={"tm": to_section, "space": to_shard},
            device_id_type=pl.DeviceIdType.MESH,
        )

    def start_copy(n):
        other = lax.rem(shard + n, shards)
        return remote(
            start.at[other // repeat],
            frame_latents.at[:, shard],
            start_send.at[n],
            start_recv.at[n],
            section,
            other,
        )

    def half_copy(n):
        other = lax.rem(section + n, sections)
        return remote(
            start.at[:, other],
            token_latents.at[pl.ds(section * own_frames, own_frames)],
            half_send.at[n],
            half_recv.at[n],
            other,
            shard,
        )

    def mix_copy(n):
        other = lax.rem(item + n, group)
        return remote(
            mix_send.at[other],
            mix_recv.at[item],
            mix_send_sem.at[n],
            mix_recv_sem.at[n],
            other // shards,
            lax.rem(other, shards),
        )

    def lat_copy(n):
        other = lax.rem(item + n, group)
        return remote(
            token_latents.at[other // repeat],
            frame_latents.at[section, shard],
            lat_send_sem.at[n],
            lat_recv_sem.at[n],
            other // shards,
            lax.rem(other, shards),
        )

    def end_copy(n):
        other = lax.rem(section + n, sections)
        return remote(
            ends.at[:, pl.ds(other * own_frames, own_frames)],
            landed.at[:, section],
            end_send.at[n],
            end_recv.at[n],
            other,
            shard,
        )

    def start_all(make, count):
        def one(n, carry):
            make(n).start()
            return carry

        lax.fori_loop(1, count, one, 0)

    def wait_all(make, count):
        def one(n, carry):
            make(n).wait()
            return carry

        lax.fori_loop(1, count, one, 0)

    start_all(start_copy, shards)
    start_all(half_copy, sections)
    frame_latents[:, shard] = start[shard // repeat]
    token_latents[pl.ds(section * own_frames, own_frames)] = start[:, section]
    lines = packed(
        fresh_noise[...].reshape(steps * frames * channels, own_tokens), steps * frames
    )
    for n, line in enumerate(lines):
        for t in range(sections):
            noise[n // frames, n % frames, t] = line[:, t * lanes : (t + 1) * lanes]
    for n in range(4):
        factor = math.log2(math.e) / math.sqrt(size) if n % 2 == 0 else 1.0
        gain_columns[n] = jnp.broadcast_to(gains[n : n + 1, :] * factor, (most, size)).T

    piece_token = lax.broadcasted_iota(jnp.int32, (piece, lanes), 0)
    lane_token = lax.broadcasted_iota(jnp.int32, (piece, lanes), 1) // channels
    own_lanes = piece_token == lane_token
    high, low = split(embed[...])
    embed_halves[...] = jnp.concatenate(
        [high.astype(f32)] * (2 * piece) + [low.astype(f32)] * piece, axis=0
    ).astype(bf16)
    high, low = split(final_weight[...])
    final_halves[...] = jnp.concatenate(
        [high.astype(f32)] * piece + [low.astype(f32)] * piece, axis=0
    ).astype(bf16)

    for copy in weight_copies[:2]:
        copy.wait()
    for slot in range(slots):
        table[slot] = level_table[levels[slot]]
    wait_all(start_copy, shards)
    wait_all(half_copy, sections)
    weight_copies[2].wait()

    def embedded(packed):
        spread = jnp.concatenate(
            [jnp.where(own_lanes, jnp.broadcast_to(row, (piece, lanes)), 0.0) for row in packed],
            axis=0,
        )
        high, low = split(spread)
        return jnp.dot(
            jnp.concatenate([high, low, high], axis=1),
            embed_halves[...],
            preferred_element_type=f32,
        )

    def frame_row(n):
        home = n // piece
        return (home % sections * shards + home // sections) * piece + n % piece

    def step_body(step, carry):
        whole = embedded(
            [frame_latents[n // shards, n % shards] for n in range(group)]
        )
        shift = table[own_slot, 0:1, :]
        scale = 1.0 + table[own_slot, 1:2, :]
        for at in range(0, tokens, slab):
            part = whole[at : at + slab] + pos[at : at + slab, :]
            normed[at : at + slab, :] = (layer_norm(part) * scale + shift).astype(bf16)
        @pl.when(step == 0)
        def _():
            projected[0 : 3 * part_width, 0:tokens] = nt_dot(
                spatial_in[...], normed[0:tokens, :]
            ).astype(bf16)

        @pl.when(step > 0)
        def _():
            projected[0 : 3 * part_width, 0:tokens] = (
                jnp.dot(normed[0:tokens, :], spatial_turned[...], preferred_element_type=f32)
                .astype(bf16)
                .T
            )

        attend(
            projected, mixed, gain_columns.at[0:2], part_heads, size, tokens, piece, False
        )
        mix_send[...] = (
            mixed[0:part_width, 0:tokens].T.astype(f32).reshape(group, piece, part_width).astype(bf16)
        )
        start_all(mix_copy, group)
        mix_recv[item] = mix_send[item]

        token_pos = pos[pl.ds(pl.multiple_of(item * piece, piece), piece), :]
        base = embedded([token_latents[n] for n in range(slots * frames)])
        for n in range(slots * frames):
            hidden[n * piece : (n + 1) * piece, :] = (
                base[n * piece : (n + 1) * piece] + token_pos
            )
        @pl.when(step == 0)
        def _():
            for copy in weight_copies[3:]:
                copy.wait()
            temporal_turned[...] = temporal_in[...].T

        wait_all(mix_copy, group)
        branch = None
        arrived = mix_recv[...].astype(f32).reshape(
            slots * frames, repeat, piece, heads // repeat * size
        )
        for n in range(repeat):
            part = jnp.dot(
                arrived[:, n].reshape(rows, part_width).astype(bf16),
                spatial_out[n * part_width : (n + 1) * part_width, :],
                preferred_element_type=f32,
            )
            branch = part if branch is None else branch + part
        for slot in range(slots):
            at = slot * slab
            frame_pos = jnp.concatenate(
                [
                    jnp.broadcast_to(
                        pos[frame_row(slot * frames + n) : frame_row(slot * frames + n) + 1, :],
                        (piece, width),
                    )
                    for n in range(frames)
                ],
                axis=0,
            )
            part = (
                hidden[at : at + slab, :]
                + table[slot, 2:3, :] * branch[at : at + slab]
                + frame_pos
            )
            hidden[at : at + slab, :] = part
            normed[at : at + slab, :] = (
                layer_norm(part) * (1.0 + table[slot, 4:5, :]) + table[slot, 3:4, :]
            ).astype(bf16)
        projected[:, 0:rows] = (
            jnp.dot(normed[0:rows, :], temporal_turned[...], preferred_element_type=f32)
            .astype(bf16)
            .T
        )
        attend(projected, mixed, gain_columns.at[2:4], heads, size, rows, piece, True)
        branch = jnp.dot(mixed[:, 0:rows].T, temporal_out[...], preferred_element_type=f32)
        for slot in range(slots):
            at = slot * slab
            part = hidden[at : at + slab, :] + table[slot, 5:6, :] * branch[at : at + slab]
            final = layer_norm(part) * (1.0 + table[slot, 7:8, :]) + table[slot, 6:7, :]
            high, low = split(final)
            finals[at : at + slab, :] = high
            finals[rows + at : rows + at + slab, :] = low
        product = nt_dot(finals[...], final_halves[...])
        spread = (
            product[0:rows, 0:lanes] + product[0:rows, lanes : 2 * lanes] + product[rows:, 0:lanes]
        )
        for n in range(slots * frames):
            velocity = jnp.sum(
                jnp.where(own_lanes, spread[n * piece : (n + 1) * piece], 0.0),
                axis=0,
                keepdims=True,
            )
            slot = n // frames
            time = (levels[slot].astype(f32) + 1.0) / LEVELS
            before = (levels[slot - 1].astype(f32) + 1.0) / LEVELS if slot > 0 else 0.0
            old = token_latents[n]
            ends[1, n] = old - time * velocity
            if slot > 0:
                token_latents[n - frames] = old - (time - before) * velocity
        for n in range(frames):
            token_latents[(slots - 1) * frames + n] = noise[step, n, section]

        @pl.when(step < steps - 1)
        def _():
            start_all(lat_copy, group)
            frame_latents[section, shard] = token_latents[frame]

            @pl.when(step == 0)
            def _():
                spatial_turned[...] = spatial_in[...].T

            wait_all(lat_copy, group)

        return carry

    lax.fori_loop(0, steps, step_body, 0)
    ends[0] = token_latents[...]
    start_all(end_copy, sections)
    landed[:, section] = ends[:, pl.ds(section * own_frames, own_frames)]
    wait_all(end_copy, sections)
    out[...] = landed[...]


def unpack(frames, landed, next_queue, denoised):
    _, sections, own_frames, _, lanes = landed.shape
    channels = next_queue.shape[2]
    piece = lanes // channels
    own_tokens = sections * piece
    piece_token = lax.broadcasted_iota(jnp.int32, (piece, lanes), 0)
    own_lanes = piece_token == lax.broadcasted_iota(jnp.int32, (piece, lanes), 1) // channels
    spread = jnp.concatenate(
        [
            jnp.where(own_lanes, jnp.broadcast_to(landed[k, t, n], (piece, lanes)), 0.0)
            for k in range(2)
            for n in range(own_frames)
            for t in range(sections)
        ],
        axis=0,
    )
    pick = jnp.where(
        lax.broadcasted_iota(jnp.int32, (channels, lanes), 0)
        == lax.rem(lax.broadcasted_iota(jnp.int32, (channels, lanes), 1), channels),
        1.0,
        0.0,
    )
    result = lax.dot_general(
        pick,
        spread,
        (((1,), (1,)), ((), ())),
        precision=lax.Precision.HIGHEST,
        preferred_element_type=f32,
    )
    for k, target in enumerate((next_queue, denoised)):
        for n in range(own_frames):
            at = (k * own_frames + n) * own_tokens
            target[n // frames, n % frames] = result[:, at : at + own_tokens]


def per_device(
    queue_latents,
    fresh_noise,
    slot_levels,
    level_table,
    embed_weight,
    spatial_in,
    spatial_out,
    temporal_in,
    temporal_out,
    norm_gains,
    final_weight,
):
    blocks, frames, channels, tokens = queue_latents.shape
    steps, slots = fresh_noise.shape[0], slot_levels.shape[0]
    sections, shards = lax.axis_size("tm"), lax.axis_size("space")
    width, size = embed_weight.shape[1], norm_gains.shape[1]
    inner = spatial_out.shape[0]
    heads = inner // size
    group = sections * shards
    repeat = group // (slots * frames)
    piece = tokens // sections
    own_frames = blocks * frames
    assert repeat * slots * frames == group and heads % repeat == 0
    assert piece * sections == tokens and own_frames * sections == slots * frames
    lanes = piece * channels
    spatial_in, temporal_in, final = spatial_in.T, temporal_in.T, final_weight.T
    part = inner // repeat
    if repeat > 1:
        which = lax.rem(lax.axis_index("space"), repeat)
        spatial_in = lax.dynamic_index_in_dim(
            spatial_in.reshape(3, repeat, part, width), which, axis=1, keepdims=False
        ).reshape(3 * part, width)
    rows = max(slots * frames * piece, group * piece)
    cfg = dict(
        sections=sections,
        shards=shards,
        repeat=repeat,
        slots=slots,
        frames=frames,
        steps=steps,
        heads=heads,
        size=size,
        piece=piece,
    )
    vmem, anywhere = pl.BlockSpec(memory_space=pltpu.VMEM), pl.BlockSpec(memory_space=pl.ANY)
    dma = pltpu.SemaphoreType.DMA
    landed = pl.pallas_call(
        functools.partial(kernel, cfg),
        out_shape=jax.ShapeDtypeStruct((2, sections, own_frames, 1, lanes), f32),
        in_specs=[pl.BlockSpec(memory_space=pltpu.SMEM)] + [vmem] * 5 + [anywhere] * 6,
        out_specs=vmem,
        scratch_shapes=[
            pltpu.VMEM((own_frames, sections, 1, lanes), f32),
            pltpu.VMEM((steps, frames, sections, 1, lanes), f32),
            pltpu.VMEM(level_table.shape, f32),
            pltpu.VMEM((group * piece, width), f32),
            pltpu.VMEM((4, size, rows), f32),
            pltpu.VMEM((sections, shards, 1, lanes), f32),
            pltpu.VMEM((slots * frames, 1, lanes), f32),
            pltpu.VMEM((group, piece, part), bf16),
            pltpu.VMEM((group, piece, part), bf16),
            pltpu.VMEM((slots, level_table.shape[1], width), f32),
            pltpu.VMEM((slots * frames * piece, width), f32),
            pltpu.VMEM((rows, width), bf16),
            pltpu.VMEM((2 * slots * frames * piece, width), bf16),
            pltpu.VMEM((3 * lanes, width), bf16),
            pltpu.VMEM((2 * lanes, width), bf16),
            pltpu.VMEM((2, slots * frames, 1, lanes), f32),
            pltpu.VMEM((2, sections, own_frames, 1, lanes), f32),
            pltpu.VMEM(spatial_in.shape, bf16),
            pltpu.VMEM(spatial_out.shape, bf16),
            pltpu.VMEM(temporal_in.shape, bf16),
            pltpu.VMEM(temporal_out.shape, bf16),
            pltpu.VMEM(spatial_in.shape[::-1], bf16),
            pltpu.VMEM(temporal_in.shape[::-1], bf16),
            pltpu.VMEM((3 * inner, rows), bf16),
            pltpu.VMEM((inner, rows), bf16),
            dma((6,)),
            dma((shards,)),
            dma((shards,)),
            dma((sections,)),
            dma((sections,)),
            dma((group,)),
            dma((group,)),
            dma((group,)),
            dma((group,)),
            dma((sections,)),
            dma((sections,)),
        ],
        compiler_params=pltpu.CompilerParams(
            collective_id=0, has_side_effects=True, vmem_limit_bytes=60 * 1024 * 1024
        ),
    )(
        slot_levels,
        queue_latents,
        fresh_noise,
        embed_weight,
        final,
        norm_gains,
        level_table,
        jnp.asarray(
            sincos(group * piece, width)
            .reshape(shards, sections, piece, width)
            .swapaxes(0, 1)
            .reshape(group * piece, width)
        ),
        spatial_in,
        spatial_out,
        temporal_in,
        temporal_out,
    )
    return pl.pallas_call(
        functools.partial(unpack, frames),
        out_shape=(jax.ShapeDtypeStruct(queue_latents.shape, f32),) * 2,
        in_specs=[vmem],
        out_specs=(vmem, vmem),
    )(landed)


def solution(mesh):
    own = P(("clip", "tm"), None, None, "space")
    return jax.shard_map(
        per_device,
        mesh=mesh,
        in_specs=(own, P("clip", None, None, "space"), P("clip")) + (P(),) * 8,
        out_specs=(own, own),
        check_vma=False,
    )
```

```python
import functools
import math

import jax
import jax.numpy as jnp
import numpy as np
from jax import lax
from jax.experimental import pallas as pl
from jax.experimental.pallas import tpu as pltpu
from jax.sharding import PartitionSpec as P

LEVELS = 16
epsilon = 1e-06
f32 = jnp.float32
bf16 = jnp.bfloat16


def sincos(count, width):
    half = width // 2
    rates = np.exp(-np.log(np.float32(10000.0)) * np.arange(half, dtype=np.float32) / np.float32(half))
    angles = np.arange(count, dtype=np.float32)[:, None] * rates[None, :].astype(np.float32)
    return np.concatenate([np.sin(angles), np.cos(angles)], axis=-1).astype(np.float32)


def layer_norm(values):
    centered = values - jnp.mean(values, axis=-1, keepdims=True)
    return centered * lax.rsqrt(jnp.mean(centered * centered, axis=-1, keepdims=True) + epsilon)


def split(values):
    high = values.astype(bf16)
    return high, (values - high.astype(f32)).astype(bf16)


def attend(projected, mixed, gains, heads, size, rows, piece, masked, after):
    inner = heads * size

    def head_normed(at, gain):
        values = projected[at : at + size, 0:rows].astype(f32)
        mean = jnp.sum(values * values, axis=0, keepdims=True) * (1.0 / size)
        return (values * lax.rsqrt(mean + epsilon) * gains[gain, :, 0:rows]).astype(bf16)

    if masked:
        row = lax.rem(lax.broadcasted_iota(jnp.int32, (piece, rows), 0), piece)
        own = row == lax.rem(lax.broadcasted_iota(jnp.int32, (piece, rows), 1), piece)
        keep = jnp.concatenate([jnp.where(own, 1.0, 0.0)] * (rows // piece), axis=0).astype(bf16)
    for at in range(0, inner, size):
        queries = head_normed(at, 0)
        keys = head_normed(inner + at, 1)
        values = projected[2 * inner + at : 2 * inner + at + size, 0:rows]
        scores = lax.dot_general(
            keys, queries, (((0,), (0,)), ((), ())), preferred_element_type=f32
        )
        weights = jnp.exp2(scores)
        rounded = weights.astype(bf16)
        if masked:
            totals = jnp.sum(weights.reshape(rows // piece, piece, rows), axis=0)
            totals = jnp.sum(jnp.where(own, totals, 0.0), axis=0, keepdims=True)
            rounded = rounded * keep
        else:
            totals = jnp.sum(weights, axis=0, keepdims=True)
        total = jnp.dot(values, rounded, preferred_element_type=f32)
        mixed[at : at + size, 0:rows] = (total * (1.0 / totals)).astype(bf16)
        after(at + size)


def nt_dot(left, right):
    return lax.dot_general(left, right, (((1,), (1,)), ((), ())), preferred_element_type=f32)


def kernel(
    cfg,
    levels_hbm,
    queue_latents_hbm,
    fresh_noise_hbm,
    embed_hbm,
    final_weight_hbm,
    gains_hbm,
    level_table_hbm,
    pos_hbm,
    spatial_in_hbm,
    spatial_out_hbm,
    temporal_in_hbm,
    temporal_out_hbm,
    out,
    levels,
    queue_latents,
    fresh_noise,
    embed,
    final_weight,
    gains,
    start,
    noise,
    level_table,
    pos,
    gain_columns,
    frame_latents,
    token_latents,
    mix_send,
    mix_recv,
    table,
    hidden,
    normed,
    finals,
    embed_halves,
    final_halves,
    ends,
    landed,
    spatial_in,
    spatial_out,
    temporal_in,
    temporal_out,
    temporal_turned,
    centered_pos,
    centered_embed,
    folded_embed,
    folded_pos,
    folded_shift,
    folding,
    projected,
    mixed,
    weight_sem,
    start_send,
    start_recv,
    half_send,
    half_recv,
    mix_send_sem,
    mix_recv_sem,
    lat_send_sem,
    lat_recv_sem,
    end_send,
    end_recv,
):
    sections, shards, repeat = cfg["sections"], cfg["shards"], cfg["repeat"]
    slots, frames, steps = cfg["slots"], cfg["frames"], cfg["steps"]
    heads, size, piece = cfg["heads"], cfg["size"], cfg["piece"]
    channels, width = embed.shape
    lanes = piece * channels
    group = sections * shards
    own_frames = slots * frames // sections
    rows = slots * frames * piece
    slab = frames * piece
    tokens = group * piece
    most = max(rows, tokens)
    part_heads = heads // repeat
    part_width = part_heads * size
    section, shard = lax.axis_index("tm"), lax.axis_index("space")
    item = section * shards + shard
    frame = item // repeat
    own_slot = frame // frames

    def flip(index, code):
        bit, other = 1, index
        while bit <= code:
            if code & bit:
                other = other + bit - 2 * bit * lax.rem(index // bit, 2)
            bit *= 2
        return other

    def partner(n):
        return flip(section, n % sections), flip(shard, n // sections)

    partners = range(group - 1, 0, -1)
    barrier = pltpu.get_barrier_semaphore()
    for n in partners:
        to_section, to_shard = partner(n)
        pl.semaphore_signal(
            barrier,
            inc=1,
            device_id={"tm": to_section, "space": to_shard},
            device_id_type=pl.DeviceIdType.MESH,
        )

    input_copies = [
        pltpu.make_async_copy(src, dst, weight_sem.at[n])
        for n, (src, dst) in enumerate(
            (
                (queue_latents_hbm, queue_latents),
                (levels_hbm, levels),
                (embed_hbm, embed),
                (level_table_hbm, level_table),
                (pos_hbm, pos),
                (spatial_in_hbm, spatial_in),
                (gains_hbm, gains),
                (fresh_noise_hbm, fresh_noise),
                (final_weight_hbm, final_weight),
                (temporal_in_hbm, temporal_in),
                (spatial_out_hbm, spatial_out),
                (temporal_out_hbm, temporal_out),
            )
        )
    ]
    for n in (0, 1, 2, 6, 7, 8, 3, 4, 5, 9, 10, 11):
        input_copies[n].start()

    def packed(latents, count):
        own_tokens = latents.shape[1]
        wide = sections * lanes
        token = lax.broadcasted_iota(jnp.int32, (own_tokens, wide), 0)
        lane = lax.broadcasted_iota(jnp.int32, (own_tokens, wide), 1)
        spread = jnp.dot(
            latents,
            jnp.where(token == lane // channels, 1.0, 0.0),
            precision=lax.Precision.HIGHEST,
            preferred_element_type=f32,
        )
        channel = lax.broadcasted_iota(jnp.int32, (channels, wide), 0)
        own = channel == lax.rem(lax.broadcasted_iota(jnp.int32, (channels, wide), 1), channels)
        return [
            jnp.sum(
                jnp.where(own, spread[n * channels : (n + 1) * channels], 0.0),
                axis=0,
                keepdims=True,
            )
            for n in range(count)
        ]

    own_tokens = sections * piece
    input_copies[0].wait()
    lines = packed(queue_latents[...].reshape(own_frames * channels, own_tokens), own_frames)
    for n, line in enumerate(lines):
        for t in range(sections):
            start[n, t] = line[:, t * lanes : (t + 1) * lanes]
    pl.semaphore_wait(barrier, group - 1)

    def remote(src, dst, send, recv, to_section, to_shard):
        return pltpu.make_async_remote_copy(
            src_ref=src,
            dst_ref=dst,
            send_sem=send,
            recv_sem=recv,
            device_id={"tm": to_section, "space": to_shard},
            device_id_type=pl.DeviceIdType.MESH,
        )

    def start_copy(n):
        other = flip(shard, n)
        return remote(
            start.at[other // repeat],
            frame_latents.at[:, shard],
            start_send.at[n],
            start_recv.at[n],
            section,
            other,
        )

    def half_copy(n):
        other = flip(section, n)
        return remote(
            start.at[:, other],
            token_latents.at[pl.ds(section * own_frames, own_frames)],
            half_send.at[n],
            half_recv.at[n],
            other,
            shard,
        )

    def mix_copy(n, start, end):
        to_section, to_shard = partner(n)
        late = 1 if start > 0 else 0
        return remote(
            mix_send.at[to_section * shards + to_shard, :, start:end],
            mix_recv.at[item, :, start:end],
            mix_send_sem.at[late, n],
            mix_recv_sem.at[late, n],
            to_section,
            to_shard,
        )

    def lat_copy(n):
        to_section, to_shard = partner(n)
        return remote(
            token_latents.at[(to_section * shards + to_shard) // repeat],
            frame_latents.at[section, shard],
            lat_send_sem.at[n],
            lat_recv_sem.at[n],
            to_section,
            to_shard,
        )

    def end_copy(n):
        other = flip(section, n)
        return remote(
            ends.at[:, pl.ds(other * own_frames, own_frames)],
            landed.at[:, section],
            end_send.at[n],
            end_recv.at[n],
            other,
            shard,
        )

    def start_all(make, count):
        for n in range(count - 1, 0, -1):
            make(n).start()

    def wait_all(make, count):
        for n in range(count - 1, 0, -1):
            make(n).wait()

    start_all(start_copy, shards)
    start_all(half_copy, sections)
    frame_latents[:, shard] = start[shard // repeat]
    token_latents[pl.ds(section * own_frames, own_frames)] = start[:, section]
    for copy in input_copies[1:5]:
        copy.wait()
    for slot in range(slots):
        table[slot] = level_table[levels[slot]]
    shift = table[own_slot, 0:1, :]
    scale = 1.0 + table[own_slot, 1:2, :]
    part_rows = 3 * part_width
    part = pos[0:tokens, :]
    part = part - jnp.mean(part, axis=-1, keepdims=True)
    centered_pos[...] = part.T
    folding[0:tokens, :] = (part * scale).astype(bf16)
    part = embed[...] - jnp.mean(embed[...], axis=-1, keepdims=True)
    high, low = split(jnp.concatenate([part] * piece, axis=0).T)
    centered_embed[...] = jnp.concatenate([high, high, low], axis=1)
    at = tokens
    for values in split(part * scale) + split(jnp.broadcast_to(shift, (channels, width))):
        folding[at : at + channels, :] = values
        at += channels
    input_copies[6].wait()
    for n in range(4):
        factor = math.log2(math.e) / math.sqrt(size) if n % 2 == 0 else 1.0
        gain_columns[n] = jnp.broadcast_to(gains[n : n + 1, :] * factor, (most, size)).T
    input_copies[5].wait()
    row = lax.broadcasted_iota(jnp.int32, (4 * channels, lanes + tokens), 0)
    lane = lax.broadcasted_iota(jnp.int32, (4 * channels, lanes + tokens), 1)
    of_embed = (row < 2 * channels) & (lane < lanes)
    of_embed = of_embed & (lax.rem(row, channels) == lax.rem(lane, channels))
    of_shift = (row >= 2 * channels) & (lane >= lanes) & (lax.rem(row, channels) == 0)
    pick = jnp.where(of_embed | of_shift, 1.0, 0.0).astype(bf16)
    for at in range(0, part_rows, part_width):
        both = nt_dot(spatial_in[at : at + part_width, :], folding[...])
        folded_pos[at : at + part_width, :] = both[:, 0:tokens]
        high, low = split(both[:, tokens:])
        both = jnp.dot(high, pick, preferred_element_type=f32) + jnp.dot(
            low, pick, preferred_element_type=f32
        )
        high, low = split(both[:, 0:lanes])
        folded_embed[at : at + part_width, :] = jnp.concatenate([high, high, low], axis=1)
        folded_shift[at : at + part_width, :] = both[:, lanes:]
    piece_token = lax.broadcasted_iota(jnp.int32, (piece, lanes), 0)
    lane_token = lax.broadcasted_iota(jnp.int32, (piece, lanes), 1) // channels
    own_lanes = piece_token == lane_token
    high, low = split(embed[...])
    embed_halves[...] = jnp.concatenate(
        [high.astype(f32)] * (2 * piece) + [low.astype(f32)] * piece, axis=0
    ).astype(bf16)
    wait_all(start_copy, shards)
    wait_all(half_copy, sections)

    def spread_out(packed):
        spread = jnp.concatenate(
            [jnp.where(own_lanes, jnp.broadcast_to(row, (piece, lanes)), 0.0) for row in packed],
            axis=0,
        )
        high, low = split(spread)
        return jnp.concatenate([high, low, high], axis=1)

    def frame_row(n):
        home = n // piece
        return (home % sections * shards + home // sections) * piece + n % piece

    def step_body(step, carry):
        spread = spread_out([frame_latents[n // shards, n % shards] for n in range(group)])
        squares = None
        chunk = width // 4
        for at in range(0, width, chunk):
            part = nt_dot(centered_embed[at : at + chunk, :], spread)
            part = part + centered_pos[at : at + chunk, :]
            part = jnp.sum(part * part, axis=0, keepdims=True)
            squares = part if squares is None else squares + part
        factor = lax.rsqrt(squares * (1.0 / width) + epsilon)
        for at in range(0, part_rows, part_width):
            part = nt_dot(folded_embed[at : at + part_width, :], spread)
            part = part + folded_pos[at : at + part_width, :]
            projected[at : at + part_width, 0:tokens] = (
                part * factor + folded_shift[at : at + part_width, :]
            ).astype(bf16)

        sent = [0]

        def send(ready):
            start = sent[0]
            end = part_width if ready == part_width else ready // 128 * 128
            if end == part_width:
                mix_send[:, :, start:end] = (
                    mixed[start:end, 0:tokens]
                    .T.astype(f32)
                    .reshape(group, piece, end - start)
                    .astype(bf16)
                )
                for n in partners:
                    mix_copy(n, start, end).start()
                sent[0] = end
                spans.append((start, end))

        spans = []
        attend(
            projected, mixed, gain_columns.at[0:2], part_heads, size, tokens, piece, False, send
        )
        mix_recv[item] = mix_send[item]

        token_pos = pos[pl.ds(pl.multiple_of(item * piece, piece), piece), :]
        base = jnp.dot(
            spread_out([token_latents[n] for n in range(slots * frames)]),
            embed_halves[...],
            preferred_element_type=f32,
        )
        for n in range(slots * frames):
            hidden[n * piece : (n + 1) * piece, :] = (
                base[n * piece : (n + 1) * piece] + token_pos
            )
        @pl.when(step == 0)
        def _():
            for copy in input_copies[9:]:
                copy.wait()
            temporal_turned[...] = temporal_in[...].T
            for copy in input_copies[7:9]:
                copy.wait()
            lines = packed(
                fresh_noise[...].reshape(steps * frames * channels, own_tokens), steps * frames
            )
            for n, line in enumerate(lines):
                for t in range(sections):
                    noise[n // frames, n % frames, t] = line[:, t * lanes : (t + 1) * lanes]
            high, low = split(final_weight[...])
            final_halves[...] = jnp.concatenate(
                [high.astype(f32)] * piece + [low.astype(f32)] * piece, axis=0
            ).astype(bf16)

        for start, end in spans:
            for n in partners:
                mix_copy(n, start, end).wait()
        branch = None
        arrived = mix_recv[...].astype(f32).reshape(
            slots * frames, repeat, piece, heads // repeat * size
        )
        for n in range(repeat):
            part = jnp.dot(
                arrived[:, n].reshape(rows, part_width).astype(bf16),
                spatial_out[n * part_width : (n + 1) * part_width, :],
                preferred_element_type=f32,
            )
            branch = part if branch is None else branch + part
        for slot in range(slots):
            at = slot * slab
            frame_pos = jnp.concatenate(
                [
                    jnp.broadcast_to(
                        pos[frame_row(slot * frames + n) : frame_row(slot * frames + n) + 1, :],
                        (piece, width),
                    )
                    for n in range(frames)
                ],
                axis=0,
            )
            part = (
                hidden[at : at + slab, :]
                + table[slot, 2:3, :] * branch[at : at + slab]
                + frame_pos
            )
            hidden[at : at + slab, :] = part
            normed[at : at + slab, :] = (
                layer_norm(part) * (1.0 + table[slot, 4:5, :]) + table[slot, 3:4, :]
            ).astype(bf16)
        projected[:, 0:rows] = (
            jnp.dot(normed[0:rows, :], temporal_turned[...], preferred_element_type=f32)
            .astype(bf16)
            .T
        )
        attend(
            projected, mixed, gain_columns.at[2:4], heads, size, rows, piece, True, lambda _: None
        )
        branch = jnp.dot(mixed[:, 0:rows].T, temporal_out[...], preferred_element_type=f32)
        for slot in range(slots):
            at = slot * slab
            part = hidden[at : at + slab, :] + table[slot, 5:6, :] * branch[at : at + slab]
            final = layer_norm(part) * (1.0 + table[slot, 7:8, :]) + table[slot, 6:7, :]
            high, low = split(final)
            finals[at : at + slab, :] = high
            finals[rows + at : rows + at + slab, :] = low
        product = nt_dot(finals[...], final_halves[...])
        spread = (
            product[0:rows, 0:lanes] + product[0:rows, lanes : 2 * lanes] + product[rows:, 0:lanes]
        )
        for n in range(slots * frames):
            velocity = jnp.sum(
                jnp.where(own_lanes, spread[n * piece : (n + 1) * piece], 0.0),
                axis=0,
                keepdims=True,
            )
            slot = n // frames
            time = (levels[slot].astype(f32) + 1.0) / LEVELS
            before = (levels[slot - 1].astype(f32) + 1.0) / LEVELS if slot > 0 else 0.0
            old = token_latents[n]
            ends[1, n] = old - time * velocity
            if slot > 0:
                token_latents[n - frames] = old - (time - before) * velocity
        for n in range(frames):
            token_latents[(slots - 1) * frames + n] = noise[step, n, section]

        @pl.when(step < steps - 1)
        def _():
            start_all(lat_copy, group)
            frame_latents[section, shard] = token_latents[frame]
            wait_all(lat_copy, group)

        return carry

    lax.fori_loop(0, steps, step_body, 0)
    ends[0] = token_latents[...]
    start_all(end_copy, sections)
    landed[:, section] = ends[:, pl.ds(section * own_frames, own_frames)]
    wait_all(end_copy, sections)
    out[...] = landed[...]


def unpack(frames, landed, next_queue, denoised):
    _, sections, own_frames, _, lanes = landed.shape
    channels = next_queue.shape[2]
    piece = lanes // channels
    own_tokens = sections * piece
    piece_token = lax.broadcasted_iota(jnp.int32, (piece, lanes), 0)
    own_lanes = piece_token == lax.broadcasted_iota(jnp.int32, (piece, lanes), 1) // channels
    spread = jnp.concatenate(
        [
            jnp.where(own_lanes, jnp.broadcast_to(landed[k, t, n], (piece, lanes)), 0.0)
            for k in range(2)
            for n in range(own_frames)
            for t in range(sections)
        ],
        axis=0,
    )
    pick = jnp.where(
        lax.broadcasted_iota(jnp.int32, (channels, lanes), 0)
        == lax.rem(lax.broadcasted_iota(jnp.int32, (channels, lanes), 1), channels),
        1.0,
        0.0,
    )
    result = lax.dot_general(
        pick,
        spread,
        (((1,), (1,)), ((), ())),
        precision=lax.Precision.HIGHEST,
        preferred_element_type=f32,
    )
    for k, target in enumerate((next_queue, denoised)):
        for n in range(own_frames):
            at = (k * own_frames + n) * own_tokens
            target[n // frames, n % frames] = result[:, at : at + own_tokens]


def per_device(
    queue_latents,
    fresh_noise,
    slot_levels,
    level_table,
    embed_weight,
    spatial_in,
    spatial_out,
    temporal_in,
    temporal_out,
    norm_gains,
    final_weight,
):
    blocks, frames, channels, tokens = queue_latents.shape
    steps, slots = fresh_noise.shape[0], slot_levels.shape[0]
    sections, shards = lax.axis_size("tm"), lax.axis_size("space")
    width, size = embed_weight.shape[1], norm_gains.shape[1]
    inner = spatial_out.shape[0]
    heads = inner // size
    group = sections * shards
    repeat = group // (slots * frames)
    piece = tokens // sections
    own_frames = blocks * frames
    assert repeat * slots * frames == group and heads % repeat == 0
    assert piece * sections == tokens and own_frames * sections == slots * frames
    lanes = piece * channels
    spatial_in, temporal_in, final = spatial_in.T, temporal_in.T, final_weight.T
    part = inner // repeat
    if repeat > 1:
        which = lax.rem(lax.axis_index("space"), repeat)
        spatial_in = lax.dynamic_index_in_dim(
            spatial_in.reshape(3, repeat, part, width), which, axis=1, keepdims=False
        ).reshape(3 * part, width)
    rows = max(slots * frames * piece, group * piece)
    cfg = dict(
        sections=sections,
        shards=shards,
        repeat=repeat,
        slots=slots,
        frames=frames,
        steps=steps,
        heads=heads,
        size=size,
        piece=piece,
    )
    vmem, anywhere = pl.BlockSpec(memory_space=pltpu.VMEM), pl.BlockSpec(memory_space=pl.ANY)
    dma = pltpu.SemaphoreType.DMA
    landed = pl.pallas_call(
        functools.partial(kernel, cfg),
        out_shape=jax.ShapeDtypeStruct((2, sections, own_frames, 1, lanes), f32),
        in_specs=[anywhere] * 12,
        out_specs=vmem,
        scratch_shapes=[
            pltpu.SMEM(slot_levels.shape, jnp.int32),
            pltpu.VMEM(queue_latents.shape, f32),
            pltpu.VMEM(fresh_noise.shape, f32),
            pltpu.VMEM(embed_weight.shape, f32),
            pltpu.VMEM(final.shape, f32),
            pltpu.VMEM(norm_gains.shape, f32),
            pltpu.VMEM((own_frames, sections, 1, lanes), f32),
            pltpu.VMEM((steps, frames, sections, 1, lanes), f32),
            pltpu.VMEM(level_table.shape, f32),
            pltpu.VMEM((group * piece, width), f32),
            pltpu.VMEM((4, size, rows), f32),
            pltpu.VMEM((sections, shards, 1, lanes), f32),
            pltpu.VMEM((slots * frames, 1, lanes), f32),
            pltpu.VMEM((group, piece, part), bf16),
            pltpu.VMEM((group, piece, part), bf16),
            pltpu.VMEM((slots, level_table.shape[1], width), f32),
            pltpu.VMEM((slots * frames * piece, width), f32),
            pltpu.VMEM((rows, width), bf16),
            pltpu.VMEM((2 * slots * frames * piece, width), bf16),
            pltpu.VMEM((3 * lanes, width), bf16),
            pltpu.VMEM((2 * lanes, width), bf16),
            pltpu.VMEM((2, slots * frames, 1, lanes), f32),
            pltpu.VMEM((2, sections, own_frames, 1, lanes), f32),
            pltpu.VMEM(spatial_in.shape, bf16),
            pltpu.VMEM(spatial_out.shape, bf16),
            pltpu.VMEM(temporal_in.shape, bf16),
            pltpu.VMEM(temporal_out.shape, bf16),
            pltpu.VMEM(temporal_in.shape[::-1], bf16),
            pltpu.VMEM((width, group * piece), f32),
            pltpu.VMEM((width, 3 * lanes), bf16),
            pltpu.VMEM((3 * part, 3 * lanes), bf16),
            pltpu.VMEM((3 * part, group * piece), f32),
            pltpu.VMEM((3 * part, group * piece), f32),
            pltpu.VMEM((group * piece + 4 * channels, width), bf16),
            pltpu.VMEM((3 * inner, rows), bf16),
            pltpu.VMEM((inner, rows), bf16),
            dma((12,)),
            dma((shards,)),
            dma((shards,)),
            dma((sections,)),
            dma((sections,)),
            dma((2, group)),
            dma((2, group)),
            dma((group,)),
            dma((group,)),
            dma((sections,)),
            dma((sections,)),
        ],
        compiler_params=pltpu.CompilerParams(
            collective_id=0, has_side_effects=True, vmem_limit_bytes=60 * 1024 * 1024
        ),
    )(
        slot_levels,
        queue_latents,
        fresh_noise,
        embed_weight,
        final,
        norm_gains,
        level_table,
        jnp.asarray(
            sincos(group * piece, width)
            .reshape(shards, sections, piece, width)
            .swapaxes(0, 1)
            .reshape(group * piece, width)
        ),
        spatial_in,
        spatial_out,
        temporal_in,
        temporal_out,
    )
    return pl.pallas_call(
        functools.partial(unpack, frames),
        out_shape=(jax.ShapeDtypeStruct(queue_latents.shape, f32),) * 2,
        in_specs=[vmem],
        out_specs=(vmem, vmem),
    )(landed)


def solution(mesh):
    own = P(("clip", "tm"), None, None, "space")
    return jax.shard_map(
        per_device,
        mesh=mesh,
        in_specs=(own, P("clip", None, None, "space"), P("clip")) + (P(),) * 8,
        out_specs=(own, own),
        check_vma=False,
    )
```

```python
import functools
import math

import jax
import jax.numpy as jnp
import numpy as np
from jax import lax
from jax.experimental import pallas as pl
from jax.experimental.pallas import tpu as pltpu
from jax.sharding import PartitionSpec as P

LEVELS = 16
epsilon = 1e-06
f32 = jnp.float32
bf16 = jnp.bfloat16


def sincos(count, width):
    half = width // 2
    rates = np.exp(-np.log(np.float32(10000.0)) * np.arange(half, dtype=np.float32) / np.float32(half))
    angles = np.arange(count, dtype=np.float32)[:, None] * rates[None, :].astype(np.float32)
    return np.concatenate([np.sin(angles), np.cos(angles)], axis=-1).astype(np.float32)


def layer_norm(values):
    centered = values - jnp.mean(values, axis=-1, keepdims=True)
    return centered * lax.rsqrt(jnp.mean(centered * centered, axis=-1, keepdims=True) + epsilon)


def split(values):
    high = values.astype(bf16)
    return high, (values - high.astype(f32)).astype(bf16)


def attend(projected, mixed, gains, heads, size, rows, keys_count, piece, masked):
    inner = heads * size

    def head_normed(at, gain, count):
        values = projected[at : at + size, 0:count].astype(f32)
        mean = jnp.sum(values * values, axis=0, keepdims=True) * (1.0 / size)
        return (values * lax.rsqrt(mean + epsilon) * gains[gain, :, 0:count]).astype(bf16)

    half = rows // 2
    if masked:
        row = lax.rem(lax.broadcasted_iota(jnp.int32, (piece, rows), 0), piece)
        own = row == lax.rem(lax.broadcasted_iota(jnp.int32, (piece, rows), 1), piece)
        keep = jnp.concatenate([jnp.where(own, 1.0, 0.0)] * (rows // piece), axis=0).astype(bf16)
    elif keys_count > rows:
        left = lax.broadcasted_iota(jnp.int32, (half, rows), 1) < half
        keep_left = jnp.where(left, 1.0, 0.0).astype(bf16)
        keep_right = jnp.where(left, 0.0, 1.0).astype(bf16)
    for at in range(0, inner, size):
        queries = head_normed(at, 0, rows)
        keys = head_normed(inner + at, 1, keys_count)
        values = projected[2 * inner + at : 2 * inner + at + size, 0:keys_count]
        scores = lax.dot_general(
            keys, queries, (((0,), (0,)), ((), ())), preferred_element_type=f32
        )
        if keys_count > rows:
            scores = jnp.concatenate(
                [
                    jnp.where(left, scores[n : n + half], scores[n + half : n + rows])
                    for n in range(0, keys_count, rows)
                ],
                axis=0,
            )
        weights = jnp.exp2(scores)
        rounded = weights.astype(bf16)
        if masked:
            totals = jnp.sum(weights.reshape(rows // piece, piece, rows), axis=0)
            totals = jnp.sum(jnp.where(own, totals, 0.0), axis=0, keepdims=True)
            rounded = rounded * keep
        else:
            totals = jnp.sum(weights, axis=0, keepdims=True)
            if keys_count > rows:
                parts = []
                for n in range(0, rows, half):
                    part = rounded[n : n + half]
                    parts += [part * keep_left, part * keep_right]
                rounded = jnp.concatenate(parts, axis=0)
        total = jnp.dot(values, rounded, preferred_element_type=f32)
        mixed[at : at + size, 0:rows] = (total * (1.0 / totals)).astype(bf16)


def nt_dot(left, right):
    return lax.dot_general(left, right, (((1,), (1,)), ((), ())), preferred_element_type=f32)


def kernel(
    cfg,
    levels_hbm,
    queue_latents_hbm,
    fresh_noise_hbm,
    embed_hbm,
    final_weight_hbm,
    gains_hbm,
    level_table_hbm,
    pos_hbm,
    spatial_in_hbm,
    spatial_out_hbm,
    temporal_in_hbm,
    temporal_out_hbm,
    out,
    levels,
    queue_latents,
    fresh_noise,
    embed,
    final_weight,
    gains,
    start,
    noise,
    level_table,
    pos,
    gain_columns,
    frame_latents,
    token_latents,
    mix_send,
    mix_recv,
    table,
    hidden,
    normed,
    finals,
    embed_halves,
    final_halves,
    ends,
    landed,
    spatial_in,
    spatial_out,
    temporal_in,
    temporal_out,
    temporal_turned,
    centered_pos,
    centered_embed,
    folded_embed,
    folded_pos,
    folded_shift,
    folding,
    projected,
    mixed,
    weight_sem,
    start_send,
    start_recv,
    half_send,
    half_recv,
    mix_send_sem,
    mix_recv_sem,
    lat_send_sem,
    lat_recv_sem,
    end_send,
    end_recv,
):
    sections, shards, repeat = cfg["sections"], cfg["shards"], cfg["repeat"]
    halves = cfg["halves"]
    slots, frames, steps = cfg["slots"], cfg["frames"], cfg["steps"]
    heads, size, piece = cfg["heads"], cfg["size"], cfg["piece"]
    channels, width = embed.shape
    lanes = piece * channels
    group = sections * shards
    own_frames = slots * frames // sections
    rows = slots * frames * piece
    slab = frames * piece
    tokens = group * piece
    team_shards = shards // halves
    team = sections * team_shards
    asked = tokens // halves
    query_rows, key_rows = halves * asked, halves * tokens
    most = max(rows, key_rows)
    part_heads = heads // repeat
    part_width = part_heads * size
    section, shard = lax.axis_index("tm"), lax.axis_index("space")
    item = section * shards + shard
    half = shard // team_shards

    def member_of(to_section, to_shard):
        return to_section * team_shards + lax.rem(to_shard, team_shards)

    def first_of(to_section, to_shard):
        return member_of(to_section, to_shard) * halves // repeat

    member = member_of(section, shard)
    frame = first_of(section, shard)
    own_slot = frame // frames
    token_order = [
        (t, lax.rem(half + n, halves) * team_shards)
        for n in range(halves)
        for t in range(sections)
    ]

    def flip(index, code):
        bit, other = 1, index
        while bit <= code:
            if code & bit:
                other = other + bit - 2 * bit * lax.rem(index // bit, 2)
            bit *= 2
        return other

    def partner(n):
        return flip(section, n % sections), flip(shard, n // sections)

    partners = range(group - 1, 0, -1)
    barrier = pltpu.get_barrier_semaphore()
    for n in partners:
        to_section, to_shard = partner(n)
        pl.semaphore_signal(
            barrier,
            inc=1,
            device_id={"tm": to_section, "space": to_shard},
            device_id_type=pl.DeviceIdType.MESH,
        )

    input_copies = [
        pltpu.make_async_copy(src, dst, weight_sem.at[n])
        for n, (src, dst) in enumerate(
            (
                (queue_latents_hbm, queue_latents),
                (levels_hbm, levels),
                (embed_hbm, embed),
                (level_table_hbm, level_table),
                (pos_hbm, pos),
                (spatial_in_hbm, spatial_in),
                (gains_hbm, gains),
                (fresh_noise_hbm, fresh_noise),
                (final_weight_hbm, final_weight),
                (temporal_in_hbm, temporal_in),
                (spatial_out_hbm, spatial_out),
                (temporal_out_hbm, temporal_out),
            )
        )
    ]
    for n in (0, 1, 2, 6, 7, 8, 3, 4, 5, 9, 10, 11):
        input_copies[n].start()

    def packed(latents, count):
        own_tokens = latents.shape[1]
        wide = sections * lanes
        token = lax.broadcasted_iota(jnp.int32, (own_tokens, wide), 0)
        lane = lax.broadcasted_iota(jnp.int32, (own_tokens, wide), 1)
        spread = jnp.dot(
            latents,
            jnp.where(token == lane // channels, 1.0, 0.0),
            precision=lax.Precision.HIGHEST,
            preferred_element_type=f32,
        )
        channel = lax.broadcasted_iota(jnp.int32, (channels, wide), 0)
        own = channel == lax.rem(lax.broadcasted_iota(jnp.int32, (channels, wide), 1), channels)
        return [
            jnp.sum(
                jnp.where(own, spread[n * channels : (n + 1) * channels], 0.0),
                axis=0,
                keepdims=True,
            )
            for n in range(count)
        ]

    own_tokens = sections * piece
    input_copies[0].wait()
    lines = packed(queue_latents[...].reshape(own_frames * channels, own_tokens), own_frames)
    for n, line in enumerate(lines):
        for t in range(sections):
            start[n, t] = line[:, t * lanes : (t + 1) * lanes]
    pl.semaphore_wait(barrier, group - 1)

    def remote(src, dst, send, recv, to_section, to_shard):
        return pltpu.make_async_remote_copy(
            src_ref=src,
            dst_ref=dst,
            send_sem=send,
            recv_sem=recv,
            device_id={"tm": to_section, "space": to_shard},
            device_id_type=pl.DeviceIdType.MESH,
        )

    def start_copy(n):
        other = flip(shard, n)
        return remote(
            start.at[pl.ds(lax.rem(other, team_shards) * halves // repeat, halves)],
            frame_latents.at[0, :, :, shard],
            start_send.at[n],
            start_recv.at[n],
            section,
            other,
        )

    def half_copy(n):
        other = flip(section, n)
        return remote(
            start.at[:, other],
            token_latents.at[pl.ds(section * own_frames, own_frames)],
            half_send.at[n],
            half_recv.at[n],
            other,
            shard,
        )

    def mix_copy(n):
        to_section, to_shard = partner(n)
        return remote(
            mix_send.at[:, member_of(to_section, to_shard)],
            mix_recv.at[pl.ds(member * halves, halves)],
            mix_send_sem.at[n],
            mix_recv_sem.at[n],
            to_section,
            to_shard,
        )

    def lat_copy(n, slot):
        to_section, to_shard = partner(n)
        return remote(
            token_latents.at[pl.ds(first_of(to_section, to_shard), halves)],
            frame_latents.at[slot, :, section, shard],
            lat_send_sem.at[slot, n],
            lat_recv_sem.at[slot, n],
            to_section,
            to_shard,
        )

    def end_copy(n):
        other = flip(section, n)
        return remote(
            ends.at[:, pl.ds(other * own_frames, own_frames)],
            landed.at[:, section],
            end_send.at[n],
            end_recv.at[n],
            other,
            shard,
        )

    def start_all(make, count):
        for n in range(count - 1, 0, -1):
            make(n).start()

    def wait_all(make, count):
        for n in range(count - 1, 0, -1):
            make(n).wait()

    start_all(start_copy, shards)
    start_all(half_copy, sections)
    own_first = lax.rem(shard, team_shards) * halves // repeat
    for n in range(halves):
        frame_latents[0, n, :, shard] = start[own_first + n]
    token_latents[pl.ds(section * own_frames, own_frames)] = start[:, section]
    for copy in input_copies[1:5]:
        copy.wait()
    for slot in range(slots):
        table[slot] = level_table[levels[slot]]
    shift = table[own_slot, 0:1, :]
    scale = 1.0 + table[own_slot, 1:2, :]
    part_rows = 3 * part_width
    block = team_shards * piece
    part = jnp.concatenate(
        [
            pos[pl.ds(pl.multiple_of((t * shards + first) * piece, piece), block), :]
            for t, first in token_order
        ],
        axis=0,
    )
    part = part - jnp.mean(part, axis=-1, keepdims=True)

    def doubled(values):
        if halves == 1:
            return values
        left = lax.broadcasted_iota(jnp.int32, values.shape, 1) < asked
        turned = pltpu.roll(values, asked, 1)
        return jnp.concatenate(
            [jnp.where(left, values, turned), jnp.where(left, turned, values)], axis=1
        )

    centered_pos[...] = doubled(part.T)
    folding[0:tokens, :] = (part * scale).astype(bf16)
    part = embed[...] - jnp.mean(embed[...], axis=-1, keepdims=True)
    high, low = split(jnp.concatenate([part] * piece, axis=0).T)
    centered_embed[...] = jnp.concatenate([high, high, low], axis=1)
    at = tokens
    for values in split(part * scale) + split(jnp.broadcast_to(shift, (channels, width))):
        folding[at : at + channels, :] = values
        at += channels
    input_copies[6].wait()
    for n in range(4):
        factor = math.log2(math.e) / math.sqrt(size) if n % 2 == 0 else 1.0
        gain_columns[n] = jnp.broadcast_to(gains[n : n + 1, :] * factor, (most, size)).T
    input_copies[5].wait()
    row = lax.broadcasted_iota(jnp.int32, (4 * channels, lanes + tokens), 0)
    lane = lax.broadcasted_iota(jnp.int32, (4 * channels, lanes + tokens), 1)
    of_embed = (row < 2 * channels) & (lane < lanes)
    of_embed = of_embed & (lax.rem(row, channels) == lax.rem(lane, channels))
    of_shift = (row >= 2 * channels) & (lane >= lanes) & (lax.rem(row, channels) == 0)
    pick = jnp.where(of_embed | of_shift, 1.0, 0.0).astype(bf16)
    for at in range(0, part_rows, part_width):
        both = nt_dot(spatial_in[at : at + part_width, :], folding[...])
        folded_pos[at : at + part_width, :] = doubled(both[:, 0:tokens])
        high, low = split(both[:, tokens:])
        both = jnp.dot(high, pick, preferred_element_type=f32) + jnp.dot(
            low, pick, preferred_element_type=f32
        )
        high, low = split(both[:, 0:lanes])
        folded_embed[at : at + part_width, :] = jnp.concatenate([high, high, low], axis=1)
        folded_shift[at : at + part_width, :] = both[:, lanes:]
    piece_token = lax.broadcasted_iota(jnp.int32, (piece, lanes), 0)
    lane_token = lax.broadcasted_iota(jnp.int32, (piece, lanes), 1) // channels
    own_lanes = piece_token == lane_token
    high, low = split(embed[...])
    embed_halves[...] = jnp.concatenate(
        [high.astype(f32)] * (2 * piece) + [low.astype(f32)] * piece, axis=0
    ).astype(bf16)
    wait_all(start_copy, shards)
    wait_all(half_copy, sections)

    def spread_out(packed):
        spread = jnp.concatenate(
            [jnp.where(own_lanes, jnp.broadcast_to(row, (piece, lanes)), 0.0) for row in packed],
            axis=0,
        )
        high, low = split(spread)
        return jnp.concatenate([high, low, high], axis=1)

    def frame_row(n):
        home = n // piece
        return (home % sections * shards + home // sections) * piece + n % piece

    def step_body(step, carry):
        spread = spread_out(
            [
                frame_latents[lax.rem(step, 2), k, t, first + n]
                for order in range(0, len(token_order), sections)
                for k in range(halves)
                for t, first in token_order[order : order + sections]
                for n in range(team_shards)
            ]
        )
        squares = None
        chunk = width // 4
        for at in range(0, width, chunk):
            part = nt_dot(centered_embed[at : at + chunk, :], spread)
            part = part + centered_pos[at : at + chunk, :]
            part = jnp.sum(part * part, axis=0, keepdims=True)
            squares = part if squares is None else squares + part
        factor = lax.rsqrt(squares * (1.0 / width) + epsilon)
        for at in range(0, part_rows, part_width):
            count = query_rows if at == 0 else key_rows
            part = nt_dot(folded_embed[at : at + part_width, :], spread[0:count])
            part = (part + folded_pos[at : at + part_width, 0:count]) * factor[:, 0:count]
            for n in range(0, count, tokens):
                projected[at : at + part_width, n : n + tokens] = (
                    part[:, n : n + tokens] + folded_shift[at : at + part_width, :]
                ).astype(bf16)

        attend(
            projected,
            mixed,
            gain_columns.at[0:2],
            part_heads,
            size,
            query_rows,
            key_rows,
            piece,
            False,
        )
        mix_send[...] = (
            mixed[0:part_width, 0:query_rows]
            .T.astype(f32)
            .reshape(halves, team, piece, part_width)
            .astype(bf16)
        )
        start_all(mix_copy, team)
        for n in range(halves):
            mix_recv[member * halves + n] = mix_send[n, member]

        token_pos = pos[pl.ds(pl.multiple_of(item * piece, piece), piece), :]
        base = jnp.dot(
            spread_out([token_latents[n] for n in range(slots * frames)]),
            embed_halves[...],
            preferred_element_type=f32,
        )
        for n in range(slots * frames):
            hidden[n * piece : (n + 1) * piece, :] = (
                base[n * piece : (n + 1) * piece] + token_pos
            )
        @pl.when(step == 0)
        def _():
            for copy in input_copies[9:]:
                copy.wait()
            temporal_turned[...] = temporal_in[...].T
            for copy in input_copies[7:9]:
                copy.wait()
            lines = packed(
                fresh_noise[...].reshape(steps * frames * channels, own_tokens), steps * frames
            )
            for n, line in enumerate(lines):
                for t in range(sections):
                    noise[n // frames, n % frames, t] = line[:, t * lanes : (t + 1) * lanes]
            high, low = split(final_weight[...])
            final_halves[...] = jnp.concatenate(
                [high.astype(f32)] * piece + [low.astype(f32)] * piece, axis=0
            ).astype(bf16)

        wait_all(mix_copy, team)
        branch = None
        arrived = mix_recv[...].astype(f32).reshape(
            slots * frames, repeat, piece, heads // repeat * size
        )
        for n in range(repeat):
            part = jnp.dot(
                arrived[:, n].reshape(rows, part_width).astype(bf16),
                spatial_out[n * part_width : (n + 1) * part_width, :],
                preferred_element_type=f32,
            )
            branch = part if branch is None else branch + part
        for slot in range(slots):
            at = slot * slab
            frame_pos = jnp.concatenate(
                [
                    jnp.broadcast_to(
                        pos[frame_row(slot * frames + n) : frame_row(slot * frames + n) + 1, :],
                        (piece, width),
                    )
                    for n in range(frames)
                ],
                axis=0,
            )
            part = (
                hidden[at : at + slab, :]
                + table[slot, 2:3, :] * branch[at : at + slab]
                + frame_pos
            )
            hidden[at : at + slab, :] = part
            normed[at : at + slab, :] = (
                layer_norm(part) * (1.0 + table[slot, 4:5, :]) + table[slot, 3:4, :]
            ).astype(bf16)
        projected[:, 0:rows] = (
            jnp.dot(normed[0:rows, :], temporal_turned[...], preferred_element_type=f32)
            .astype(bf16)
            .T
        )
        attend(projected, mixed, gain_columns.at[2:4], heads, size, rows, rows, piece, True)
        branch = jnp.dot(mixed[:, 0:rows].T, temporal_out[...], preferred_element_type=f32)
        for slot in range(slots):
            at = slot * slab
            part = hidden[at : at + slab, :] + table[slot, 5:6, :] * branch[at : at + slab]
            final = layer_norm(part) * (1.0 + table[slot, 7:8, :]) + table[slot, 6:7, :]
            high, low = split(final)
            finals[at : at + slab, :] = high
            finals[rows + at : rows + at + slab, :] = low
        product = nt_dot(finals[...], final_halves[...])
        spread = (
            product[0:rows, 0:lanes] + product[0:rows, lanes : 2 * lanes] + product[rows:, 0:lanes]
        )
        for n in range(slots * frames):
            velocity = jnp.sum(
                jnp.where(own_lanes, spread[n * piece : (n + 1) * piece], 0.0),
                axis=0,
                keepdims=True,
            )
            slot = n // frames
            time = (levels[slot].astype(f32) + 1.0) / LEVELS
            before = (levels[slot - 1].astype(f32) + 1.0) / LEVELS if slot > 0 else 0.0
            old = token_latents[n]
            ends[1, n] = old - time * velocity
            if slot > 0:
                token_latents[n - frames] = old - (time - before) * velocity
        for n in range(frames):
            token_latents[(slots - 1) * frames + n] = noise[step, n, section]

        @pl.when(step < steps - 1)
        def _():
            slot = lax.rem(step + 1, 2)
            start_all(functools.partial(lat_copy, slot=slot), group)
            for n in range(halves):
                frame_latents[slot, n, section, shard] = token_latents[frame + n]
            wait_all(functools.partial(lat_copy, slot=slot), group)

        return carry

    lax.fori_loop(0, steps, step_body, 0)
    ends[0] = token_latents[...]
    start_all(end_copy, sections)
    landed[:, section] = ends[:, pl.ds(section * own_frames, own_frames)]
    wait_all(end_copy, sections)
    out[...] = landed[...]


def unpack(frames, landed, next_queue, denoised):
    _, sections, own_frames, _, lanes = landed.shape
    channels = next_queue.shape[2]
    piece = lanes // channels
    own_tokens = sections * piece
    piece_token = lax.broadcasted_iota(jnp.int32, (piece, lanes), 0)
    own_lanes = piece_token == lax.broadcasted_iota(jnp.int32, (piece, lanes), 1) // channels
    spread = jnp.concatenate(
        [
            jnp.where(own_lanes, jnp.broadcast_to(landed[k, t, n], (piece, lanes)), 0.0)
            for k in range(2)
            for n in range(own_frames)
            for t in range(sections)
        ],
        axis=0,
    )
    pick = jnp.where(
        lax.broadcasted_iota(jnp.int32, (channels, lanes), 0)
        == lax.rem(lax.broadcasted_iota(jnp.int32, (channels, lanes), 1), channels),
        1.0,
        0.0,
    )
    result = lax.dot_general(
        pick,
        spread,
        (((1,), (1,)), ((), ())),
        precision=lax.Precision.HIGHEST,
        preferred_element_type=f32,
    )
    for k, target in enumerate((next_queue, denoised)):
        for n in range(own_frames):
            at = (k * own_frames + n) * own_tokens
            target[n // frames, n % frames] = result[:, at : at + own_tokens]


def per_device(
    queue_latents,
    fresh_noise,
    slot_levels,
    level_table,
    embed_weight,
    spatial_in,
    spatial_out,
    temporal_in,
    temporal_out,
    norm_gains,
    final_weight,
):
    blocks, frames, channels, tokens = queue_latents.shape
    steps, slots = fresh_noise.shape[0], slot_levels.shape[0]
    sections, shards = lax.axis_size("tm"), lax.axis_size("space")
    width, size = embed_weight.shape[1], norm_gains.shape[1]
    inner = spatial_out.shape[0]
    heads = inner // size
    group = sections * shards
    repeat = group // (slots * frames)
    halves = 2 if repeat == 1 and frames % 2 == 0 and shards % 2 == 0 else 1
    piece = tokens // sections
    own_frames = blocks * frames
    assert repeat * slots * frames == group and heads % repeat == 0
    assert piece * sections == tokens and own_frames * sections == slots * frames
    lanes = piece * channels
    spatial_in, temporal_in, final = spatial_in.T, temporal_in.T, final_weight.T
    part = inner // repeat
    if repeat > 1:
        which = lax.rem(lax.axis_index("space"), repeat)
        spatial_in = lax.dynamic_index_in_dim(
            spatial_in.reshape(3, repeat, part, width), which, axis=1, keepdims=False
        ).reshape(3 * part, width)
    rows = max(slots * frames * piece, halves * group * piece)
    cfg = dict(
        sections=sections,
        shards=shards,
        repeat=repeat,
        halves=halves,
        slots=slots,
        frames=frames,
        steps=steps,
        heads=heads,
        size=size,
        piece=piece,
    )
    vmem, anywhere = pl.BlockSpec(memory_space=pltpu.VMEM), pl.BlockSpec(memory_space=pl.ANY)
    dma = pltpu.SemaphoreType.DMA
    landed = pl.pallas_call(
        functools.partial(kernel, cfg),
        out_shape=jax.ShapeDtypeStruct((2, sections, own_frames, 1, lanes), f32),
        in_specs=[anywhere] * 12,
        out_specs=vmem,
        scratch_shapes=[
            pltpu.SMEM(slot_levels.shape, jnp.int32),
            pltpu.VMEM(queue_latents.shape, f32),
            pltpu.VMEM(fresh_noise.shape, f32),
            pltpu.VMEM(embed_weight.shape, f32),
            pltpu.VMEM(final.shape, f32),
            pltpu.VMEM(norm_gains.shape, f32),
            pltpu.VMEM((own_frames, sections, 1, lanes), f32),
            pltpu.VMEM((steps, frames, sections, 1, lanes), f32),
            pltpu.VMEM(level_table.shape, f32),
            pltpu.VMEM((group * piece, width), f32),
            pltpu.VMEM((4, size, rows), f32),
            pltpu.VMEM((2, halves, sections, shards, 1, lanes), f32),
            pltpu.VMEM((slots * frames, 1, lanes), f32),
            pltpu.VMEM((halves, group // halves, piece, part), bf16),
            pltpu.VMEM((group, piece, part), bf16),
            pltpu.VMEM((slots, level_table.shape[1], width), f32),
            pltpu.VMEM((slots * frames * piece, width), f32),
            pltpu.VMEM((rows, width), bf16),
            pltpu.VMEM((2 * slots * frames * piece, width), bf16),
            pltpu.VMEM((3 * lanes, width), bf16),
            pltpu.VMEM((2 * lanes, width), bf16),
            pltpu.VMEM((2, slots * frames, 1, lanes), f32),
            pltpu.VMEM((2, sections, own_frames, 1, lanes), f32),
            pltpu.VMEM(spatial_in.shape, bf16),
            pltpu.VMEM(spatial_out.shape, bf16),
            pltpu.VMEM(temporal_in.shape, bf16),
            pltpu.VMEM(temporal_out.shape, bf16),
            pltpu.VMEM(temporal_in.shape[::-1], bf16),
            pltpu.VMEM((width, halves * group * piece), f32),
            pltpu.VMEM((width, 3 * lanes), bf16),
            pltpu.VMEM((3 * part, 3 * lanes), bf16),
            pltpu.VMEM((3 * part, halves * group * piece), f32),
            pltpu.VMEM((3 * part, group * piece), f32),
            pltpu.VMEM((group * piece + 4 * channels, width), bf16),
            pltpu.VMEM((3 * inner, rows), bf16),
            pltpu.VMEM((inner, rows), bf16),
            dma((12,)),
            dma((shards,)),
            dma((shards,)),
            dma((sections,)),
            dma((sections,)),
            dma((group,)),
            dma((group,)),
            dma((2, group)),
            dma((2, group)),
            dma((sections,)),
            dma((sections,)),
        ],
        compiler_params=pltpu.CompilerParams(
            collective_id=0, has_side_effects=True, vmem_limit_bytes=60 * 1024 * 1024
        ),
    )(
        slot_levels,
        queue_latents,
        fresh_noise,
        embed_weight,
        final,
        norm_gains,
        level_table,
        jnp.asarray(
            sincos(group * piece, width)
            .reshape(shards, sections, piece, width)
            .swapaxes(0, 1)
            .reshape(group * piece, width)
        ),
        spatial_in,
        spatial_out,
        temporal_in,
        temporal_out,
    )
    return pl.pallas_call(
        functools.partial(unpack, frames),
        out_shape=(jax.ShapeDtypeStruct(queue_latents.shape, f32),) * 2,
        in_specs=[vmem],
        out_specs=(vmem, vmem),
    )(landed)


def solution(mesh):
    own = P(("clip", "tm"), None, None, "space")
    return jax.shard_map(
        per_device,
        mesh=mesh,
        in_specs=(own, P("clip", None, None, "space"), P("clip")) + (P(),) * 8,
        out_specs=(own, own),
        check_vma=False,
    )
```

```python
import functools
import math

import jax
import jax.numpy as jnp
import numpy as np
from jax import lax
from jax.experimental import pallas as pl
from jax.experimental.pallas import tpu as pltpu
from jax.sharding import PartitionSpec as P

LEVELS = 16
epsilon = 1e-06
f32 = jnp.float32
bf16 = jnp.bfloat16


def sincos(count, width):
    half = width // 2
    rates = np.exp(-np.log(np.float32(10000.0)) * np.arange(half, dtype=np.float32) / np.float32(half))
    angles = np.arange(count, dtype=np.float32)[:, None] * rates[None, :].astype(np.float32)
    return np.concatenate([np.sin(angles), np.cos(angles)], axis=-1).astype(np.float32)


def layer_norm(values):
    centered = values - jnp.mean(values, axis=-1, keepdims=True)
    return centered * lax.rsqrt(jnp.mean(centered * centered, axis=-1, keepdims=True) + epsilon)


def split(values):
    high = values.astype(bf16)
    return high, (values - high.astype(f32)).astype(bf16)


def attend(projected, mixed, gains, heads, size, rows, keys_count, piece, masked):
    inner = heads * size

    def head_normed(at, gain, count):
        values = projected[at : at + size, 0:count].astype(f32)
        mean = jnp.sum(values * values, axis=0, keepdims=True) * (1.0 / size)
        return (values * lax.rsqrt(mean + epsilon) * gains[gain, :, 0:count]).astype(bf16)

    half = rows // 2
    if masked:
        row = lax.rem(lax.broadcasted_iota(jnp.int32, (piece, rows), 0), piece)
        own = row == lax.rem(lax.broadcasted_iota(jnp.int32, (piece, rows), 1), piece)
        keep = jnp.concatenate([jnp.where(own, 1.0, 0.0)] * (rows // piece), axis=0).astype(bf16)
    elif keys_count > rows:
        left = lax.broadcasted_iota(jnp.int32, (half, rows), 1) < half
        keep_left = jnp.where(left, 1.0, 0.0).astype(bf16)
        keep_right = jnp.where(left, 0.0, 1.0).astype(bf16)
    for at in range(0, inner, size):
        queries = head_normed(at, 0, rows)
        keys = head_normed(inner + at, 1, keys_count)
        values = projected[2 * inner + at : 2 * inner + at + size, 0:keys_count]
        scores = lax.dot_general(
            keys, queries, (((0,), (0,)), ((), ())), preferred_element_type=f32
        )
        if keys_count > rows:
            scores = jnp.concatenate(
                [
                    jnp.where(left, scores[n : n + half], scores[n + half : n + rows])
                    for n in range(0, keys_count, rows)
                ],
                axis=0,
            )
        weights = jnp.exp2(scores)
        rounded = weights.astype(bf16)
        if masked:
            totals = jnp.sum(weights.reshape(rows // piece, piece, rows), axis=0)
            totals = jnp.sum(jnp.where(own, totals, 0.0), axis=0, keepdims=True)
            rounded = rounded * keep
        else:
            totals = jnp.sum(weights, axis=0, keepdims=True)
            if keys_count > rows:
                parts = []
                for n in range(0, rows, half):
                    part = rounded[n : n + half]
                    parts += [part * keep_left, part * keep_right]
                rounded = jnp.concatenate(parts, axis=0)
        total = jnp.dot(values, rounded, preferred_element_type=f32)
        mixed[at : at + size, 0:rows] = (total * (1.0 / totals)).astype(bf16)


def nt_dot(left, right):
    return lax.dot_general(left, right, (((1,), (1,)), ((), ())), preferred_element_type=f32)


def kernel(
    cfg,
    levels_hbm,
    queue_latents_hbm,
    fresh_noise_hbm,
    embed_hbm,
    final_weight_hbm,
    gains_hbm,
    level_table_hbm,
    pos_hbm,
    spatial_in_hbm,
    spatial_out_hbm,
    temporal_in_hbm,
    temporal_out_hbm,
    out,
    levels,
    queue_latents,
    fresh_noise,
    embed,
    final_weight,
    gains,
    start,
    noise,
    level_table,
    pos,
    gain_columns,
    frame_latents,
    token_latents,
    mix_send,
    mix_recv,
    table,
    hidden,
    normed,
    finals,
    embed_halves,
    final_halves,
    ends,
    landed,
    spatial_in,
    spatial_out,
    temporal_in,
    temporal_out,
    temporal_turned,
    centered_pos,
    centered_embed,
    folded_embed,
    folded_pos,
    folded_shift,
    folding,
    projected,
    mixed,
    weight_sem,
    start_send,
    start_recv,
    half_send,
    half_recv,
    mix_send_sem,
    mix_recv_sem,
    lat_send_sem,
    lat_recv_sem,
    end_send,
    end_recv,
):
    sections, shards, repeat = cfg["sections"], cfg["shards"], cfg["repeat"]
    halves = cfg["halves"]
    slots, frames, steps = cfg["slots"], cfg["frames"], cfg["steps"]
    heads, size, piece = cfg["heads"], cfg["size"], cfg["piece"]
    channels, width = embed.shape
    lanes = piece * channels
    group = sections * shards
    own_frames = slots * frames // sections
    rows = slots * frames * piece
    slab = frames * piece
    tokens = group * piece
    team_shards = shards // halves
    team = sections * team_shards
    asked = tokens // halves
    query_rows, key_rows = halves * asked, halves * tokens
    most = max(rows, key_rows)
    part_heads = heads // repeat
    part_width = part_heads * size
    section, shard = lax.axis_index("tm"), lax.axis_index("space")
    item = section * shards + shard
    half = shard // team_shards

    def member_of(to_section, to_shard):
        return to_section * team_shards + lax.rem(to_shard, team_shards)

    def first_of(to_section, to_shard):
        return member_of(to_section, to_shard) * halves // repeat

    member = member_of(section, shard)
    frame = first_of(section, shard)
    own_slot = frame // frames
    token_order = [
        (t, lax.rem(half + n, halves) * team_shards)
        for n in range(halves)
        for t in range(sections)
    ]

    def flip(index, code):
        bit, other = 1, index
        while bit <= code:
            if code & bit:
                other = other + bit - 2 * bit * lax.rem(index // bit, 2)
            bit *= 2
        return other

    def partner(n):
        return flip(section, n % sections), flip(shard, n // sections)

    partners = range(group - 1, 0, -1)
    barrier = pltpu.get_barrier_semaphore()
    for n in partners:
        to_section, to_shard = partner(n)
        pl.semaphore_signal(
            barrier,
            inc=1,
            device_id={"tm": to_section, "space": to_shard},
            device_id_type=pl.DeviceIdType.MESH,
        )

    input_copies = [
        pltpu.make_async_copy(src, dst, weight_sem.at[n])
        for n, (src, dst) in enumerate(
            (
                (queue_latents_hbm, queue_latents),
                (levels_hbm, levels),
                (embed_hbm, embed),
                (level_table_hbm, level_table),
                (pos_hbm, pos),
                (spatial_in_hbm, spatial_in),
                (gains_hbm, gains),
                (fresh_noise_hbm, fresh_noise),
                (final_weight_hbm, final_weight),
                (temporal_in_hbm, temporal_in),
                (spatial_out_hbm, spatial_out),
                (temporal_out_hbm, temporal_out),
            )
        )
    ]
    for n in (0, 1, 2, 6, 7, 8, 3, 4, 5, 9, 10, 11):
        input_copies[n].start()

    def packed(latents, count):
        own_tokens = latents.shape[1]
        wide = sections * lanes
        token = lax.broadcasted_iota(jnp.int32, (own_tokens, wide), 0)
        lane = lax.broadcasted_iota(jnp.int32, (own_tokens, wide), 1)
        spread = jnp.dot(
            latents,
            jnp.where(token == lane // channels, 1.0, 0.0),
            precision=lax.Precision.HIGHEST,
            preferred_element_type=f32,
        )
        channel = lax.broadcasted_iota(jnp.int32, (channels, wide), 0)
        own = channel == lax.rem(lax.broadcasted_iota(jnp.int32, (channels, wide), 1), channels)
        return [
            jnp.sum(
                jnp.where(own, spread[n * channels : (n + 1) * channels], 0.0),
                axis=0,
                keepdims=True,
            )
            for n in range(count)
        ]

    own_tokens = sections * piece
    input_copies[0].wait()
    lines = packed(queue_latents[...].reshape(own_frames * channels, own_tokens), own_frames)
    for n, line in enumerate(lines):
        for t in range(sections):
            start[n, t] = line[:, t * lanes : (t + 1) * lanes]
    pl.semaphore_wait(barrier, group - 1)

    def remote(src, dst, send, recv, to_section, to_shard):
        return pltpu.make_async_remote_copy(
            src_ref=src,
            dst_ref=dst,
            send_sem=send,
            recv_sem=recv,
            device_id={"tm": to_section, "space": to_shard},
            device_id_type=pl.DeviceIdType.MESH,
        )

    def start_copy(n):
        other = flip(shard, n)
        return remote(
            start.at[pl.ds(lax.rem(other, team_shards) * halves // repeat, halves)],
            frame_latents.at[0, :, :, shard],
            start_send.at[n],
            start_recv.at[n],
            section,
            other,
        )

    def half_copy(n):
        other = flip(section, n)
        return remote(
            start.at[:, other],
            token_latents.at[pl.ds(section * own_frames, own_frames)],
            half_send.at[n],
            half_recv.at[n],
            other,
            shard,
        )

    def mix_copy(n):
        to_section, to_shard = partner(n)
        return remote(
            mix_send.at[:, member_of(to_section, to_shard)],
            mix_recv.at[pl.ds(member * halves, halves)],
            mix_send_sem.at[n],
            mix_recv_sem.at[n],
            to_section,
            to_shard,
        )

    def lat_copy(n, slot):
        to_section, to_shard = partner(n)
        return remote(
            token_latents.at[pl.ds(first_of(to_section, to_shard), halves)],
            frame_latents.at[slot, :, section, shard],
            lat_send_sem.at[slot, n],
            lat_recv_sem.at[slot, n],
            to_section,
            to_shard,
        )

    def end_copy(n):
        other = flip(section, n)
        return remote(
            ends.at[:, pl.ds(other * own_frames, own_frames)],
            landed.at[:, section],
            end_send.at[n],
            end_recv.at[n],
            other,
            shard,
        )

    def start_all(make, count):
        for n in range(count - 1, 0, -1):
            make(n).start()

    def wait_all(make, count):
        for n in range(count - 1, 0, -1):
            make(n).wait()

    start_all(start_copy, shards)
    start_all(half_copy, sections)
    own_first = lax.rem(shard, team_shards) * halves // repeat
    for n in range(halves):
        frame_latents[0, n, :, shard] = start[own_first + n]
    token_latents[pl.ds(section * own_frames, own_frames)] = start[:, section]
    for copy in input_copies[1:5]:
        copy.wait()
    for slot in range(slots):
        table[slot] = level_table[levels[slot]]
        for row in (4, 7):
            table[slot, row : row + 1, :] = 1.0 + table[slot, row : row + 1, :]
    shift = table[own_slot, 0:1, :]
    scale = 1.0 + table[own_slot, 1:2, :]
    part_rows = 3 * part_width
    block = team_shards * piece
    part = jnp.concatenate(
        [
            pos[pl.ds(pl.multiple_of((t * shards + first) * piece, piece), block), :]
            for t, first in token_order
        ],
        axis=0,
    )
    part = part - jnp.mean(part, axis=-1, keepdims=True)

    def doubled(values):
        if halves == 1:
            return values
        left = lax.broadcasted_iota(jnp.int32, values.shape, 1) < asked
        turned = pltpu.roll(values, asked, 1)
        return jnp.concatenate(
            [jnp.where(left, values, turned), jnp.where(left, turned, values)], axis=1
        )

    centered_pos[...] = doubled(part.T)
    folding[0:tokens, :] = (part * scale).astype(bf16)
    part = embed[...] - jnp.mean(embed[...], axis=-1, keepdims=True)
    high = jnp.concatenate([part] * piece, axis=0).T.astype(bf16)
    centered_embed[...] = jnp.concatenate([high, high], axis=1)
    at = tokens
    for values in split(part * scale) + split(jnp.broadcast_to(shift, (channels, width))):
        folding[at : at + channels, :] = values
        at += channels
    input_copies[6].wait()
    for n in range(4):
        factor = math.log2(math.e) / math.sqrt(size) if n % 2 == 0 else 1.0
        gain_columns[n] = jnp.broadcast_to(gains[n : n + 1, :] * factor, (most, size)).T
    input_copies[5].wait()
    row = lax.broadcasted_iota(jnp.int32, (4 * channels, lanes + tokens), 0)
    lane = lax.broadcasted_iota(jnp.int32, (4 * channels, lanes + tokens), 1)
    of_embed = (row < 2 * channels) & (lane < lanes)
    of_embed = of_embed & (lax.rem(row, channels) == lax.rem(lane, channels))
    of_shift = (row >= 2 * channels) & (lane >= lanes) & (lax.rem(row, channels) == 0)
    pick = jnp.where(of_embed | of_shift, 1.0, 0.0).astype(bf16)
    for at in range(0, part_rows, part_width):
        both = nt_dot(spatial_in[at : at + part_width, :], folding[...])
        folded_pos[at : at + part_width, :] = doubled(both[:, 0:tokens])
        high, low = split(both[:, tokens:])
        both = jnp.dot(high, pick, preferred_element_type=f32) + jnp.dot(
            low, pick, preferred_element_type=f32
        )
        high = both[:, 0:lanes].astype(bf16)
        folded_embed[at : at + part_width, :] = jnp.concatenate([high, high], axis=1)
        folded_shift[at : at + part_width, :] = both[:, lanes:]
    piece_token = lax.broadcasted_iota(jnp.int32, (piece, lanes), 0)
    lane_token = lax.broadcasted_iota(jnp.int32, (piece, lanes), 1) // channels
    own_lanes = piece_token == lane_token
    high, low = split(embed[...])
    embed_halves[...] = jnp.concatenate(
        [high.astype(f32)] * (2 * piece) + [low.astype(f32)] * piece, axis=0
    ).astype(bf16)
    wait_all(start_copy, shards)
    wait_all(half_copy, sections)

    def spread_out(packed):
        spread = jnp.concatenate(
            [jnp.where(own_lanes, jnp.broadcast_to(row, (piece, lanes)), 0.0) for row in packed],
            axis=0,
        )
        return split(spread)

    def frame_row(n):
        home = n // piece
        return (home % sections * shards + home // sections) * piece + n % piece

    def step_body(step, carry):
        halved = spread_out(
            [
                frame_latents[lax.rem(step, 2), k, t, first + n]
                for order in range(0, len(token_order), sections)
                for k in range(halves)
                for t, first in token_order[order : order + sections]
                for n in range(team_shards)
            ]
        )
        spread = jnp.concatenate(halved, axis=1)
        squares = None
        chunk = width // 4
        for at in range(0, width, chunk):
            part = nt_dot(centered_embed[at : at + chunk, :], spread)
            part = part + centered_pos[at : at + chunk, :]
            part = jnp.sum(part * part, axis=0, keepdims=True)
            squares = part if squares is None else squares + part
        factor = lax.rsqrt(squares * (1.0 / width) + epsilon)
        for at in range(0, part_rows, part_width):
            count = query_rows if at == 0 else key_rows
            part = nt_dot(folded_embed[at : at + part_width, :], spread[0:count])
            part = (part + folded_pos[at : at + part_width, 0:count]) * factor[:, 0:count]
            for n in range(0, count, tokens):
                projected[at : at + part_width, n : n + tokens] = (
                    part[:, n : n + tokens] + folded_shift[at : at + part_width, :]
                ).astype(bf16)

        attend(
            projected,
            mixed,
            gain_columns.at[0:2],
            part_heads,
            size,
            query_rows,
            key_rows,
            piece,
            False,
        )
        mix_send[...] = (
            mixed[0:part_width, 0:query_rows]
            .T.astype(f32)
            .reshape(halves, team, piece, part_width)
            .astype(bf16)
        )
        start_all(mix_copy, team)
        for n in range(halves):
            mix_recv[member * halves + n] = mix_send[n, member]

        token_pos = pos[pl.ds(pl.multiple_of(item * piece, piece), piece), :]
        high, low = spread_out([token_latents[n] for n in range(slots * frames)])
        base = jnp.dot(
            jnp.concatenate([high, low, high], axis=1),
            embed_halves[...],
            preferred_element_type=f32,
        )
        for n in range(slots * frames):
            hidden[n * piece : (n + 1) * piece, :] = (
                base[n * piece : (n + 1) * piece]
                + token_pos
                + pos[frame_row(n) : frame_row(n) + 1, :]
            )
        @pl.when(step == 0)
        def _():
            for copy in input_copies[9:]:
                copy.wait()
            temporal_turned[...] = temporal_in[...].T
            for copy in input_copies[7:9]:
                copy.wait()
            lines = packed(
                fresh_noise[...].reshape(steps * frames * channels, own_tokens), steps * frames
            )
            for n, line in enumerate(lines):
                for t in range(sections):
                    noise[n // frames, n % frames, t] = line[:, t * lanes : (t + 1) * lanes]
            high, low = split(final_weight[...])
            final_halves[...] = jnp.concatenate(
                [high.astype(f32)] * piece + [low.astype(f32)] * piece, axis=0
            ).T.astype(bf16)

        wait_all(mix_copy, team)
        branch = None
        arrived = mix_recv[...].astype(f32).reshape(
            slots * frames, repeat, piece, heads // repeat * size
        )
        for n in range(repeat):
            part = jnp.dot(
                arrived[:, n].reshape(rows, part_width).astype(bf16),
                spatial_out[n * part_width : (n + 1) * part_width, :],
                preferred_element_type=f32,
            )
            branch = part if branch is None else branch + part
        for slot in range(slots):
            at = slot * slab
            part = (
                hidden[at : at + slab, :]
                + table[slot, 2:3, :] * branch[at : at + slab]
            )
            hidden[at : at + slab, :] = part
            normed[at : at + slab, :] = (
                layer_norm(part) * table[slot, 4:5, :] + table[slot, 3:4, :]
            ).astype(bf16)
        projected[:, 0:rows] = (
            jnp.dot(normed[0:rows, :], temporal_turned[...], preferred_element_type=f32)
            .astype(bf16)
            .T
        )
        attend(projected, mixed, gain_columns.at[2:4], heads, size, rows, rows, piece, True)
        branch = jnp.dot(mixed[:, 0:rows].T, temporal_out[...], preferred_element_type=f32)
        for slot in range(slots):
            at = slot * slab
            part = hidden[at : at + slab, :] + table[slot, 5:6, :] * branch[at : at + slab]
            final = layer_norm(part) * table[slot, 7:8, :] + table[slot, 6:7, :]
            finals[at : at + slab, :] = final.astype(bf16)
        product = jnp.dot(finals[...], final_halves[...], preferred_element_type=f32)
        spread = product[:, 0:lanes] + product[:, lanes : 2 * lanes]
        for n in range(slots * frames):
            velocity = jnp.sum(
                jnp.where(own_lanes, spread[n * piece : (n + 1) * piece], 0.0),
                axis=0,
                keepdims=True,
            )
            slot = n // frames
            time = (levels[slot].astype(f32) + 1.0) / LEVELS
            before = (levels[slot - 1].astype(f32) + 1.0) / LEVELS if slot > 0 else 0.0
            old = token_latents[n]
            ends[1, n] = old - time * velocity
            if slot > 0:
                token_latents[n - frames] = old - (time - before) * velocity
        for n in range(frames):
            token_latents[(slots - 1) * frames + n] = noise[step, n, section]

        @pl.when(step < steps - 1)
        def _():
            slot = lax.rem(step + 1, 2)
            start_all(functools.partial(lat_copy, slot=slot), group)
            for n in range(halves):
                frame_latents[slot, n, section, shard] = token_latents[frame + n]
            wait_all(functools.partial(lat_copy, slot=slot), group)

        return carry

    lax.fori_loop(0, steps, step_body, 0)
    ends[0] = token_latents[...]
    start_all(end_copy, sections)
    landed[:, section] = ends[:, pl.ds(section * own_frames, own_frames)]
    wait_all(end_copy, sections)
    out[...] = landed[...]


def unpack(frames, landed, next_queue, denoised):
    _, sections, own_frames, _, lanes = landed.shape
    channels = next_queue.shape[2]
    piece = lanes // channels
    own_tokens = sections * piece
    piece_token = lax.broadcasted_iota(jnp.int32, (piece, lanes), 0)
    own_lanes = piece_token == lax.broadcasted_iota(jnp.int32, (piece, lanes), 1) // channels
    spread = jnp.concatenate(
        [
            jnp.where(own_lanes, jnp.broadcast_to(landed[k, t, n], (piece, lanes)), 0.0)
            for k in range(2)
            for n in range(own_frames)
            for t in range(sections)
        ],
        axis=0,
    )
    pick = jnp.where(
        lax.broadcasted_iota(jnp.int32, (channels, lanes), 0)
        == lax.rem(lax.broadcasted_iota(jnp.int32, (channels, lanes), 1), channels),
        1.0,
        0.0,
    )
    result = lax.dot_general(
        pick,
        spread,
        (((1,), (1,)), ((), ())),
        precision=lax.Precision.HIGHEST,
        preferred_element_type=f32,
    )
    for k, target in enumerate((next_queue, denoised)):
        for n in range(own_frames):
            at = (k * own_frames + n) * own_tokens
            target[n // frames, n % frames] = result[:, at : at + own_tokens]


def per_device(
    queue_latents,
    fresh_noise,
    slot_levels,
    level_table,
    embed_weight,
    spatial_in,
    spatial_out,
    temporal_in,
    temporal_out,
    norm_gains,
    final_weight,
):
    blocks, frames, channels, tokens = queue_latents.shape
    steps, slots = fresh_noise.shape[0], slot_levels.shape[0]
    sections, shards = lax.axis_size("tm"), lax.axis_size("space")
    width, size = embed_weight.shape[1], norm_gains.shape[1]
    inner = spatial_out.shape[0]
    heads = inner // size
    group = sections * shards
    repeat = group // (slots * frames)
    halves = 2 if repeat == 1 and frames % 2 == 0 and shards % 2 == 0 else 1
    piece = tokens // sections
    own_frames = blocks * frames
    assert repeat * slots * frames == group and heads % repeat == 0
    assert piece * sections == tokens and own_frames * sections == slots * frames
    lanes = piece * channels
    spatial_in, temporal_in, final = spatial_in.T, temporal_in.T, final_weight.T
    part = inner // repeat
    if repeat > 1:
        which = lax.rem(lax.axis_index("space"), repeat)
        spatial_in = lax.dynamic_index_in_dim(
            spatial_in.reshape(3, repeat, part, width), which, axis=1, keepdims=False
        ).reshape(3 * part, width)
    rows = max(slots * frames * piece, halves * group * piece)
    cfg = dict(
        sections=sections,
        shards=shards,
        repeat=repeat,
        halves=halves,
        slots=slots,
        frames=frames,
        steps=steps,
        heads=heads,
        size=size,
        piece=piece,
    )
    vmem, anywhere = pl.BlockSpec(memory_space=pltpu.VMEM), pl.BlockSpec(memory_space=pl.ANY)
    dma = pltpu.SemaphoreType.DMA
    landed = pl.pallas_call(
        functools.partial(kernel, cfg),
        out_shape=jax.ShapeDtypeStruct((2, sections, own_frames, 1, lanes), f32),
        in_specs=[anywhere] * 12,
        out_specs=vmem,
        scratch_shapes=[
            pltpu.SMEM(slot_levels.shape, jnp.int32),
            pltpu.VMEM(queue_latents.shape, f32),
            pltpu.VMEM(fresh_noise.shape, f32),
            pltpu.VMEM(embed_weight.shape, f32),
            pltpu.VMEM(final.shape, f32),
            pltpu.VMEM(norm_gains.shape, f32),
            pltpu.VMEM((own_frames, sections, 1, lanes), f32),
            pltpu.VMEM((steps, frames, sections, 1, lanes), f32),
            pltpu.VMEM(level_table.shape, f32),
            pltpu.VMEM((group * piece, width), f32),
            pltpu.VMEM((4, size, rows), f32),
            pltpu.VMEM((2, halves, sections, shards, 1, lanes), f32),
            pltpu.VMEM((slots * frames, 1, lanes), f32),
            pltpu.VMEM((halves, group // halves, piece, part), bf16),
            pltpu.VMEM((group, piece, part), bf16),
            pltpu.VMEM((slots, level_table.shape[1], width), f32),
            pltpu.VMEM((slots * frames * piece, width), f32),
            pltpu.VMEM((rows, width), bf16),
            pltpu.VMEM((slots * frames * piece, width), bf16),
            pltpu.VMEM((3 * lanes, width), bf16),
            pltpu.VMEM((width, 2 * lanes), bf16),
            pltpu.VMEM((2, slots * frames, 1, lanes), f32),
            pltpu.VMEM((2, sections, own_frames, 1, lanes), f32),
            pltpu.VMEM(spatial_in.shape, bf16),
            pltpu.VMEM(spatial_out.shape, bf16),
            pltpu.VMEM(temporal_in.shape, bf16),
            pltpu.VMEM(temporal_out.shape, bf16),
            pltpu.VMEM(temporal_in.shape[::-1], bf16),
            pltpu.VMEM((width, halves * group * piece), f32),
            pltpu.VMEM((width, 2 * lanes), bf16),
            pltpu.VMEM((3 * part, 2 * lanes), bf16),
            pltpu.VMEM((3 * part, halves * group * piece), f32),
            pltpu.VMEM((3 * part, group * piece), f32),
            pltpu.VMEM((group * piece + 4 * channels, width), bf16),
            pltpu.VMEM((3 * inner, rows), bf16),
            pltpu.VMEM((inner, rows), bf16),
            dma((12,)),
            dma((shards,)),
            dma((shards,)),
            dma((sections,)),
            dma((sections,)),
            dma((group,)),
            dma((group,)),
            dma((2, group)),
            dma((2, group)),
            dma((sections,)),
            dma((sections,)),
        ],
        compiler_params=pltpu.CompilerParams(
            collective_id=0, has_side_effects=True, vmem_limit_bytes=60 * 1024 * 1024
        ),
    )(
        slot_levels,
        queue_latents,
        fresh_noise,
        embed_weight,
        final,
        norm_gains,
        level_table,
        jnp.asarray(
            sincos(group * piece, width)
            .reshape(shards, sections, piece, width)
            .swapaxes(0, 1)
            .reshape(group * piece, width)
        ),
        spatial_in,
        spatial_out,
        temporal_in,
        temporal_out,
    )
    return pl.pallas_call(
        functools.partial(unpack, frames),
        out_shape=(jax.ShapeDtypeStruct(queue_latents.shape, f32),) * 2,
        in_specs=[vmem],
        out_specs=(vmem, vmem),
    )(landed)


def solution(mesh):
    own = P(("clip", "tm"), None, None, "space")
    return jax.shard_map(
        per_device,
        mesh=mesh,
        in_specs=(own, P("clip", None, None, "space"), P("clip")) + (P(),) * 8,
        out_specs=(own, own),
        check_vma=False,
    )
```

```python
import functools
import math

import jax
import jax.numpy as jnp
import numpy as np
from jax import lax
from jax.experimental import pallas as pl
from jax.experimental.pallas import tpu as pltpu
from jax.sharding import PartitionSpec as P

LEVELS = 16
epsilon = 1e-06
f32 = jnp.float32
bf16 = jnp.bfloat16


def sincos(count, width):
    half = width // 2
    rates = np.exp(-np.log(np.float32(10000.0)) * np.arange(half, dtype=np.float32) / np.float32(half))
    angles = np.arange(count, dtype=np.float32)[:, None] * rates[None, :].astype(np.float32)
    return np.concatenate([np.sin(angles), np.cos(angles)], axis=-1).astype(np.float32)


def layer_norm(values):
    centered = values - jnp.mean(values, axis=-1, keepdims=True)
    return centered * lax.rsqrt(jnp.mean(centered * centered, axis=-1, keepdims=True) + epsilon)


def split(values):
    high = values.astype(bf16)
    return high, (values - high.astype(f32)).astype(bf16)


def attend(projected, mixed, gains, heads, size, rows, keys_count, piece, masked):
    inner = heads * size

    def head_normed(at, gain, count):
        values = projected[at : at + size, 0:count].astype(f32)
        mean = jnp.sum(values * values, axis=0, keepdims=True) * (1.0 / size)
        return (values * lax.rsqrt(mean + epsilon) * gains[gain, :, 0:count]).astype(bf16)

    half = rows // 2
    if masked:
        row = lax.rem(lax.broadcasted_iota(jnp.int32, (piece, rows), 0), piece)
        own = row == lax.rem(lax.broadcasted_iota(jnp.int32, (piece, rows), 1), piece)
        keep = jnp.concatenate([jnp.where(own, 1.0, 0.0)] * (rows // piece), axis=0).astype(bf16)
    elif keys_count > rows:
        left = lax.broadcasted_iota(jnp.int32, (half, rows), 1) < half
        keep_left = jnp.where(left, 1.0, 0.0).astype(bf16)
        keep_right = jnp.where(left, 0.0, 1.0).astype(bf16)
    for at in range(0, inner, size):
        queries = head_normed(at, 0, rows)
        keys = head_normed(inner + at, 1, keys_count)
        values = projected[2 * inner + at : 2 * inner + at + size, 0:keys_count]
        scores = lax.dot_general(
            keys, queries, (((0,), (0,)), ((), ())), preferred_element_type=f32
        )
        if keys_count > rows:
            scores = jnp.concatenate(
                [
                    jnp.where(left, scores[n : n + half], scores[n + half : n + rows])
                    for n in range(0, keys_count, rows)
                ],
                axis=0,
            )
        weights = jnp.exp2(scores)
        rounded = weights.astype(bf16)
        if masked:
            totals = jnp.sum(weights.reshape(rows // piece, piece, rows), axis=0)
            totals = jnp.sum(jnp.where(own, totals, 0.0), axis=0, keepdims=True)
            rounded = rounded * keep
        else:
            totals = jnp.sum(weights, axis=0, keepdims=True)
            if keys_count > rows:
                parts = []
                for n in range(0, rows, half):
                    part = rounded[n : n + half]
                    parts += [part * keep_left, part * keep_right]
                rounded = jnp.concatenate(parts, axis=0)
        total = jnp.dot(values, rounded, preferred_element_type=f32)
        mixed[at : at + size, 0:rows] = (total * (1.0 / totals)).astype(bf16)


def nt_dot(left, right):
    return lax.dot_general(left, right, (((1,), (1,)), ((), ())), preferred_element_type=f32)


def kernel(
    cfg,
    levels_hbm,
    queue_latents_hbm,
    fresh_noise_hbm,
    embed_hbm,
    final_weight_hbm,
    gains_hbm,
    level_table_hbm,
    pos_hbm,
    spatial_in_hbm,
    spatial_out_hbm,
    temporal_in_hbm,
    temporal_out_hbm,
    out,
    levels,
    queue_latents,
    fresh_noise,
    embed,
    final_weight,
    gains,
    start,
    noise,
    level_table,
    pos,
    gain_columns,
    frame_latents,
    token_latents,
    mix_send,
    mix_recv,
    table,
    hidden,
    normed,
    finals,
    embed_halves,
    final_halves,
    ends,
    landed,
    spatial_in,
    spatial_out,
    temporal_in,
    temporal_out,
    temporal_turned,
    centered_pos,
    centered_embed,
    folded_embed,
    folded_pos,
    folded_shift,
    folding,
    projected,
    mixed,
    weight_sem,
    start_send,
    start_recv,
    half_send,
    half_recv,
    mix_send_sem,
    mix_recv_sem,
    lat_send_sem,
    lat_recv_sem,
    end_send,
    end_recv,
):
    sections, shards, repeat = cfg["sections"], cfg["shards"], cfg["repeat"]
    halves = cfg["halves"]
    slots, frames, steps = cfg["slots"], cfg["frames"], cfg["steps"]
    heads, size, piece = cfg["heads"], cfg["size"], cfg["piece"]
    channels, width = embed.shape
    lanes = piece * channels
    group = sections * shards
    own_frames = slots * frames // sections
    rows = slots * frames * piece
    slab = frames * piece
    tokens = group * piece
    team_shards = shards // halves
    team = sections * team_shards
    asked = tokens // halves
    query_rows, key_rows = halves * asked, halves * tokens
    most = max(rows, key_rows)
    part_heads = heads // repeat
    part_width = part_heads * size
    section, shard = lax.axis_index("tm"), lax.axis_index("space")
    item = section * shards + shard
    half = shard // team_shards

    def member_of(to_section, to_shard):
        return to_section * team_shards + lax.rem(to_shard, team_shards)

    def first_of(to_section, to_shard):
        return member_of(to_section, to_shard) * halves // repeat

    member = member_of(section, shard)
    frame = first_of(section, shard)
    own_slot = frame // frames
    token_order = [
        (t, lax.rem(half + n, halves) * team_shards)
        for n in range(halves)
        for t in range(sections)
    ]

    def flip(index, code):
        bit, other = 1, index
        while bit <= code:
            if code & bit:
                other = other + bit - 2 * bit * lax.rem(index // bit, 2)
            bit *= 2
        return other

    def partner(n):
        return flip(section, n % sections), flip(shard, n // sections)

    partners = range(group - 1, 0, -1)
    barrier = pltpu.get_barrier_semaphore()
    for n in partners:
        to_section, to_shard = partner(n)
        pl.semaphore_signal(
            barrier,
            inc=1,
            device_id={"tm": to_section, "space": to_shard},
            device_id_type=pl.DeviceIdType.MESH,
        )

    input_copies = [
        pltpu.make_async_copy(src, dst, weight_sem.at[n])
        for n, (src, dst) in enumerate(
            (
                (queue_latents_hbm, queue_latents),
                (levels_hbm, levels),
                (embed_hbm, embed),
                (level_table_hbm, level_table),
                (pos_hbm, pos),
                (spatial_in_hbm, spatial_in),
                (gains_hbm, gains),
                (fresh_noise_hbm, fresh_noise),
                (final_weight_hbm, final_weight),
                (temporal_in_hbm, temporal_in),
                (spatial_out_hbm, spatial_out),
                (temporal_out_hbm, temporal_out),
            )
        )
    ]
    for n in (0, 1, 2, 6, 7, 8, 3, 4, 5, 9, 10, 11):
        input_copies[n].start()

    def packed(latents, count):
        own_tokens = latents.shape[1]
        wide = sections * lanes
        token = lax.broadcasted_iota(jnp.int32, (own_tokens, wide), 0)
        lane = lax.broadcasted_iota(jnp.int32, (own_tokens, wide), 1)
        spread = jnp.dot(
            latents,
            jnp.where(token == lane // channels, 1.0, 0.0),
            precision=lax.Precision.HIGHEST,
            preferred_element_type=f32,
        )
        channel = lax.broadcasted_iota(jnp.int32, (channels, wide), 0)
        own = channel == lax.rem(lax.broadcasted_iota(jnp.int32, (channels, wide), 1), channels)
        return [
            jnp.sum(
                jnp.where(own, spread[n * channels : (n + 1) * channels], 0.0),
                axis=0,
                keepdims=True,
            )
            for n in range(count)
        ]

    own_tokens = sections * piece
    input_copies[0].wait()
    lines = packed(queue_latents[...].reshape(own_frames * channels, own_tokens), own_frames)
    for n, line in enumerate(lines):
        for t in range(sections):
            start[n, t] = line[:, t * lanes : (t + 1) * lanes]
    pl.semaphore_wait(barrier, group - 1)

    def remote(src, dst, send, recv, to_section, to_shard):
        return pltpu.make_async_remote_copy(
            src_ref=src,
            dst_ref=dst,
            send_sem=send,
            recv_sem=recv,
            device_id={"tm": to_section, "space": to_shard},
            device_id_type=pl.DeviceIdType.MESH,
        )

    def start_copy(n):
        other = flip(shard, n)
        return remote(
            start.at[pl.ds(lax.rem(other, team_shards) * halves // repeat, halves)],
            frame_latents.at[0, :, :, shard],
            start_send.at[n],
            start_recv.at[n],
            section,
            other,
        )

    def half_copy(n):
        other = flip(section, n)
        return remote(
            start.at[:, other],
            token_latents.at[pl.ds(section * own_frames, own_frames)],
            half_send.at[n],
            half_recv.at[n],
            other,
            shard,
        )

    def mix_copy(n):
        to_section, to_shard = partner(n)
        return remote(
            mix_send.at[:, member_of(to_section, to_shard)],
            mix_recv.at[pl.ds(member * halves, halves)],
            mix_send_sem.at[n],
            mix_recv_sem.at[n],
            to_section,
            to_shard,
        )

    def lat_copy(n, slot):
        to_section, to_shard = partner(n)
        return remote(
            token_latents.at[pl.ds(first_of(to_section, to_shard), halves)],
            frame_latents.at[slot, :, section, shard],
            lat_send_sem.at[slot, n],
            lat_recv_sem.at[slot, n],
            to_section,
            to_shard,
        )

    def end_copy(n):
        other = flip(section, n)
        return remote(
            ends.at[:, pl.ds(other * own_frames, own_frames)],
            landed.at[:, section],
            end_send.at[n],
            end_recv.at[n],
            other,
            shard,
        )

    def start_all(make, count):
        for n in range(count - 1, 0, -1):
            make(n).start()

    def wait_all(make, count):
        for n in range(count - 1, 0, -1):
            make(n).wait()

    start_all(start_copy, shards)
    start_all(half_copy, sections)
    own_first = lax.rem(shard, team_shards) * halves // repeat
    for n in range(halves):
        frame_latents[0, n, :, shard] = start[own_first + n]
    token_latents[pl.ds(section * own_frames, own_frames)] = start[:, section]
    for copy in input_copies[1:5]:
        copy.wait()
    for slot in range(slots):
        table[slot] = level_table[levels[slot]]
        for row in (4, 7):
            table[slot, row : row + 1, :] = 1.0 + table[slot, row : row + 1, :]
    shift = table[own_slot, 0:1, :]
    scale = 1.0 + table[own_slot, 1:2, :]
    part_rows = 3 * part_width
    block = team_shards * piece
    part = jnp.concatenate(
        [
            pos[pl.ds(pl.multiple_of((t * shards + first) * piece, piece), block), :]
            for t, first in token_order
        ],
        axis=0,
    )
    part = part - jnp.mean(part, axis=-1, keepdims=True)

    def doubled(values):
        if halves == 1:
            return values
        left = lax.broadcasted_iota(jnp.int32, values.shape, 1) < asked
        turned = pltpu.roll(values, asked, 1)
        return jnp.concatenate(
            [jnp.where(left, values, turned), jnp.where(left, turned, values)], axis=1
        )

    centered_pos[...] = doubled(part.T)
    folding[0:tokens, :] = (part * scale).astype(bf16)
    part = embed[...] - jnp.mean(embed[...], axis=-1, keepdims=True)
    high = jnp.concatenate([part] * piece, axis=0).T.astype(bf16)
    centered_embed[...] = jnp.concatenate([high, high], axis=1)
    at = tokens
    for values in split(part * scale) + split(jnp.broadcast_to(shift, (channels, width))):
        folding[at : at + channels, :] = values
        at += channels
    input_copies[6].wait()
    for n in range(4):
        factor = math.log2(math.e) / math.sqrt(size) if n % 2 == 0 else 1.0
        gain_columns[n] = jnp.broadcast_to(gains[n : n + 1, :] * factor, (most, size)).T
    input_copies[5].wait()
    row = lax.broadcasted_iota(jnp.int32, (4 * channels, lanes + tokens), 0)
    lane = lax.broadcasted_iota(jnp.int32, (4 * channels, lanes + tokens), 1)
    of_embed = (row < 2 * channels) & (lane < lanes)
    of_embed = of_embed & (lax.rem(row, channels) == lax.rem(lane, channels))
    of_shift = (row >= 2 * channels) & (lane >= lanes) & (lax.rem(row, channels) == 0)
    pick = jnp.where(of_embed | of_shift, 1.0, 0.0).astype(bf16)
    for at in range(0, part_rows, part_width):
        both = nt_dot(spatial_in[at : at + part_width, :], folding[...])
        folded_pos[at : at + part_width, :] = doubled(both[:, 0:tokens])
        high, low = split(both[:, tokens:])
        both = jnp.dot(high, pick, preferred_element_type=f32) + jnp.dot(
            low, pick, preferred_element_type=f32
        )
        high = both[:, 0:lanes].astype(bf16)
        folded_embed[at : at + part_width, :] = jnp.concatenate([high, high], axis=1)
        folded_shift[at : at + part_width, :] = both[:, lanes:]
    piece_token = lax.broadcasted_iota(jnp.int32, (piece, lanes), 0)
    lane_token = lax.broadcasted_iota(jnp.int32, (piece, lanes), 1) // channels
    own_lanes = piece_token == lane_token
    high, low = split(embed[...])
    embed_halves[...] = jnp.concatenate(
        [high.astype(f32)] * (2 * piece) + [low.astype(f32)] * piece, axis=0
    ).astype(bf16)
    wait_all(start_copy, shards)
    wait_all(half_copy, sections)

    def spread_out(packed):
        spread = jnp.concatenate(
            [jnp.where(own_lanes, jnp.broadcast_to(row, (piece, lanes)), 0.0) for row in packed],
            axis=0,
        )
        return split(spread)

    def frame_row(n):
        home = n // piece
        return (home % sections * shards + home // sections) * piece + n % piece

    def step_body(step, carry):
        halved = spread_out(
            [
                frame_latents[lax.rem(step, 2), k, t, first + n]
                for order in range(0, len(token_order), sections)
                for k in range(halves)
                for t, first in token_order[order : order + sections]
                for n in range(team_shards)
            ]
        )
        spread = jnp.concatenate(halved, axis=1)
        squares = None
        chunk = width // 4
        for at in range(0, width, chunk):
            part = nt_dot(centered_embed[at : at + chunk, :], spread)
            part = part + centered_pos[at : at + chunk, :]
            part = jnp.sum(part * part, axis=0, keepdims=True)
            squares = part if squares is None else squares + part
        factor = lax.rsqrt(squares * (1.0 / width) + epsilon)
        for at in range(0, part_rows, part_width):
            count = query_rows if at == 0 else key_rows
            part = nt_dot(folded_embed[at : at + part_width, :], spread[0:count])
            part = (part + folded_pos[at : at + part_width, 0:count]) * factor[:, 0:count]
            for n in range(0, count, tokens):
                projected[at : at + part_width, n : n + tokens] = (
                    part[:, n : n + tokens] + folded_shift[at : at + part_width, :]
                ).astype(bf16)

        attend(
            projected,
            mixed,
            gain_columns.at[0:2],
            part_heads,
            size,
            query_rows,
            key_rows,
            piece,
            False,
        )
        mix_send[...] = (
            mixed[0:part_width, 0:query_rows]
            .T.astype(f32)
            .reshape(halves, team, piece, part_width)
            .astype(bf16)
        )
        start_all(mix_copy, team)
        for n in range(halves):
            mix_recv[member * halves + n] = mix_send[n, member]

        token_pos = pos[pl.ds(pl.multiple_of(item * piece, piece), piece), :]
        high, low = spread_out([token_latents[n] for n in range(slots * frames)])
        base = jnp.dot(
            jnp.concatenate([high, low, high], axis=1),
            embed_halves[...],
            preferred_element_type=f32,
        )
        for n in range(slots * frames):
            hidden[n * piece : (n + 1) * piece, :] = (
                base[n * piece : (n + 1) * piece]
                + token_pos
                + pos[frame_row(n) : frame_row(n) + 1, :]
            )
        @pl.when(step == 0)
        def _():
            for copy in input_copies[9:]:
                copy.wait()
            temporal_turned[...] = temporal_in[...].T
            for copy in input_copies[7:9]:
                copy.wait()
            lines = packed(
                fresh_noise[...].reshape(steps * frames * channels, own_tokens), steps * frames
            )
            for n, line in enumerate(lines):
                for t in range(sections):
                    noise[n // frames, n % frames, t] = line[:, t * lanes : (t + 1) * lanes]
            high, low = split(final_weight[...])
            final_halves[...] = jnp.concatenate(
                [high.astype(f32)] * piece + [low.astype(f32)] * piece, axis=0
            ).T.astype(bf16)

        wait_all(mix_copy, team)
        branch = None
        arrived = mix_recv[...].astype(f32).reshape(
            slots * frames, repeat, piece, heads // repeat * size
        )
        for n in range(repeat):
            part = jnp.dot(
                arrived[:, n].reshape(rows, part_width).astype(bf16),
                spatial_out[n * part_width : (n + 1) * part_width, :],
                preferred_element_type=f32,
            )
            branch = part if branch is None else branch + part
        for slot in range(slots):
            at = slot * slab
            part = (
                hidden[at : at + slab, :]
                + table[slot, 2:3, :] * branch[at : at + slab]
            )
            hidden[at : at + slab, :] = part
            normed[at : at + slab, :] = (
                layer_norm(part) * table[slot, 4:5, :] + table[slot, 3:4, :]
            ).astype(bf16)
        projected[:, 0:rows] = (
            jnp.dot(normed[0:rows, :], temporal_turned[...], preferred_element_type=f32)
            .astype(bf16)
            .T
        )
        attend(projected, mixed, gain_columns.at[2:4], heads, size, rows, rows, piece, True)
        branch = jnp.dot(mixed[:, 0:rows].T, temporal_out[...], preferred_element_type=f32)
        for slot in range(slots):
            at = slot * slab
            part = hidden[at : at + slab, :] + table[slot, 5:6, :] * branch[at : at + slab]
            final = layer_norm(part) * table[slot, 7:8, :] + table[slot, 6:7, :]
            high, low = split(final)
            finals[at : at + slab, :] = high
            finals[rows + at : rows + at + slab, :] = low
        product = jnp.dot(finals[...], final_halves[...], preferred_element_type=f32)
        spread = (
            product[0:rows, 0:lanes] + product[0:rows, lanes : 2 * lanes] + product[rows:, 0:lanes]
        )
        for n in range(slots * frames):
            velocity = jnp.sum(
                jnp.where(own_lanes, spread[n * piece : (n + 1) * piece], 0.0),
                axis=0,
                keepdims=True,
            )
            slot = n // frames
            time = (levels[slot].astype(f32) + 1.0) / LEVELS
            before = (levels[slot - 1].astype(f32) + 1.0) / LEVELS if slot > 0 else 0.0
            old = token_latents[n]
            ends[1, n] = old - time * velocity
            if slot > 0:
                token_latents[n - frames] = old - (time - before) * velocity
        for n in range(frames):
            token_latents[(slots - 1) * frames + n] = noise[step, n, section]

        @pl.when(step < steps - 1)
        def _():
            slot = lax.rem(step + 1, 2)
            start_all(functools.partial(lat_copy, slot=slot), group)
            for n in range(halves):
                frame_latents[slot, n, section, shard] = token_latents[frame + n]
            wait_all(functools.partial(lat_copy, slot=slot), group)

        return carry

    lax.fori_loop(0, steps, step_body, 0)
    ends[0] = token_latents[...]
    start_all(end_copy, sections)
    landed[:, section] = ends[:, pl.ds(section * own_frames, own_frames)]
    wait_all(end_copy, sections)
    out[...] = landed[...]


def unpack(frames, landed, next_queue, denoised):
    _, sections, own_frames, _, lanes = landed.shape
    channels = next_queue.shape[2]
    piece = lanes // channels
    own_tokens = sections * piece
    piece_token = lax.broadcasted_iota(jnp.int32, (piece, lanes), 0)
    own_lanes = piece_token == lax.broadcasted_iota(jnp.int32, (piece, lanes), 1) // channels
    spread = jnp.concatenate(
        [
            jnp.where(own_lanes, jnp.broadcast_to(landed[k, t, n], (piece, lanes)), 0.0)
            for k in range(2)
            for n in range(own_frames)
            for t in range(sections)
        ],
        axis=0,
    )
    pick = jnp.where(
        lax.broadcasted_iota(jnp.int32, (channels, lanes), 0)
        == lax.rem(lax.broadcasted_iota(jnp.int32, (channels, lanes), 1), channels),
        1.0,
        0.0,
    )
    result = lax.dot_general(
        pick,
        spread,
        (((1,), (1,)), ((), ())),
        precision=lax.Precision.HIGHEST,
        preferred_element_type=f32,
    )
    for k, target in enumerate((next_queue, denoised)):
        for n in range(own_frames):
            at = (k * own_frames + n) * own_tokens
            target[n // frames, n % frames] = result[:, at : at + own_tokens]


def per_device(
    queue_latents,
    fresh_noise,
    slot_levels,
    level_table,
    embed_weight,
    spatial_in,
    spatial_out,
    temporal_in,
    temporal_out,
    norm_gains,
    final_weight,
):
    blocks, frames, channels, tokens = queue_latents.shape
    steps, slots = fresh_noise.shape[0], slot_levels.shape[0]
    sections, shards = lax.axis_size("tm"), lax.axis_size("space")
    width, size = embed_weight.shape[1], norm_gains.shape[1]
    inner = spatial_out.shape[0]
    heads = inner // size
    group = sections * shards
    repeat = group // (slots * frames)
    halves = 2 if repeat == 1 and frames % 2 == 0 and shards % 2 == 0 else 1
    piece = tokens // sections
    own_frames = blocks * frames
    assert repeat * slots * frames == group and heads % repeat == 0
    assert piece * sections == tokens and own_frames * sections == slots * frames
    lanes = piece * channels
    spatial_in, temporal_in, final = spatial_in.T, temporal_in.T, final_weight.T
    part = inner // repeat
    if repeat > 1:
        which = lax.rem(lax.axis_index("space"), repeat)
        spatial_in = lax.dynamic_index_in_dim(
            spatial_in.reshape(3, repeat, part, width), which, axis=1, keepdims=False
        ).reshape(3 * part, width)
    rows = max(slots * frames * piece, halves * group * piece)
    cfg = dict(
        sections=sections,
        shards=shards,
        repeat=repeat,
        halves=halves,
        slots=slots,
        frames=frames,
        steps=steps,
        heads=heads,
        size=size,
        piece=piece,
    )
    vmem, anywhere = pl.BlockSpec(memory_space=pltpu.VMEM), pl.BlockSpec(memory_space=pl.ANY)
    dma = pltpu.SemaphoreType.DMA
    landed = pl.pallas_call(
        functools.partial(kernel, cfg),
        out_shape=jax.ShapeDtypeStruct((2, sections, own_frames, 1, lanes), f32),
        in_specs=[anywhere] * 12,
        out_specs=vmem,
        scratch_shapes=[
            pltpu.SMEM(slot_levels.shape, jnp.int32),
            pltpu.VMEM(queue_latents.shape, f32),
            pltpu.VMEM(fresh_noise.shape, f32),
            pltpu.VMEM(embed_weight.shape, f32),
            pltpu.VMEM(final.shape, f32),
            pltpu.VMEM(norm_gains.shape, f32),
            pltpu.VMEM((own_frames, sections, 1, lanes), f32),
            pltpu.VMEM((steps, frames, sections, 1, lanes), f32),
            pltpu.VMEM(level_table.shape, f32),
            pltpu.VMEM((group * piece, width), f32),
            pltpu.VMEM((4, size, rows), f32),
            pltpu.VMEM((2, halves, sections, shards, 1, lanes), f32),
            pltpu.VMEM((slots * frames, 1, lanes), f32),
            pltpu.VMEM((halves, group // halves, piece, part), bf16),
            pltpu.VMEM((group, piece, part), bf16),
            pltpu.VMEM((slots, level_table.shape[1], width), f32),
            pltpu.VMEM((slots * frames * piece, width), f32),
            pltpu.VMEM((rows, width), bf16),
            pltpu.VMEM((2 * slots * frames * piece, width), bf16),
            pltpu.VMEM((3 * lanes, width), bf16),
            pltpu.VMEM((width, 2 * lanes), bf16),
            pltpu.VMEM((2, slots * frames, 1, lanes), f32),
            pltpu.VMEM((2, sections, own_frames, 1, lanes), f32),
            pltpu.VMEM(spatial_in.shape, bf16),
            pltpu.VMEM(spatial_out.shape, bf16),
            pltpu.VMEM(temporal_in.shape, bf16),
            pltpu.VMEM(temporal_out.shape, bf16),
            pltpu.VMEM(temporal_in.shape[::-1], bf16),
            pltpu.VMEM((width, halves * group * piece), f32),
            pltpu.VMEM((width, 2 * lanes), bf16),
            pltpu.VMEM((3 * part, 2 * lanes), bf16),
            pltpu.VMEM((3 * part, halves * group * piece), f32),
            pltpu.VMEM((3 * part, group * piece), f32),
            pltpu.VMEM((group * piece + 4 * channels, width), bf16),
            pltpu.VMEM((3 * inner, rows), bf16),
            pltpu.VMEM((inner, rows), bf16),
            dma((12,)),
            dma((shards,)),
            dma((shards,)),
            dma((sections,)),
            dma((sections,)),
            dma((group,)),
            dma((group,)),
            dma((2, group)),
            dma((2, group)),
            dma((sections,)),
            dma((sections,)),
        ],
        compiler_params=pltpu.CompilerParams(
            collective_id=0, has_side_effects=True, vmem_limit_bytes=60 * 1024 * 1024
        ),
    )(
        slot_levels,
        queue_latents,
        fresh_noise,
        embed_weight,
        final,
        norm_gains,
        level_table,
        jnp.asarray(
            sincos(group * piece, width)
            .reshape(shards, sections, piece, width)
            .swapaxes(0, 1)
            .reshape(group * piece, width)
        ),
        spatial_in,
        spatial_out,
        temporal_in,
        temporal_out,
    )
    return pl.pallas_call(
        functools.partial(unpack, frames),
        out_shape=(jax.ShapeDtypeStruct(queue_latents.shape, f32),) * 2,
        in_specs=[vmem],
        out_specs=(vmem, vmem),
    )(landed)


def solution(mesh):
    own = P(("clip", "tm"), None, None, "space")
    return jax.shard_map(
        per_device,
        mesh=mesh,
        in_specs=(own, P("clip", None, None, "space"), P("clip")) + (P(),) * 8,
        out_specs=(own, own),
        check_vma=False,
    )
```

```python
import functools
import math

import jax
import jax.numpy as jnp
import numpy as np
from jax import lax
from jax.experimental import pallas as pl
from jax.experimental.pallas import tpu as pltpu
from jax.sharding import PartitionSpec as P

LEVELS = 16
epsilon = 1e-06
f32 = jnp.float32
bf16 = jnp.bfloat16


def sincos(count, width):
    half = width // 2
    rates = np.exp(-np.log(np.float32(10000.0)) * np.arange(half, dtype=np.float32) / np.float32(half))
    angles = np.arange(count, dtype=np.float32)[:, None] * rates[None, :].astype(np.float32)
    return np.concatenate([np.sin(angles), np.cos(angles)], axis=-1).astype(np.float32)


def layer_norm(values):
    centered = values - jnp.mean(values, axis=-1, keepdims=True)
    return centered * lax.rsqrt(jnp.mean(centered * centered, axis=-1, keepdims=True) + epsilon)


def split(values):
    high = values.astype(bf16)
    return high, (values - high.astype(f32)).astype(bf16)


def terms(values):
    high = values.astype(bf16)
    rest = values - high.astype(f32)
    middle = rest.astype(bf16)
    return high, middle, (rest - middle.astype(f32)).astype(bf16)


def attend(projected, mixed, gains, heads, size, rows, keys_count, piece, masked):
    inner = heads * size

    def head_normed(at, gain, count):
        values = projected[at : at + size, 0:count].astype(f32)
        mean = jnp.sum(values * values, axis=0, keepdims=True) * (1.0 / size)
        return (values * lax.rsqrt(mean + epsilon) * gains[gain, :, 0:count]).astype(bf16)

    half = rows // 2
    if masked:
        row = lax.rem(lax.broadcasted_iota(jnp.int32, (piece, rows), 0), piece)
        own = row == lax.rem(lax.broadcasted_iota(jnp.int32, (piece, rows), 1), piece)
        keep = jnp.concatenate([jnp.where(own, 1.0, 0.0)] * (rows // piece), axis=0).astype(bf16)
    elif keys_count > rows:
        left = lax.broadcasted_iota(jnp.int32, (half, rows), 1) < half
        keep_left = jnp.where(left, 1.0, 0.0).astype(bf16)
        keep_right = jnp.where(left, 0.0, 1.0).astype(bf16)
    for at in range(0, inner, size):
        queries = head_normed(at, 0, rows)
        keys = head_normed(inner + at, 1, keys_count)
        values = projected[2 * inner + at : 2 * inner + at + size, 0:keys_count]
        scores = lax.dot_general(
            keys, queries, (((0,), (0,)), ((), ())), preferred_element_type=f32
        )
        if keys_count > rows:
            scores = jnp.concatenate(
                [
                    jnp.where(left, scores[n : n + half], scores[n + half : n + rows])
                    for n in range(0, keys_count, rows)
                ],
                axis=0,
            )
        weights = jnp.exp2(scores)
        rounded = weights.astype(bf16)
        if masked:
            totals = jnp.sum(weights.reshape(rows // piece, piece, rows), axis=0)
            totals = jnp.sum(jnp.where(own, totals, 0.0), axis=0, keepdims=True)
            rounded = rounded * keep
        else:
            totals = jnp.sum(weights, axis=0, keepdims=True)
            if keys_count > rows:
                parts = []
                for n in range(0, rows, half):
                    part = rounded[n : n + half]
                    parts += [part * keep_left, part * keep_right]
                rounded = jnp.concatenate(parts, axis=0)
        total = jnp.dot(values, rounded, preferred_element_type=f32)
        mixed[at : at + size, 0:rows] = (total * (1.0 / totals)).astype(bf16)


def nt_dot(left, right):
    return lax.dot_general(left, right, (((1,), (1,)), ((), ())), preferred_element_type=f32)


def kernel(
    cfg,
    levels_hbm,
    queue_latents_hbm,
    fresh_noise_hbm,
    embed_hbm,
    final_weight_hbm,
    gains_hbm,
    level_table_hbm,
    pos_hbm,
    spatial_in_hbm,
    spatial_out_hbm,
    temporal_in_hbm,
    temporal_out_hbm,
    out,
    levels,
    queue_latents,
    fresh_noise,
    embed,
    final_weight,
    gains,
    start,
    noise,
    level_table,
    pos,
    gain_columns,
    frame_latents,
    token_latents,
    mix_send,
    mix_recv,
    table,
    hidden,
    normed,
    finals,
    embed_halves,
    final_halves,
    ends,
    landed,
    spatial_in,
    spatial_out,
    temporal_in,
    temporal_out,
    temporal_turned,
    centered_pos,
    centered_embed,
    folded_embed,
    folded_pos,
    folded_shift,
    folding,
    projected,
    mixed,
    weight_sem,
    start_send,
    start_recv,
    half_send,
    half_recv,
    mix_send_sem,
    mix_recv_sem,
    lat_send_sem,
    lat_recv_sem,
    end_send,
    end_recv,
):
    sections, shards, repeat = cfg["sections"], cfg["shards"], cfg["repeat"]
    halves = cfg["halves"]
    slots, frames, steps = cfg["slots"], cfg["frames"], cfg["steps"]
    heads, size, piece = cfg["heads"], cfg["size"], cfg["piece"]
    channels, width = embed.shape
    lanes = piece * channels
    group = sections * shards
    own_frames = slots * frames // sections
    rows = slots * frames * piece
    slab = frames * piece
    tokens = group * piece
    team_shards = shards // halves
    team = sections * team_shards
    asked = tokens // halves
    query_rows, key_rows = halves * asked, halves * tokens
    most = max(rows, key_rows)
    part_heads = heads // repeat
    part_width = part_heads * size
    section, shard = lax.axis_index("tm"), lax.axis_index("space")
    item = section * shards + shard
    half = shard // team_shards

    def member_of(to_section, to_shard):
        return to_section * team_shards + lax.rem(to_shard, team_shards)

    def first_of(to_section, to_shard):
        return member_of(to_section, to_shard) * halves // repeat

    member = member_of(section, shard)
    frame = first_of(section, shard)
    own_slot = frame // frames
    token_order = [
        (t, lax.rem(half + n, halves) * team_shards)
        for n in range(halves)
        for t in range(sections)
    ]

    def flip(index, code):
        bit, other = 1, index
        while bit <= code:
            if code & bit:
                other = other + bit - 2 * bit * lax.rem(index // bit, 2)
            bit *= 2
        return other

    def partner(n):
        return flip(section, n % sections), flip(shard, n // sections)

    input_copies = [
        pltpu.make_async_copy(src, dst, weight_sem.at[n])
        for n, (src, dst) in enumerate(
            (
                (queue_latents_hbm, queue_latents),
                (levels_hbm, levels),
                (embed_hbm, embed),
                (level_table_hbm, level_table),
                (pos_hbm, pos),
                (spatial_in_hbm, spatial_in),
                (gains_hbm, gains),
                (fresh_noise_hbm, fresh_noise),
                (final_weight_hbm, final_weight),
                (temporal_in_hbm, temporal_in),
                (spatial_out_hbm, spatial_out),
                (temporal_out_hbm, temporal_out),
            )
        )
    ]
    input_copies[0].start()
    partners = range(group - 1, 0, -1)
    barrier = pltpu.get_barrier_semaphore()
    for n in partners:
        to_section, to_shard = partner(n)
        pl.semaphore_signal(
            barrier,
            inc=1,
            device_id={"tm": to_section, "space": to_shard},
            device_id_type=pl.DeviceIdType.MESH,
        )

    for n in (1, 2, 6, 7, 8, 3, 4, 5, 9, 10, 11):
        input_copies[n].start()

    def packed(latents, count):
        own_tokens = latents.shape[1]
        wide = sections * lanes
        token = lax.broadcasted_iota(jnp.int32, (own_tokens, wide), 0)
        lane = lax.broadcasted_iota(jnp.int32, (own_tokens, wide), 1)
        place = jnp.where(token == lane // channels, 1.0, 0.0).astype(bf16)
        spread = None
        for term in terms(latents):
            part = jnp.dot(term, place, preferred_element_type=f32)
            spread = part if spread is None else spread + part
        channel = lax.broadcasted_iota(jnp.int32, (channels, wide), 0)
        own = channel == lax.rem(lax.broadcasted_iota(jnp.int32, (channels, wide), 1), channels)
        return [
            jnp.sum(
                jnp.where(own, spread[n * channels : (n + 1) * channels], 0.0),
                axis=0,
                keepdims=True,
            )
            for n in range(count)
        ]

    own_tokens = sections * piece
    input_copies[0].wait()
    lines = packed(queue_latents[...].reshape(own_frames * channels, own_tokens), own_frames)
    for n, line in enumerate(lines):
        for t in range(sections):
            start[t, n] = line[:, t * lanes : (t + 1) * lanes]
    pl.semaphore_wait(barrier, group - 1)

    def remote(src, dst, send, recv, to_section, to_shard):
        return pltpu.make_async_remote_copy(
            src_ref=src,
            dst_ref=dst,
            send_sem=send,
            recv_sem=recv,
            device_id={"tm": to_section, "space": to_shard},
            device_id_type=pl.DeviceIdType.MESH,
        )

    def start_copy(n):
        other = flip(shard, n)
        return remote(
            start.at[:, pl.ds(lax.rem(other, team_shards) * halves // repeat, halves)],
            frame_latents.at[0, :, shard],
            start_send.at[n],
            start_recv.at[n],
            section,
            other,
        )

    def half_copy(n):
        other = flip(section, n)
        return remote(
            start.at[other],
            token_latents.at[pl.ds(section * own_frames, own_frames)],
            half_send.at[n],
            half_recv.at[n],
            other,
            shard,
        )

    def mix_copy(n):
        to_section, to_shard = partner(n)
        return remote(
            mix_send.at[member_of(to_section, to_shard)],
            mix_recv.at[pl.ds(member * halves, halves)],
            mix_send_sem.at[n],
            mix_recv_sem.at[n],
            to_section,
            to_shard,
        )

    def lat_copy(n, slot):
        to_section, to_shard = partner(n)
        return remote(
            token_latents.at[pl.ds(first_of(to_section, to_shard), halves)],
            frame_latents.at[slot, section, shard],
            lat_send_sem.at[slot, n],
            lat_recv_sem.at[slot, n],
            to_section,
            to_shard,
        )

    def end_copy(n):
        other = flip(section, n)
        return remote(
            ends.at[:, pl.ds(other * own_frames, own_frames)],
            landed.at[:, section],
            end_send.at[n],
            end_recv.at[n],
            other,
            shard,
        )

    def start_all(make, count):
        for n in range(count - 1, 0, -1):
            make(n).start()

    def wait_all(make, count):
        for n in range(count - 1, 0, -1):
            make(n).wait()

    start_all(start_copy, shards)
    start_all(half_copy, sections)
    own_first = lax.rem(shard, team_shards) * halves // repeat
    for t in range(sections):
        frame_latents[0, t, shard] = start[t, pl.ds(own_first, halves)]
    token_latents[pl.ds(section * own_frames, own_frames)] = start[section]
    for copy in input_copies[1:5]:
        copy.wait()
    for slot in range(slots):
        table[slot] = level_table[levels[slot]]
        for row in (4, 7):
            table[slot, row : row + 1, :] = 1.0 + table[slot, row : row + 1, :]
    shift = table[own_slot, 0:1, :]
    scale = 1.0 + table[own_slot, 1:2, :]
    part_rows = 3 * part_width
    block = team_shards * piece
    part = jnp.concatenate(
        [
            pos[pl.ds(pl.multiple_of((t * shards + first) * piece, piece), block), :]
            for t, first in token_order
        ],
        axis=0,
    )
    part = part - jnp.mean(part, axis=-1, keepdims=True)

    def doubled(values):
        if halves == 1:
            return values
        left = lax.broadcasted_iota(jnp.int32, values.shape, 1) < asked
        turned = pltpu.roll(values, asked, 1)
        return jnp.concatenate(
            [jnp.where(left, values, turned), jnp.where(left, turned, values)], axis=1
        )

    centered_pos[...] = doubled(part.T)
    folding[0:tokens, :] = (part * scale).astype(bf16)
    part = embed[...] - jnp.mean(embed[...], axis=-1, keepdims=True)
    high = jnp.concatenate([part] * piece, axis=0).T.astype(bf16)
    centered_embed[...] = jnp.concatenate([high, high], axis=1)
    at = tokens
    for values in split(part * scale) + split(jnp.broadcast_to(shift, (channels, width))):
        folding[at : at + channels, :] = values
        at += channels
    input_copies[6].wait()
    for n in range(4):
        factor = math.log2(math.e) / math.sqrt(size) if n % 2 == 0 else 1.0
        gain_columns[n] = jnp.broadcast_to(gains[n : n + 1, :] * factor, (most, size)).T
    input_copies[5].wait()
    row = lax.broadcasted_iota(jnp.int32, (4 * channels, lanes + tokens), 0)
    lane = lax.broadcasted_iota(jnp.int32, (4 * channels, lanes + tokens), 1)
    of_embed = (row < 2 * channels) & (lane < lanes)
    of_embed = of_embed & (lax.rem(row, channels) == lax.rem(lane, channels))
    of_shift = (row >= 2 * channels) & (lane >= lanes) & (lax.rem(row, channels) == 0)
    pick = jnp.where(of_embed | of_shift, 1.0, 0.0).astype(bf16)
    for at in range(0, part_rows, part_width):
        both = nt_dot(spatial_in[at : at + part_width, :], folding[...])
        folded_pos[at : at + part_width, :] = doubled(both[:, 0:tokens])
        high, low = split(both[:, tokens:])
        both = jnp.dot(high, pick, preferred_element_type=f32) + jnp.dot(
            low, pick, preferred_element_type=f32
        )
        high = both[:, 0:lanes].astype(bf16)
        folded_embed[at : at + part_width, :] = jnp.concatenate([high, high], axis=1)
        folded_shift[at : at + part_width, :] = both[:, lanes:]
    piece_token = lax.broadcasted_iota(jnp.int32, (piece, lanes), 0)
    lane_token = lax.broadcasted_iota(jnp.int32, (piece, lanes), 1) // channels
    own_lanes = piece_token == lane_token
    high, low = split(embed[...])
    embed_halves[...] = jnp.concatenate(
        [high.astype(f32)] * (2 * piece) + [low.astype(f32)] * piece, axis=0
    ).astype(bf16)
    wait_all(start_copy, shards)
    wait_all(half_copy, sections)

    def spread_out(packed):
        spread = jnp.concatenate(
            [jnp.where(own_lanes, jnp.broadcast_to(row, (piece, lanes)), 0.0) for row in packed],
            axis=0,
        )
        return split(spread)

    def frame_row(n):
        home = n // piece
        return (home % sections * shards + home // sections) * piece + n % piece

    def step_body(step, carry):
        halved = spread_out(
            [
                frame_latents[lax.rem(step, 2), t, first + n, k]
                for order in range(0, len(token_order), sections)
                for k in range(halves)
                for t, first in token_order[order : order + sections]
                for n in range(team_shards)
            ]
        )
        spread = jnp.concatenate(halved, axis=1)
        squares = None
        chunk = width // 4
        for at in range(0, width, chunk):
            part = nt_dot(centered_embed[at : at + chunk, :], spread)
            part = part + centered_pos[at : at + chunk, :]
            part = jnp.sum(part * part, axis=0, keepdims=True)
            squares = part if squares is None else squares + part
        factor = lax.rsqrt(squares * (1.0 / width) + epsilon)
        for at in range(0, part_rows, part_width):
            count = query_rows if at == 0 else key_rows
            part = nt_dot(folded_embed[at : at + part_width, :], spread[0:count])
            part = (part + folded_pos[at : at + part_width, 0:count]) * factor[:, 0:count]
            for n in range(0, count, tokens):
                projected[at : at + part_width, n : n + tokens] = (
                    part[:, n : n + tokens] + folded_shift[at : at + part_width, :]
                ).astype(bf16)

        attend(
            projected,
            mixed,
            gain_columns.at[0:2],
            part_heads,
            size,
            query_rows,
            key_rows,
            piece,
            False,
        )
        results = (
            mixed[0:part_width, 0:query_rows].T.astype(f32).reshape(halves, team, piece, part_width)
        )
        for n in range(halves):
            mix_send[:, n] = results[n].astype(bf16)
        start_all(mix_copy, team)
        mix_recv[pl.ds(member * halves, halves)] = mix_send[member]

        token_pos = pos[pl.ds(pl.multiple_of(item * piece, piece), piece), :]
        high, low = spread_out([token_latents[n] for n in range(slots * frames)])
        base = jnp.dot(
            jnp.concatenate([high, low, high], axis=1),
            embed_halves[...],
            preferred_element_type=f32,
        )
        for n in range(slots * frames):
            hidden[n * piece : (n + 1) * piece, :] = (
                base[n * piece : (n + 1) * piece]
                + token_pos
                + pos[frame_row(n) : frame_row(n) + 1, :]
            )
        @pl.when(step == 0)
        def _():
            for copy in input_copies[9:]:
                copy.wait()
            temporal_turned[...] = temporal_in[...].T
            for copy in input_copies[7:9]:
                copy.wait()
            lines = packed(
                fresh_noise[...].reshape(steps * frames * channels, own_tokens), steps * frames
            )
            for n, line in enumerate(lines):
                for t in range(sections):
                    noise[n // frames, n % frames, t] = line[:, t * lanes : (t + 1) * lanes]
            high, low = split(final_weight[...])
            final_halves[...] = jnp.concatenate(
                [high.astype(f32)] * piece + [low.astype(f32)] * piece, axis=0
            ).T.astype(bf16)

        wait_all(mix_copy, team)
        branch = None
        arrived = mix_recv[...].astype(f32).reshape(
            slots * frames, repeat, piece, heads // repeat * size
        )
        for n in range(repeat):
            part = jnp.dot(
                arrived[:, n].reshape(rows, part_width).astype(bf16),
                spatial_out[n * part_width : (n + 1) * part_width, :],
                preferred_element_type=f32,
            )
            branch = part if branch is None else branch + part
        for slot in range(slots):
            at = slot * slab
            part = (
                hidden[at : at + slab, :]
                + table[slot, 2:3, :] * branch[at : at + slab]
            )
            hidden[at : at + slab, :] = part
            normed[at : at + slab, :] = (
                layer_norm(part) * table[slot, 4:5, :] + table[slot, 3:4, :]
            ).astype(bf16)
        projected[:, 0:rows] = (
            jnp.dot(normed[0:rows, :], temporal_turned[...], preferred_element_type=f32)
            .astype(bf16)
            .T
        )
        attend(projected, mixed, gain_columns.at[2:4], heads, size, rows, rows, piece, True)
        branch = jnp.dot(mixed[:, 0:rows].T, temporal_out[...], preferred_element_type=f32)
        for slot in range(slots):
            at = slot * slab
            part = hidden[at : at + slab, :] + table[slot, 5:6, :] * branch[at : at + slab]
            final = layer_norm(part) * table[slot, 7:8, :] + table[slot, 6:7, :]
            high, low = split(final)
            finals[at : at + slab, :] = high
            finals[rows + at : rows + at + slab, :] = low
        product = jnp.dot(finals[...], final_halves[...], preferred_element_type=f32)
        spread = (
            product[0:rows, 0:lanes] + product[0:rows, lanes : 2 * lanes] + product[rows:, 0:lanes]
        )
        for n in range(slots * frames):
            velocity = jnp.sum(
                jnp.where(own_lanes, spread[n * piece : (n + 1) * piece], 0.0),
                axis=0,
                keepdims=True,
            )
            slot = n // frames
            time = (levels[slot].astype(f32) + 1.0) / LEVELS
            before = (levels[slot - 1].astype(f32) + 1.0) / LEVELS if slot > 0 else 0.0
            old = token_latents[n]
            ends[1, n] = old - time * velocity
            if slot > 0:
                token_latents[n - frames] = old - (time - before) * velocity
        for n in range(frames):
            token_latents[(slots - 1) * frames + n] = noise[step, n, section]

        @pl.when(step < steps - 1)
        def _():
            slot = lax.rem(step + 1, 2)
            start_all(functools.partial(lat_copy, slot=slot), group)
            frame_latents[slot, section, shard] = token_latents[pl.ds(frame, halves)]
            wait_all(functools.partial(lat_copy, slot=slot), group)

        return carry

    lax.fori_loop(0, steps, step_body, 0)
    ends[0] = token_latents[...]
    start_all(end_copy, sections)
    landed[:, section] = ends[:, pl.ds(section * own_frames, own_frames)]
    wait_all(end_copy, sections)
    out[...] = landed[...]


def unpack(frames, landed, next_queue, denoised):
    _, sections, own_frames, _, lanes = landed.shape
    channels = next_queue.shape[2]
    piece = lanes // channels
    own_tokens = sections * piece
    piece_token = lax.broadcasted_iota(jnp.int32, (piece, lanes), 0)
    own_lanes = piece_token == lax.broadcasted_iota(jnp.int32, (piece, lanes), 1) // channels
    spread = jnp.concatenate(
        [
            jnp.where(own_lanes, jnp.broadcast_to(landed[k, t, n], (piece, lanes)), 0.0)
            for k in range(2)
            for n in range(own_frames)
            for t in range(sections)
        ],
        axis=0,
    )
    pick = jnp.where(
        lax.broadcasted_iota(jnp.int32, (channels, lanes), 0)
        == lax.rem(lax.broadcasted_iota(jnp.int32, (channels, lanes), 1), channels),
        1.0,
        0.0,
    ).astype(bf16)
    result = None
    for term in terms(spread):
        part = nt_dot(pick, term)
        result = part if result is None else result + part
    for k, target in enumerate((next_queue, denoised)):
        for n in range(own_frames):
            at = (k * own_frames + n) * own_tokens
            target[n // frames, n % frames] = result[:, at : at + own_tokens]


def per_device(
    queue_latents,
    fresh_noise,
    slot_levels,
    level_table,
    embed_weight,
    spatial_in,
    spatial_out,
    temporal_in,
    temporal_out,
    norm_gains,
    final_weight,
):
    blocks, frames, channels, tokens = queue_latents.shape
    steps, slots = fresh_noise.shape[0], slot_levels.shape[0]
    sections, shards = lax.axis_size("tm"), lax.axis_size("space")
    width, size = embed_weight.shape[1], norm_gains.shape[1]
    inner = spatial_out.shape[0]
    heads = inner // size
    group = sections * shards
    repeat = group // (slots * frames)
    halves = 2 if repeat == 1 and frames % 2 == 0 and shards % 2 == 0 else 1
    piece = tokens // sections
    own_frames = blocks * frames
    assert repeat * slots * frames == group and heads % repeat == 0
    assert piece * sections == tokens and own_frames * sections == slots * frames
    lanes = piece * channels
    spatial_in, temporal_in, final = spatial_in.T, temporal_in.T, final_weight.T
    part = inner // repeat
    if repeat > 1:
        which = lax.rem(lax.axis_index("space"), repeat)
        spatial_in = lax.dynamic_index_in_dim(
            spatial_in.reshape(3, repeat, part, width), which, axis=1, keepdims=False
        ).reshape(3 * part, width)
    rows = max(slots * frames * piece, halves * group * piece)
    cfg = dict(
        sections=sections,
        shards=shards,
        repeat=repeat,
        halves=halves,
        slots=slots,
        frames=frames,
        steps=steps,
        heads=heads,
        size=size,
        piece=piece,
    )
    vmem, anywhere = pl.BlockSpec(memory_space=pltpu.VMEM), pl.BlockSpec(memory_space=pl.ANY)
    dma = pltpu.SemaphoreType.DMA
    landed = pl.pallas_call(
        functools.partial(kernel, cfg),
        out_shape=pltpu.VMEM((2, sections, own_frames, 1, lanes), f32),
        in_specs=[anywhere] * 12,
        out_specs=vmem,
        scratch_shapes=[
            pltpu.SMEM(slot_levels.shape, jnp.int32),
            pltpu.VMEM(queue_latents.shape, f32),
            pltpu.VMEM(fresh_noise.shape, f32),
            pltpu.VMEM(embed_weight.shape, f32),
            pltpu.VMEM(final.shape, f32),
            pltpu.VMEM(norm_gains.shape, f32),
            pltpu.VMEM((sections, own_frames, 1, lanes), f32),
            pltpu.VMEM((steps, frames, sections, 1, lanes), f32),
            pltpu.VMEM(level_table.shape, f32),
            pltpu.VMEM((group * piece, width), f32),
            pltpu.VMEM((4, size, rows), f32),
            pltpu.VMEM((2, sections, shards, halves, 1, lanes), f32),
            pltpu.VMEM((slots * frames, 1, lanes), f32),
            pltpu.VMEM((group // halves, halves, piece, part), bf16),
            pltpu.VMEM((group, piece, part), bf16),
            pltpu.VMEM((slots, level_table.shape[1], width), f32),
            pltpu.VMEM((slots * frames * piece, width), f32),
            pltpu.VMEM((rows, width), bf16),
            pltpu.VMEM((2 * slots * frames * piece, width), bf16),
            pltpu.VMEM((3 * lanes, width), bf16),
            pltpu.VMEM((width, 2 * lanes), bf16),
            pltpu.VMEM((2, slots * frames, 1, lanes), f32),
            pltpu.VMEM((2, sections, own_frames, 1, lanes), f32),
            pltpu.VMEM(spatial_in.shape, bf16),
            pltpu.VMEM(spatial_out.shape, bf16),
            pltpu.VMEM(temporal_in.shape, bf16),
            pltpu.VMEM(temporal_out.shape, bf16),
            pltpu.VMEM(temporal_in.shape[::-1], bf16),
            pltpu.VMEM((width, halves * group * piece), f32),
            pltpu.VMEM((width, 2 * lanes), bf16),
            pltpu.VMEM((3 * part, 2 * lanes), bf16),
            pltpu.VMEM((3 * part, halves * group * piece), f32),
            pltpu.VMEM((3 * part, group * piece), f32),
            pltpu.VMEM((group * piece + 4 * channels, width), bf16),
            pltpu.VMEM((3 * inner, rows), bf16),
            pltpu.VMEM((inner, rows), bf16),
            dma((12,)),
            dma((shards,)),
            dma((shards,)),
            dma((sections,)),
            dma((sections,)),
            dma((group,)),
            dma((group,)),
            dma((2, group)),
            dma((2, group)),
            dma((sections,)),
            dma((sections,)),
        ],
        compiler_params=pltpu.CompilerParams(
            collective_id=0, has_side_effects=True, vmem_limit_bytes=60 * 1024 * 1024
        ),
    )(
        slot_levels,
        queue_latents,
        fresh_noise,
        embed_weight,
        final,
        norm_gains,
        level_table,
        jnp.asarray(
            sincos(group * piece, width)
            .reshape(shards, sections, piece, width)
            .swapaxes(0, 1)
            .reshape(group * piece, width)
        ),
        spatial_in,
        spatial_out,
        temporal_in,
        temporal_out,
    )
    return pl.pallas_call(
        functools.partial(unpack, frames),
        out_shape=(jax.ShapeDtypeStruct(queue_latents.shape, f32),) * 2,
        in_specs=[vmem],
        out_specs=(vmem, vmem),
    )(pltpu.with_memory_space_constraint(landed, pltpu.VMEM))


def solution(mesh):
    own = P(("clip", "tm"), None, None, "space")
    return jax.shard_map(
        per_device,
        mesh=mesh,
        in_specs=(own, P("clip", None, None, "space"), P("clip")) + (P(),) * 8,
        out_specs=(own, own),
        check_vma=False,
    )
```

```python
import functools
import math

import jax
import jax.numpy as jnp
import numpy as np
from jax import lax
from jax.experimental import pallas as pl
from jax.experimental.pallas import tpu as pltpu
from jax.sharding import PartitionSpec as P

LEVELS = 16
epsilon = 1e-06
f32 = jnp.float32
bf16 = jnp.bfloat16


def sincos(count, width):
    half = width // 2
    rates = np.exp(-np.log(np.float32(10000.0)) * np.arange(half, dtype=np.float32) / np.float32(half))
    angles = np.arange(count, dtype=np.float32)[:, None] * rates[None, :].astype(np.float32)
    return np.concatenate([np.sin(angles), np.cos(angles)], axis=-1).astype(np.float32)


def layer_norm(values):
    centered = values - jnp.mean(values, axis=-1, keepdims=True)
    return centered * lax.rsqrt(jnp.mean(centered * centered, axis=-1, keepdims=True) + epsilon)


def split(values):
    high = values.astype(bf16)
    return high, (values - high.astype(f32)).astype(bf16)


def terms(values):
    high = values.astype(bf16)
    rest = values - high.astype(f32)
    middle = rest.astype(bf16)
    return high, middle, (rest - middle.astype(f32)).astype(bf16)


def attend(projected, mixed, gains, heads, size, rows, keys_count, piece, masked):
    inner = heads * size

    def head_normed(at, gain, count):
        values = projected[at : at + size, 0:count].astype(f32)
        mean = jnp.sum(values * values, axis=0, keepdims=True) * (1.0 / size)
        return (values * lax.rsqrt(mean + epsilon) * gains[gain, :, 0:count]).astype(bf16)

    half = rows // 2
    if masked:
        row = lax.rem(lax.broadcasted_iota(jnp.int32, (piece, rows), 0), piece)
        own = row == lax.rem(lax.broadcasted_iota(jnp.int32, (piece, rows), 1), piece)
        keep = jnp.concatenate([jnp.where(own, 1.0, 0.0)] * (rows // piece), axis=0).astype(bf16)
    elif keys_count > rows:
        left = lax.broadcasted_iota(jnp.int32, (half, rows), 1) < half
        keep_left = jnp.where(left, 1.0, 0.0).astype(bf16)
        keep_right = jnp.where(left, 0.0, 1.0).astype(bf16)
    for at in range(0, inner, size):
        queries = head_normed(at, 0, rows)
        keys = head_normed(inner + at, 1, keys_count)
        values = projected[2 * inner + at : 2 * inner + at + size, 0:keys_count]
        scores = lax.dot_general(
            keys, queries, (((0,), (0,)), ((), ())), preferred_element_type=f32
        )
        if keys_count > rows:
            scores = jnp.concatenate(
                [
                    jnp.where(left, scores[n : n + half], scores[n + half : n + rows])
                    for n in range(0, keys_count, rows)
                ],
                axis=0,
            )
        weights = jnp.exp2(scores)
        rounded = weights.astype(bf16)
        if masked:
            totals = jnp.sum(weights.reshape(rows // piece, piece, rows), axis=0)
            totals = jnp.sum(jnp.where(own, totals, 0.0), axis=0, keepdims=True)
            rounded = rounded * keep
        else:
            totals = jnp.sum(weights, axis=0, keepdims=True)
            if keys_count > rows:
                parts = []
                for n in range(0, rows, half):
                    part = rounded[n : n + half]
                    parts += [part * keep_left, part * keep_right]
                rounded = jnp.concatenate(parts, axis=0)
        total = jnp.dot(values, rounded, preferred_element_type=f32)
        mixed[at : at + size, 0:rows] = (total * (1.0 / totals)).astype(bf16)


def nt_dot(left, right):
    return lax.dot_general(left, right, (((1,), (1,)), ((), ())), preferred_element_type=f32)


def kernel(
    cfg,
    levels_hbm,
    queue_latents_hbm,
    fresh_noise_hbm,
    embed_hbm,
    final_weight_hbm,
    gains_hbm,
    level_table_hbm,
    pos_hbm,
    spatial_in_hbm,
    spatial_out_hbm,
    temporal_in_hbm,
    temporal_out_hbm,
    out,
    levels,
    queue_latents,
    fresh_noise,
    embed,
    final_weight,
    gains,
    start,
    noise,
    level_table,
    pos,
    gain_columns,
    frame_latents,
    token_latents,
    mix_send,
    mix_recv,
    table,
    hidden,
    normed,
    finals,
    embed_halves,
    final_halves,
    ends,
    landed,
    spatial_in,
    spatial_out,
    temporal_in,
    temporal_out,
    temporal_turned,
    centered_pos,
    centered_embed,
    folded_embed,
    folded_pos,
    folded_shift,
    folding,
    projected,
    mixed,
    weight_sem,
    start_send,
    start_recv,
    half_send,
    half_recv,
    mix_send_sem,
    mix_recv_sem,
    lat_send_sem,
    lat_recv_sem,
    end_send,
    end_recv,
):
    sections, shards, repeat = cfg["sections"], cfg["shards"], cfg["repeat"]
    halves = cfg["halves"]
    slots, frames, steps = cfg["slots"], cfg["frames"], cfg["steps"]
    heads, size, piece = cfg["heads"], cfg["size"], cfg["piece"]
    channels, width = embed.shape
    lanes = piece * channels
    group = sections * shards
    own_frames = slots * frames // sections
    rows = slots * frames * piece
    slab = frames * piece
    tokens = group * piece
    team_shards = shards // halves
    team = sections * team_shards
    asked = tokens // halves
    query_rows, key_rows = halves * asked, halves * tokens
    most = max(rows, key_rows)
    part_heads = heads // repeat
    part_width = part_heads * size
    section, shard = lax.axis_index("tm"), lax.axis_index("space")
    item = section * shards + shard
    half = shard // team_shards

    def member_of(to_section, to_shard):
        return to_section * team_shards + lax.rem(to_shard, team_shards)

    def first_of(to_section, to_shard):
        return member_of(to_section, to_shard) * halves // repeat

    member = member_of(section, shard)
    frame = first_of(section, shard)
    own_slot = frame // frames
    token_order = [
        (t, lax.rem(half + n, halves) * team_shards)
        for n in range(halves)
        for t in range(sections)
    ]

    def flip(index, code):
        bit, other = 1, index
        while bit <= code:
            if code & bit:
                other = other + bit - 2 * bit * lax.rem(index // bit, 2)
            bit *= 2
        return other

    def partner(n):
        return flip(section, n % sections), flip(shard, n // sections)

    input_copies = [
        pltpu.make_async_copy(src, dst, weight_sem.at[n])
        for n, (src, dst) in enumerate(
            (
                (queue_latents_hbm, queue_latents),
                (levels_hbm, levels),
                (embed_hbm, embed),
                (level_table_hbm, level_table),
                (pos_hbm, pos),
                (spatial_in_hbm, spatial_in),
                (gains_hbm, gains),
                (fresh_noise_hbm, fresh_noise),
                (final_weight_hbm, final_weight),
                (temporal_in_hbm, temporal_in),
                (spatial_out_hbm, spatial_out),
                (temporal_out_hbm, temporal_out),
            )
        )
    ]
    input_copies[0].start()
    partners = range(group - 1, 0, -1)
    barrier = pltpu.get_barrier_semaphore()
    for n in partners:
        to_section, to_shard = partner(n)
        pl.semaphore_signal(
            barrier,
            inc=1,
            device_id={"tm": to_section, "space": to_shard},
            device_id_type=pl.DeviceIdType.MESH,
        )

    for n in (1, 2, 6, 7, 8, 3, 4, 5, 9, 10, 11):
        input_copies[n].start()

    def packed(latents, count):
        own_tokens = latents.shape[1]
        wide = sections * lanes
        token = lax.broadcasted_iota(jnp.int32, (own_tokens, wide), 0)
        lane = lax.broadcasted_iota(jnp.int32, (own_tokens, wide), 1)
        place = jnp.where(token == lane // channels, 1.0, 0.0).astype(bf16)
        spread = None
        for term in terms(latents):
            part = jnp.dot(term, place, preferred_element_type=f32)
            spread = part if spread is None else spread + part
        channel = lax.broadcasted_iota(jnp.int32, (channels, wide), 0)
        own = channel == lax.rem(lax.broadcasted_iota(jnp.int32, (channels, wide), 1), channels)
        return [
            jnp.sum(
                jnp.where(own, spread[n * channels : (n + 1) * channels], 0.0),
                axis=0,
                keepdims=True,
            )
            for n in range(count)
        ]

    own_tokens = sections * piece
    input_copies[0].wait()
    lines = packed(queue_latents[...].reshape(own_frames * channels, own_tokens), own_frames)
    for n, line in enumerate(lines):
        for t in range(sections):
            start[t, n] = line[:, t * lanes : (t + 1) * lanes]
    pl.semaphore_wait(barrier, group - 1)

    def remote(src, dst, send, recv, to_section, to_shard):
        return pltpu.make_async_remote_copy(
            src_ref=src,
            dst_ref=dst,
            send_sem=send,
            recv_sem=recv,
            device_id={"tm": to_section, "space": to_shard},
            device_id_type=pl.DeviceIdType.MESH,
        )

    def start_copy(n):
        other = flip(shard, n)
        return remote(
            start.at[:, pl.ds(lax.rem(other, team_shards) * halves // repeat, halves)],
            frame_latents.at[0, :, shard],
            start_send.at[n],
            start_recv.at[n],
            section,
            other,
        )

    def half_copy(n):
        other = flip(section, n)
        return remote(
            start.at[other],
            token_latents.at[pl.ds(section * own_frames, own_frames)],
            half_send.at[n],
            half_recv.at[n],
            other,
            shard,
        )

    def mix_copy(n):
        to_section, to_shard = partner(n)
        return remote(
            mix_send.at[member_of(to_section, to_shard)],
            mix_recv.at[pl.ds(member * halves, halves)],
            mix_send_sem.at[n],
            mix_recv_sem.at[n],
            to_section,
            to_shard,
        )

    def lat_copy(n, slot):
        to_section, to_shard = partner(n)
        return remote(
            token_latents.at[pl.ds(first_of(to_section, to_shard), halves)],
            frame_latents.at[slot, section, shard],
            lat_send_sem.at[slot, n],
            lat_recv_sem.at[slot, n],
            to_section,
            to_shard,
        )

    def end_copy(n):
        other = flip(section, n)
        return remote(
            ends.at[:, pl.ds(other * own_frames, own_frames)],
            landed.at[:, section],
            end_send.at[n],
            end_recv.at[n],
            other,
            shard,
        )

    def start_all(make, count):
        for n in range(count - 1, 0, -1):
            make(n).start()

    def wait_all(make, count):
        for n in range(count - 1, 0, -1):
            make(n).wait()

    start_all(start_copy, shards)
    start_all(half_copy, sections)
    own_first = lax.rem(shard, team_shards) * halves // repeat
    for t in range(sections):
        frame_latents[0, t, shard] = start[t, pl.ds(own_first, halves)]
    token_latents[pl.ds(section * own_frames, own_frames)] = start[section]
    for copy in input_copies[1:5]:
        copy.wait()
    for slot in range(slots):
        table[slot] = level_table[levels[slot]]
        for row in (4, 7):
            table[slot, row : row + 1, :] = 1.0 + table[slot, row : row + 1, :]
    shift = table[own_slot, 0:1, :]
    scale = 1.0 + table[own_slot, 1:2, :]
    part_rows = 3 * part_width
    block = team_shards * piece
    part = jnp.concatenate(
        [
            pos[pl.ds(pl.multiple_of((t * shards + first) * piece, piece), block), :]
            for t, first in token_order
        ],
        axis=0,
    )
    part = part - jnp.mean(part, axis=-1, keepdims=True)

    def doubled(values):
        if halves == 1:
            return values
        left = lax.broadcasted_iota(jnp.int32, values.shape, 1) < asked
        turned = pltpu.roll(values, asked, 1)
        return jnp.concatenate(
            [jnp.where(left, values, turned), jnp.where(left, turned, values)], axis=1
        )

    centered_pos[...] = doubled(part.T)
    folding[0:tokens, :] = (part * scale).astype(bf16)
    part = embed[...] - jnp.mean(embed[...], axis=-1, keepdims=True)
    high = jnp.concatenate([part] * piece, axis=0).T.astype(bf16)
    centered_embed[...] = jnp.concatenate([high, high], axis=1)
    at = tokens
    for values in split(part * scale) + split(jnp.broadcast_to(shift, (channels, width))):
        folding[at : at + channels, :] = values
        at += channels
    input_copies[6].wait()
    for n in range(2):
        factor = math.log2(math.e) / math.sqrt(size) if n % 2 == 0 else 1.0
        gain_columns[n] = jnp.broadcast_to(gains[n : n + 1, :] * factor, (most, size)).T
    input_copies[5].wait()
    row = lax.broadcasted_iota(jnp.int32, (4 * channels, lanes + tokens), 0)
    lane = lax.broadcasted_iota(jnp.int32, (4 * channels, lanes + tokens), 1)
    of_embed = (row < 2 * channels) & (lane < lanes)
    of_embed = of_embed & (lax.rem(row, channels) == lax.rem(lane, channels))
    of_shift = (row >= 2 * channels) & (lane >= lanes) & (lax.rem(row, channels) == 0)
    pick = jnp.where(of_embed | of_shift, 1.0, 0.0).astype(bf16)
    for at in range(0, part_rows, part_width):
        both = nt_dot(spatial_in[at : at + part_width, :], folding[...])
        folded_pos[at : at + part_width, :] = doubled(both[:, 0:tokens])
        high, low = split(both[:, tokens:])
        both = jnp.dot(high, pick, preferred_element_type=f32) + jnp.dot(
            low, pick, preferred_element_type=f32
        )
        high = both[:, 0:lanes].astype(bf16)
        folded_embed[at : at + part_width, :] = jnp.concatenate([high, high], axis=1)
        folded_shift[at : at + part_width, :] = both[:, lanes:]
    piece_token = lax.broadcasted_iota(jnp.int32, (piece, lanes), 0)
    lane_token = lax.broadcasted_iota(jnp.int32, (piece, lanes), 1) // channels
    own_lanes = piece_token == lane_token
    wait_all(start_copy, shards)
    wait_all(half_copy, sections)

    def spread_out(packed):
        spread = jnp.concatenate(
            [jnp.where(own_lanes, jnp.broadcast_to(row, (piece, lanes)), 0.0) for row in packed],
            axis=0,
        )
        return split(spread)

    def frame_row(n):
        home = n // piece
        return (home % sections * shards + home // sections) * piece + n % piece

    def step_body(step, carry):
        halved = spread_out(
            [
                frame_latents[lax.rem(step, 2), t, first + n, k]
                for order in range(0, len(token_order), sections)
                for k in range(halves)
                for t, first in token_order[order : order + sections]
                for n in range(team_shards)
            ]
        )
        spread = jnp.concatenate(halved, axis=1)
        squares = None
        chunk = width // 4
        for at in range(0, width, chunk):
            part = nt_dot(centered_embed[at : at + chunk, :], spread)
            part = part + centered_pos[at : at + chunk, :]
            part = jnp.sum(part * part, axis=0, keepdims=True)
            squares = part if squares is None else squares + part
        factor = lax.rsqrt(squares * (1.0 / width) + epsilon)
        for at in range(0, part_rows, part_width):
            count = query_rows if at == 0 else key_rows
            part = nt_dot(folded_embed[at : at + part_width, :], spread[0:count])
            part = (part + folded_pos[at : at + part_width, 0:count]) * factor[:, 0:count]
            for n in range(0, count, tokens):
                projected[at : at + part_width, n : n + tokens] = (
                    part[:, n : n + tokens] + folded_shift[at : at + part_width, :]
                ).astype(bf16)

        attend(
            projected,
            mixed,
            gain_columns.at[0:2],
            part_heads,
            size,
            query_rows,
            key_rows,
            piece,
            False,
        )
        results = mixed[0:part_width, 0:query_rows].T.reshape(halves, team, piece, part_width)
        for n in range(halves):
            mix_send[:, n] = results[n]
        start_all(mix_copy, team)
        mix_recv[pl.ds(member * halves, halves)] = mix_send[member]

        @pl.when(step == 0)
        def _():
            for n in range(2, 4):
                factor = math.log2(math.e) / math.sqrt(size) if n % 2 == 0 else 1.0
                gain_columns[n] = jnp.broadcast_to(gains[n : n + 1, :] * factor, (most, size)).T
            high, low = split(embed[...])
            embed_halves[...] = jnp.concatenate(
                [high.astype(f32)] * (2 * piece) + [low.astype(f32)] * piece, axis=0
            ).astype(bf16)

        token_pos = pos[pl.ds(pl.multiple_of(item * piece, piece), piece), :]
        high, low = spread_out([token_latents[n] for n in range(slots * frames)])
        base = jnp.dot(
            jnp.concatenate([high, low, high], axis=1),
            embed_halves[...],
            preferred_element_type=f32,
        )
        for n in range(slots * frames):
            hidden[n * piece : (n + 1) * piece, :] = (
                base[n * piece : (n + 1) * piece]
                + token_pos
                + pos[frame_row(n) : frame_row(n) + 1, :]
            )
        @pl.when(step == 0)
        def _():
            for copy in input_copies[9:]:
                copy.wait()
            temporal_turned[...] = temporal_in[...].T
            for copy in input_copies[7:9]:
                copy.wait()
            lines = packed(
                fresh_noise[...].reshape(steps * frames * channels, own_tokens), steps * frames
            )
            for n, line in enumerate(lines):
                for t in range(sections):
                    noise[n // frames, n % frames, t] = line[:, t * lanes : (t + 1) * lanes]
            high, low = split(final_weight[...])
            final_halves[...] = jnp.concatenate(
                [high.astype(f32)] * piece + [low.astype(f32)] * piece, axis=0
            ).T.astype(bf16)

        wait_all(mix_copy, team)
        branch = None
        arrived = mix_recv[...].reshape(slots * frames, repeat, piece, part_width)
        for n in range(repeat):
            part = jnp.dot(
                arrived[:, n].reshape(rows, part_width),
                spatial_out[n * part_width : (n + 1) * part_width, :],
                preferred_element_type=f32,
            )
            branch = part if branch is None else branch + part
        for slot in range(slots):
            at = slot * slab
            part = (
                hidden[at : at + slab, :]
                + table[slot, 2:3, :] * branch[at : at + slab]
            )
            hidden[at : at + slab, :] = part
            normed[at : at + slab, :] = (
                layer_norm(part) * table[slot, 4:5, :] + table[slot, 3:4, :]
            ).astype(bf16)
        projected[:, 0:rows] = (
            jnp.dot(normed[0:rows, :], temporal_turned[...], preferred_element_type=f32)
            .astype(bf16)
            .T
        )
        attend(projected, mixed, gain_columns.at[2:4], heads, size, rows, rows, piece, True)
        branch = jnp.dot(mixed[:, 0:rows].T, temporal_out[...], preferred_element_type=f32)
        for slot in range(slots):
            at = slot * slab
            part = hidden[at : at + slab, :] + table[slot, 5:6, :] * branch[at : at + slab]
            final = layer_norm(part) * table[slot, 7:8, :] + table[slot, 6:7, :]
            high, low = split(final)
            finals[at : at + slab, :] = high
            finals[rows + at : rows + at + slab, :] = low
        product = jnp.dot(finals[...], final_halves[...], preferred_element_type=f32)
        spread = (
            product[0:rows, 0:lanes] + product[0:rows, lanes : 2 * lanes] + product[rows:, 0:lanes]
        )
        for n in range(slots * frames):
            velocity = jnp.sum(
                jnp.where(own_lanes, spread[n * piece : (n + 1) * piece], 0.0),
                axis=0,
                keepdims=True,
            )
            slot = n // frames
            time = (levels[slot].astype(f32) + 1.0) / LEVELS
            before = (levels[slot - 1].astype(f32) + 1.0) / LEVELS if slot > 0 else 0.0
            old = token_latents[n]
            ends[1, n] = old - time * velocity
            if slot > 0:
                token_latents[n - frames] = old - (time - before) * velocity
        for n in range(frames):
            token_latents[(slots - 1) * frames + n] = noise[step, n, section]

        @pl.when(step < steps - 1)
        def _():
            slot = lax.rem(step + 1, 2)
            start_all(functools.partial(lat_copy, slot=slot), group)
            frame_latents[slot, section, shard] = token_latents[pl.ds(frame, halves)]
            wait_all(functools.partial(lat_copy, slot=slot), group)

        return carry

    lax.fori_loop(0, steps, step_body, 0)
    ends[0] = token_latents[...]
    start_all(end_copy, sections)
    landed[:, section] = ends[:, pl.ds(section * own_frames, own_frames)]
    wait_all(end_copy, sections)
    out[...] = landed[...]


def unpack(frames, landed, next_queue, denoised):
    _, sections, own_frames, _, lanes = landed.shape
    channels = next_queue.shape[2]
    piece = lanes // channels
    own_tokens = sections * piece
    piece_token = lax.broadcasted_iota(jnp.int32, (piece, lanes), 0)
    own_lanes = piece_token == lax.broadcasted_iota(jnp.int32, (piece, lanes), 1) // channels
    spread = jnp.concatenate(
        [
            jnp.where(own_lanes, jnp.broadcast_to(landed[k, t, n], (piece, lanes)), 0.0)
            for k in range(2)
            for n in range(own_frames)
            for t in range(sections)
        ],
        axis=0,
    )
    pick = jnp.where(
        lax.broadcasted_iota(jnp.int32, (channels, lanes), 0)
        == lax.rem(lax.broadcasted_iota(jnp.int32, (channels, lanes), 1), channels),
        1.0,
        0.0,
    ).astype(bf16)
    result = None
    for term in terms(spread):
        part = nt_dot(pick, term)
        result = part if result is None else result + part
    for k, target in enumerate((next_queue, denoised)):
        for n in range(own_frames):
            at = (k * own_frames + n) * own_tokens
            target[n // frames, n % frames] = result[:, at : at + own_tokens]


def per_device(
    queue_latents,
    fresh_noise,
    slot_levels,
    level_table,
    embed_weight,
    spatial_in,
    spatial_out,
    temporal_in,
    temporal_out,
    norm_gains,
    final_weight,
):
    blocks, frames, channels, tokens = queue_latents.shape
    steps, slots = fresh_noise.shape[0], slot_levels.shape[0]
    sections, shards = lax.axis_size("tm"), lax.axis_size("space")
    width, size = embed_weight.shape[1], norm_gains.shape[1]
    inner = spatial_out.shape[0]
    heads = inner // size
    group = sections * shards
    repeat = group // (slots * frames)
    halves = 2 if repeat == 1 and frames % 2 == 0 and shards % 2 == 0 else 1
    piece = tokens // sections
    own_frames = blocks * frames
    assert repeat * slots * frames == group and heads % repeat == 0
    assert piece * sections == tokens and own_frames * sections == slots * frames
    lanes = piece * channels
    spatial_in, temporal_in, final = spatial_in.T, temporal_in.T, final_weight.T
    part = inner // repeat
    if repeat > 1:
        which = lax.rem(lax.axis_index("space"), repeat)
        spatial_in = lax.dynamic_index_in_dim(
            spatial_in.reshape(3, repeat, part, width), which, axis=1, keepdims=False
        ).reshape(3 * part, width)
    rows = max(slots * frames * piece, halves * group * piece)
    cfg = dict(
        sections=sections,
        shards=shards,
        repeat=repeat,
        halves=halves,
        slots=slots,
        frames=frames,
        steps=steps,
        heads=heads,
        size=size,
        piece=piece,
    )
    vmem, anywhere = pl.BlockSpec(memory_space=pltpu.VMEM), pl.BlockSpec(memory_space=pl.ANY)
    dma = pltpu.SemaphoreType.DMA
    landed = pl.pallas_call(
        functools.partial(kernel, cfg),
        out_shape=pltpu.VMEM((2, sections, own_frames, 1, lanes), f32),
        in_specs=[anywhere] * 12,
        out_specs=vmem,
        scratch_shapes=[
            pltpu.SMEM(slot_levels.shape, jnp.int32),
            pltpu.VMEM(queue_latents.shape, f32),
            pltpu.VMEM(fresh_noise.shape, f32),
            pltpu.VMEM(embed_weight.shape, f32),
            pltpu.VMEM(final.shape, f32),
            pltpu.VMEM(norm_gains.shape, f32),
            pltpu.VMEM((sections, own_frames, 1, lanes), f32),
            pltpu.VMEM((steps, frames, sections, 1, lanes), f32),
            pltpu.VMEM(level_table.shape, f32),
            pltpu.VMEM((group * piece, width), f32),
            pltpu.VMEM((4, size, rows), f32),
            pltpu.VMEM((2, sections, shards, halves, 1, lanes), f32),
            pltpu.VMEM((slots * frames, 1, lanes), f32),
            pltpu.VMEM((group // halves, halves, piece, part), bf16),
            pltpu.VMEM((group, piece, part), bf16),
            pltpu.VMEM((slots, level_table.shape[1], width), f32),
            pltpu.VMEM((slots * frames * piece, width), f32),
            pltpu.VMEM((rows, width), bf16),
            pltpu.VMEM((2 * slots * frames * piece, width), bf16),
            pltpu.VMEM((3 * lanes, width), bf16),
            pltpu.VMEM((width, 2 * lanes), bf16),
            pltpu.VMEM((2, slots * frames, 1, lanes), f32),
            pltpu.VMEM((2, sections, own_frames, 1, lanes), f32),
            pltpu.VMEM(spatial_in.shape, bf16),
            pltpu.VMEM(spatial_out.shape, bf16),
            pltpu.VMEM(temporal_in.shape, bf16),
            pltpu.VMEM(temporal_out.shape, bf16),
            pltpu.VMEM(temporal_in.shape[::-1], bf16),
            pltpu.VMEM((width, halves * group * piece), f32),
            pltpu.VMEM((width, 2 * lanes), bf16),
            pltpu.VMEM((3 * part, 2 * lanes), bf16),
            pltpu.VMEM((3 * part, halves * group * piece), f32),
            pltpu.VMEM((3 * part, group * piece), f32),
            pltpu.VMEM((group * piece + 4 * channels, width), bf16),
            pltpu.VMEM((3 * inner, rows), bf16),
            pltpu.VMEM((inner, rows), bf16),
            dma((12,)),
            dma((shards,)),
            dma((shards,)),
            dma((sections,)),
            dma((sections,)),
            dma((group,)),
            dma((group,)),
            dma((2, group)),
            dma((2, group)),
            dma((sections,)),
            dma((sections,)),
        ],
        compiler_params=pltpu.CompilerParams(
            collective_id=0, has_side_effects=True, vmem_limit_bytes=60 * 1024 * 1024
        ),
    )(
        slot_levels,
        queue_latents,
        fresh_noise,
        embed_weight,
        final,
        norm_gains,
        level_table,
        jnp.asarray(
            sincos(group * piece, width)
            .reshape(shards, sections, piece, width)
            .swapaxes(0, 1)
            .reshape(group * piece, width)
        ),
        spatial_in,
        spatial_out,
        temporal_in,
        temporal_out,
    )
    return pl.pallas_call(
        functools.partial(unpack, frames),
        out_shape=(jax.ShapeDtypeStruct(queue_latents.shape, f32),) * 2,
        in_specs=[vmem],
        out_specs=(vmem, vmem),
    )(pltpu.with_memory_space_constraint(landed, pltpu.VMEM))


def solution(mesh):
    own = P(("clip", "tm"), None, None, "space")
    return jax.shard_map(
        per_device,
        mesh=mesh,
        in_specs=(own, P("clip", None, None, "space"), P("clip")) + (P(),) * 8,
        out_specs=(own, own),
        check_vma=False,
    )
```

```python
import functools
import math

import jax
import jax.numpy as jnp
import numpy as np
from jax import lax
from jax.experimental import pallas as pl
from jax.experimental.pallas import tpu as pltpu
from jax.sharding import PartitionSpec as P

LEVELS = 16
epsilon = 1e-06
f32 = jnp.float32
bf16 = jnp.bfloat16


def sincos(count, width):
    half = width // 2
    rates = np.exp(-np.log(np.float32(10000.0)) * np.arange(half, dtype=np.float32) / np.float32(half))
    angles = np.arange(count, dtype=np.float32)[:, None] * rates[None, :].astype(np.float32)
    return np.concatenate([np.sin(angles), np.cos(angles)], axis=-1).astype(np.float32)


def layer_norm(values):
    centered = values - jnp.mean(values, axis=-1, keepdims=True)
    return centered * lax.rsqrt(jnp.mean(centered * centered, axis=-1, keepdims=True) + epsilon)


def split(values):
    high = values.astype(bf16)
    return high, (values - high.astype(f32)).astype(bf16)


def terms(values):
    high = values.astype(bf16)
    rest = values - high.astype(f32)
    middle = rest.astype(bf16)
    return high, middle, (rest - middle.astype(f32)).astype(bf16)


def attend(projected, mixed, gains, heads, size, rows, keys_count, piece, masked):
    inner = heads * size

    def head_normed(at, gain, count):
        values = projected[at : at + size, 0:count].astype(f32)
        mean = jnp.sum(values * values, axis=0, keepdims=True) * (1.0 / size)
        return (values * lax.rsqrt(mean + epsilon) * gains[gain, :, 0:count]).astype(bf16)

    half = rows // 2
    if masked:
        row = lax.rem(lax.broadcasted_iota(jnp.int32, (piece, rows), 0), piece)
        own = row == lax.rem(lax.broadcasted_iota(jnp.int32, (piece, rows), 1), piece)
        keep = jnp.concatenate([jnp.where(own, 1.0, 0.0)] * (rows // piece), axis=0).astype(bf16)
    elif keys_count > rows:
        left = lax.broadcasted_iota(jnp.int32, (half, rows), 1) < half
        keep_left = jnp.where(left, 1.0, 0.0).astype(bf16)
        keep_right = jnp.where(left, 0.0, 1.0).astype(bf16)
    for at in range(0, inner, size):
        queries = head_normed(at, 0, rows)
        keys = head_normed(inner + at, 1, keys_count)
        values = projected[2 * inner + at : 2 * inner + at + size, 0:keys_count]
        scores = lax.dot_general(
            keys, queries, (((0,), (0,)), ((), ())), preferred_element_type=f32
        )
        if keys_count > rows:
            scores = jnp.concatenate(
                [
                    jnp.where(left, scores[n : n + half], scores[n + half : n + rows])
                    for n in range(0, keys_count, rows)
                ],
                axis=0,
            )
        weights = jnp.exp2(scores)
        rounded = weights.astype(bf16)
        if masked:
            totals = jnp.sum(weights.reshape(rows // piece, piece, rows), axis=0)
            totals = jnp.sum(jnp.where(own, totals, 0.0), axis=0, keepdims=True)
            rounded = rounded * keep
        else:
            totals = jnp.sum(weights, axis=0, keepdims=True)
            if keys_count > rows:
                parts = []
                for n in range(0, rows, half):
                    part = rounded[n : n + half]
                    parts += [part * keep_left, part * keep_right]
                rounded = jnp.concatenate(parts, axis=0)
        total = jnp.dot(values, rounded, preferred_element_type=f32)
        mixed[at : at + size, 0:rows] = (total * (1.0 / totals)).astype(bf16)


def nt_dot(left, right):
    return lax.dot_general(left, right, (((1,), (1,)), ((), ())), preferred_element_type=f32)


def kernel(
    cfg,
    levels_hbm,
    queue_latents_hbm,
    fresh_noise_hbm,
    embed_hbm,
    final_weight_hbm,
    gains_hbm,
    level_table_hbm,
    pos_hbm,
    spatial_in_hbm,
    spatial_out_hbm,
    temporal_in_hbm,
    temporal_out_hbm,
    out,
    levels,
    queue_latents,
    fresh_noise,
    embed,
    final_weight,
    gains,
    start,
    noise,
    level_table,
    pos,
    gain_columns,
    frame_latents,
    token_latents,
    mix_send,
    mix_recv,
    table,
    hidden,
    normed,
    finals,
    embed_halves,
    final_halves,
    ends,
    landed,
    spatial_in,
    spatial_out,
    temporal_in,
    temporal_out,
    temporal_turned,
    centered_pos,
    centered_embed,
    folded_embed,
    folded_pos,
    folded_shift,
    folding,
    projected,
    mixed,
    weight_sem,
    start_send,
    start_recv,
    half_send,
    half_recv,
    mix_send_sem,
    mix_recv_sem,
    lat_send_sem,
    lat_recv_sem,
    end_send,
    end_recv,
):
    sections, shards, repeat = cfg["sections"], cfg["shards"], cfg["repeat"]
    halves = cfg["halves"]
    slots, frames, steps = cfg["slots"], cfg["frames"], cfg["steps"]
    heads, size, piece = cfg["heads"], cfg["size"], cfg["piece"]
    channels, width = embed.shape
    lanes = piece * channels
    group = sections * shards
    own_frames = slots * frames // sections
    rows = slots * frames * piece
    slab = frames * piece
    tokens = group * piece
    team_shards = shards // halves
    team = sections * team_shards
    asked = tokens // halves
    query_rows, key_rows = halves * asked, halves * tokens
    most = max(rows, key_rows)
    part_heads = heads // repeat
    part_width = part_heads * size
    section, shard = lax.axis_index("tm"), lax.axis_index("space")
    item = section * shards + shard
    half = shard // team_shards

    def member_of(to_section, to_shard):
        return to_section * team_shards + lax.rem(to_shard, team_shards)

    def first_of(to_section, to_shard):
        return member_of(to_section, to_shard) * halves // repeat

    member = member_of(section, shard)
    frame = first_of(section, shard)
    own_slot = frame // frames
    token_order = [
        (t, lax.rem(half + n, halves) * team_shards)
        for n in range(halves)
        for t in range(sections)
    ]

    def flip(index, code):
        bit, other = 1, index
        while bit <= code:
            if code & bit:
                other = other + bit - 2 * bit * lax.rem(index // bit, 2)
            bit *= 2
        return other

    def partner(n):
        return flip(section, n % sections), flip(shard, n // sections)

    input_copies = [
        pltpu.make_async_copy(src, dst, weight_sem.at[n])
        for n, (src, dst) in enumerate(
            (
                (queue_latents_hbm, queue_latents),
                (levels_hbm, levels),
                (embed_hbm, embed),
                (level_table_hbm, level_table),
                (pos_hbm, pos),
                (spatial_in_hbm, spatial_in),
                (gains_hbm, gains),
                (fresh_noise_hbm, fresh_noise),
                (final_weight_hbm, final_weight),
                (temporal_in_hbm, temporal_in),
                (spatial_out_hbm, spatial_out),
                (temporal_out_hbm, temporal_out),
            )
        )
    ]
    input_copies[0].start()
    partners = range(group - 1, 0, -1)
    barrier = pltpu.get_barrier_semaphore()
    for n in partners:
        to_section, to_shard = partner(n)
        pl.semaphore_signal(
            barrier,
            inc=1,
            device_id={"tm": to_section, "space": to_shard},
            device_id_type=pl.DeviceIdType.MESH,
        )

    for n in (1, 2, 6, 7, 8, 3, 4, 5, 9, 10, 11):
        input_copies[n].start()

    def packed(latents, count):
        own_tokens = latents.shape[1]
        wide = sections * lanes
        token = lax.broadcasted_iota(jnp.int32, (own_tokens, wide), 0)
        lane = lax.broadcasted_iota(jnp.int32, (own_tokens, wide), 1)
        place = jnp.where(token == lane // channels, 1.0, 0.0).astype(bf16)
        spread = None
        for term in terms(latents):
            part = jnp.dot(term, place, preferred_element_type=f32)
            spread = part if spread is None else spread + part
        channel = lax.broadcasted_iota(jnp.int32, (channels, wide), 0)
        own = channel == lax.rem(lax.broadcasted_iota(jnp.int32, (channels, wide), 1), channels)
        return [
            jnp.sum(
                jnp.where(own, spread[n * channels : (n + 1) * channels], 0.0),
                axis=0,
                keepdims=True,
            )
            for n in range(count)
        ]

    own_tokens = sections * piece
    input_copies[0].wait()
    lines = packed(queue_latents[...].reshape(own_frames * channels, own_tokens), own_frames)
    for n, line in enumerate(lines):
        for t in range(sections):
            start[t, n] = line[:, t * lanes : (t + 1) * lanes]
    pl.semaphore_wait(barrier, group - 1)

    def remote(src, dst, send, recv, to_section, to_shard):
        return pltpu.make_async_remote_copy(
            src_ref=src,
            dst_ref=dst,
            send_sem=send,
            recv_sem=recv,
            device_id={"tm": to_section, "space": to_shard},
            device_id_type=pl.DeviceIdType.MESH,
        )

    def start_copy(n):
        other = flip(shard, n)
        return remote(
            start.at[:, pl.ds(lax.rem(other, team_shards) * halves // repeat, halves)],
            frame_latents.at[0, :, shard],
            start_send.at[n],
            start_recv.at[n],
            section,
            other,
        )

    def half_copy(n):
        other = flip(section, n)
        return remote(
            start.at[other],
            token_latents.at[pl.ds(section * own_frames, own_frames)],
            half_send.at[n],
            half_recv.at[n],
            other,
            shard,
        )

    def mix_copy(n):
        to_section, to_shard = partner(n)
        return remote(
            mix_send.at[member_of(to_section, to_shard)],
            mix_recv.at[pl.ds(member * halves, halves)],
            mix_send_sem.at[n],
            mix_recv_sem.at[n],
            to_section,
            to_shard,
        )

    def lat_copy(n, slot):
        to_section, to_shard = partner(n)
        return remote(
            token_latents.at[pl.ds(first_of(to_section, to_shard), halves)],
            frame_latents.at[slot, section, shard],
            lat_send_sem.at[slot, n],
            lat_recv_sem.at[slot, n],
            to_section,
            to_shard,
        )

    def end_copy(n):
        other = flip(section, n)
        return remote(
            ends.at[:, pl.ds(other * own_frames, own_frames)],
            landed.at[:, section],
            end_send.at[n],
            end_recv.at[n],
            other,
            shard,
        )

    def start_all(make, count):
        for n in range(count - 1, 0, -1):
            make(n).start()

    def wait_all(make, count):
        for n in range(count - 1, 0, -1):
            make(n).wait()

    start_all(start_copy, shards)
    start_all(half_copy, sections)
    own_first = lax.rem(shard, team_shards) * halves // repeat
    for t in range(sections):
        frame_latents[0, t, shard] = start[t, pl.ds(own_first, halves)]
    token_latents[pl.ds(section * own_frames, own_frames)] = start[section]
    for copy in input_copies[1:5]:
        copy.wait()
    for slot in range(slots):
        table[slot] = level_table[levels[slot]]
        for row in (4, 7):
            table[slot, row : row + 1, :] = 1.0 + table[slot, row : row + 1, :]
    shift = table[own_slot, 0:1, :]
    scale = 1.0 + table[own_slot, 1:2, :]
    part_rows = 3 * part_width
    block = team_shards * piece
    part = jnp.concatenate(
        [
            pos[pl.ds(pl.multiple_of((t * shards + first) * piece, piece), block), :]
            for t, first in token_order
        ],
        axis=0,
    )
    part = part - jnp.mean(part, axis=-1, keepdims=True)

    def doubled(values):
        if halves == 1:
            return values
        left = lax.broadcasted_iota(jnp.int32, values.shape, 1) < asked
        turned = pltpu.roll(values, asked, 1)
        return jnp.concatenate(
            [jnp.where(left, values, turned), jnp.where(left, turned, values)], axis=1
        )

    centered_pos[...] = doubled(part.T)
    folding[0:tokens, :] = (part * scale).astype(bf16)
    part = embed[...] - jnp.mean(embed[...], axis=-1, keepdims=True)
    high = jnp.concatenate([part] * piece, axis=0).T.astype(bf16)
    centered_embed[...] = jnp.concatenate([high, high], axis=1)
    at = tokens
    for values in split(part * scale) + split(jnp.broadcast_to(shift, (channels, width))):
        folding[at : at + channels, :] = values
        at += channels
    input_copies[6].wait()
    for n in range(4):
        factor = math.log2(math.e) / math.sqrt(size) if n % 2 == 0 else 1.0
        gain_columns[n] = jnp.broadcast_to(gains[n : n + 1, :] * factor, (most, size)).T
    input_copies[5].wait()
    row = lax.broadcasted_iota(jnp.int32, (4 * channels, lanes + tokens), 0)
    lane = lax.broadcasted_iota(jnp.int32, (4 * channels, lanes + tokens), 1)
    of_embed = (row < 2 * channels) & (lane < lanes)
    of_embed = of_embed & (lax.rem(row, channels) == lax.rem(lane, channels))
    of_shift = (row >= 2 * channels) & (lane >= lanes) & (lax.rem(row, channels) == 0)
    pick = jnp.where(of_embed | of_shift, 1.0, 0.0).astype(bf16)
    for at in range(0, part_rows, part_width):
        both = nt_dot(spatial_in[at : at + part_width, :], folding[...])
        folded_pos[at : at + part_width, :] = doubled(both[:, 0:tokens])
        high, low = split(both[:, tokens:])
        both = jnp.dot(high, pick, preferred_element_type=f32) + jnp.dot(
            low, pick, preferred_element_type=f32
        )
        high = both[:, 0:lanes].astype(bf16)
        folded_embed[at : at + part_width, :] = jnp.concatenate([high, high], axis=1)
        folded_shift[at : at + part_width, :] = both[:, lanes:]
    piece_token = lax.broadcasted_iota(jnp.int32, (piece, lanes), 0)
    lane_token = lax.broadcasted_iota(jnp.int32, (piece, lanes), 1) // channels
    own_lanes = piece_token == lane_token
    high, low = split(embed[...])
    embed_halves[...] = jnp.concatenate(
        [high.astype(f32)] * (2 * piece) + [low.astype(f32)] * piece, axis=0
    ).astype(bf16)
    wait_all(start_copy, shards)
    wait_all(half_copy, sections)

    def spread_out(packed):
        spread = jnp.concatenate(
            [jnp.where(own_lanes, jnp.broadcast_to(row, (piece, lanes)), 0.0) for row in packed],
            axis=0,
        )
        return split(spread)

    def frame_row(n):
        home = n // piece
        return (home % sections * shards + home // sections) * piece + n % piece

    def step_body(step, carry):
        halved = spread_out(
            [
                frame_latents[lax.rem(step, 2), t, first + n, k]
                for order in range(0, len(token_order), sections)
                for k in range(halves)
                for t, first in token_order[order : order + sections]
                for n in range(team_shards)
            ]
        )
        spread = jnp.concatenate(halved, axis=1)
        squares = None
        chunk = width // 4
        for at in range(0, width, chunk):
            part = nt_dot(centered_embed[at : at + chunk, :], spread)
            part = part + centered_pos[at : at + chunk, :]
            part = jnp.sum(part * part, axis=0, keepdims=True)
            squares = part if squares is None else squares + part
        factor = lax.rsqrt(squares * (1.0 / width) + epsilon)
        for at in range(0, part_rows, part_width):
            count = query_rows if at == 0 else key_rows
            part = nt_dot(folded_embed[at : at + part_width, :], spread[0:count])
            part = (part + folded_pos[at : at + part_width, 0:count]) * factor[:, 0:count]
            for n in range(0, count, tokens):
                projected[at : at + part_width, n : n + tokens] = (
                    part[:, n : n + tokens] + folded_shift[at : at + part_width, :]
                ).astype(bf16)

        attend(
            projected,
            mixed,
            gain_columns.at[0:2],
            part_heads,
            size,
            query_rows,
            key_rows,
            piece,
            False,
        )
        results = (
            mixed[0:part_width, 0:query_rows].T.astype(f32).reshape(halves, team, piece, part_width)
        )
        for n in range(halves):
            mix_send[:, n] = results[n].astype(bf16)
        start_all(mix_copy, team)
        mix_recv[pl.ds(member * halves, halves)] = mix_send[member]

        token_pos = pos[pl.ds(pl.multiple_of(item * piece, piece), piece), :]
        high, low = spread_out([token_latents[n] for n in range(slots * frames)])
        base = jnp.dot(
            jnp.concatenate([high, low, high], axis=1),
            embed_halves[...],
            preferred_element_type=f32,
        )
        for n in range(slots * frames):
            hidden[n * piece : (n + 1) * piece, :] = (
                base[n * piece : (n + 1) * piece]
                + token_pos
                + pos[frame_row(n) : frame_row(n) + 1, :]
            )
        @pl.when(step == 0)
        def _():
            for copy in input_copies[9:]:
                copy.wait()
            temporal_turned[...] = temporal_in[...].T
            for copy in input_copies[7:9]:
                copy.wait()
            lines = packed(
                fresh_noise[...].reshape(steps * frames * channels, own_tokens), steps * frames
            )
            for n, line in enumerate(lines):
                for t in range(sections):
                    noise[n // frames, n % frames, t] = line[:, t * lanes : (t + 1) * lanes]
            high, low = split(final_weight[...])
            final_halves[...] = jnp.concatenate(
                [high.astype(f32)] * piece + [low.astype(f32)] * piece, axis=0
            ).T.astype(bf16)

        wait_all(mix_copy, team)
        branch = None
        arrived = mix_recv[...].astype(f32).reshape(
            slots * frames, repeat, piece, heads // repeat * size
        )
        for n in range(repeat):
            part = jnp.dot(
                arrived[:, n].reshape(rows, part_width).astype(bf16),
                spatial_out[n * part_width : (n + 1) * part_width, :],
                preferred_element_type=f32,
            )
            branch = part if branch is None else branch + part
        for slot in range(slots):
            at = slot * slab
            part = (
                hidden[at : at + slab, :]
                + table[slot, 2:3, :] * branch[at : at + slab]
            )
            hidden[at : at + slab, :] = part
            normed[at : at + slab, :] = (
                layer_norm(part) * table[slot, 4:5, :] + table[slot, 3:4, :]
            ).astype(bf16)
        wide = temporal_turned.shape[1]
        for at in range(0, wide, 512):
            end = min(at + 512, wide)
            projected[at:end, 0:rows] = (
                jnp.dot(
                    normed[0:rows, :], temporal_turned[:, at:end], preferred_element_type=f32
                )
                .astype(bf16)
                .T
            )
        attend(projected, mixed, gain_columns.at[2:4], heads, size, rows, rows, piece, True)
        branch = jnp.dot(mixed[:, 0:rows].T, temporal_out[...], preferred_element_type=f32)
        for slot in range(slots):
            at = slot * slab
            part = hidden[at : at + slab, :] + table[slot, 5:6, :] * branch[at : at + slab]
            final = layer_norm(part) * table[slot, 7:8, :] + table[slot, 6:7, :]
            high, low = split(final)
            finals[at : at + slab, :] = high
            finals[rows + at : rows + at + slab, :] = low
        product = jnp.dot(finals[...], final_halves[...], preferred_element_type=f32)
        spread = (
            product[0:rows, 0:lanes] + product[0:rows, lanes : 2 * lanes] + product[rows:, 0:lanes]
        )
        for n in range(slots * frames):
            velocity = jnp.sum(
                jnp.where(own_lanes, spread[n * piece : (n + 1) * piece], 0.0),
                axis=0,
                keepdims=True,
            )
            slot = n // frames
            time = (levels[slot].astype(f32) + 1.0) / LEVELS
            before = (levels[slot - 1].astype(f32) + 1.0) / LEVELS if slot > 0 else 0.0
            old = token_latents[n]
            ends[1, n] = old - time * velocity
            if slot > 0:
                token_latents[n - frames] = old - (time - before) * velocity
        for n in range(frames):
            token_latents[(slots - 1) * frames + n] = noise[step, n, section]

        @pl.when(step < steps - 1)
        def _():
            slot = lax.rem(step + 1, 2)
            start_all(functools.partial(lat_copy, slot=slot), group)
            frame_latents[slot, section, shard] = token_latents[pl.ds(frame, halves)]
            wait_all(functools.partial(lat_copy, slot=slot), group)

        return carry

    lax.fori_loop(0, steps, step_body, 0)
    ends[0] = token_latents[...]
    start_all(end_copy, sections)
    landed[:, section] = ends[:, pl.ds(section * own_frames, own_frames)]
    wait_all(end_copy, sections)
    out[...] = landed[...]


def unpack(frames, landed, next_queue, denoised):
    _, sections, own_frames, _, lanes = landed.shape
    channels = next_queue.shape[2]
    piece = lanes // channels
    own_tokens = sections * piece
    piece_token = lax.broadcasted_iota(jnp.int32, (piece, lanes), 0)
    own_lanes = piece_token == lax.broadcasted_iota(jnp.int32, (piece, lanes), 1) // channels
    spread = jnp.concatenate(
        [
            jnp.where(own_lanes, jnp.broadcast_to(landed[k, t, n], (piece, lanes)), 0.0)
            for k in range(2)
            for n in range(own_frames)
            for t in range(sections)
        ],
        axis=0,
    )
    pick = jnp.where(
        lax.broadcasted_iota(jnp.int32, (channels, lanes), 0)
        == lax.rem(lax.broadcasted_iota(jnp.int32, (channels, lanes), 1), channels),
        1.0,
        0.0,
    ).astype(bf16)
    result = None
    for term in terms(spread):
        part = nt_dot(pick, term)
        result = part if result is None else result + part
    for k, target in enumerate((next_queue, denoised)):
        for n in range(own_frames):
            at = (k * own_frames + n) * own_tokens
            target[n // frames, n % frames] = result[:, at : at + own_tokens]


def per_device(
    queue_latents,
    fresh_noise,
    slot_levels,
    level_table,
    embed_weight,
    spatial_in,
    spatial_out,
    temporal_in,
    temporal_out,
    norm_gains,
    final_weight,
):
    blocks, frames, channels, tokens = queue_latents.shape
    steps, slots = fresh_noise.shape[0], slot_levels.shape[0]
    sections, shards = lax.axis_size("tm"), lax.axis_size("space")
    width, size = embed_weight.shape[1], norm_gains.shape[1]
    inner = spatial_out.shape[0]
    heads = inner // size
    group = sections * shards
    repeat = group // (slots * frames)
    halves = 2 if repeat == 1 and frames % 2 == 0 and shards % 2 == 0 else 1
    piece = tokens // sections
    own_frames = blocks * frames
    assert repeat * slots * frames == group and heads % repeat == 0
    assert piece * sections == tokens and own_frames * sections == slots * frames
    lanes = piece * channels
    spatial_in, temporal_in, final = spatial_in.T, temporal_in.T, final_weight.T
    part = inner // repeat
    if repeat > 1:
        which = lax.rem(lax.axis_index("space"), repeat)
        spatial_in = lax.dynamic_index_in_dim(
            spatial_in.reshape(3, repeat, part, width), which, axis=1, keepdims=False
        ).reshape(3 * part, width)
    rows = max(slots * frames * piece, halves * group * piece)
    cfg = dict(
        sections=sections,
        shards=shards,
        repeat=repeat,
        halves=halves,
        slots=slots,
        frames=frames,
        steps=steps,
        heads=heads,
        size=size,
        piece=piece,
    )
    vmem, anywhere = pl.BlockSpec(memory_space=pltpu.VMEM), pl.BlockSpec(memory_space=pl.ANY)
    dma = pltpu.SemaphoreType.DMA
    landed = pl.pallas_call(
        functools.partial(kernel, cfg),
        out_shape=pltpu.VMEM((2, sections, own_frames, 1, lanes), f32),
        in_specs=[anywhere] * 12,
        out_specs=vmem,
        scratch_shapes=[
            pltpu.SMEM(slot_levels.shape, jnp.int32),
            pltpu.VMEM(queue_latents.shape, f32),
            pltpu.VMEM(fresh_noise.shape, f32),
            pltpu.VMEM(embed_weight.shape, f32),
            pltpu.VMEM(final.shape, f32),
            pltpu.VMEM(norm_gains.shape, f32),
            pltpu.VMEM((sections, own_frames, 1, lanes), f32),
            pltpu.VMEM((steps, frames, sections, 1, lanes), f32),
            pltpu.VMEM(level_table.shape, f32),
            pltpu.VMEM((group * piece, width), f32),
            pltpu.VMEM((4, size, rows), f32),
            pltpu.VMEM((2, sections, shards, halves, 1, lanes), f32),
            pltpu.VMEM((slots * frames, 1, lanes), f32),
            pltpu.VMEM((group // halves, halves, piece, part), bf16),
            pltpu.VMEM((group, piece, part), bf16),
            pltpu.VMEM((slots, level_table.shape[1], width), f32),
            pltpu.VMEM((slots * frames * piece, width), f32),
            pltpu.VMEM((rows, width), bf16),
            pltpu.VMEM((2 * slots * frames * piece, width), bf16),
            pltpu.VMEM((3 * lanes, width), bf16),
            pltpu.VMEM((width, 2 * lanes), bf16),
            pltpu.VMEM((2, slots * frames, 1, lanes), f32),
            pltpu.VMEM((2, sections, own_frames, 1, lanes), f32),
            pltpu.VMEM(spatial_in.shape, bf16),
            pltpu.VMEM(spatial_out.shape, bf16),
            pltpu.VMEM(temporal_in.shape, bf16),
            pltpu.VMEM(temporal_out.shape, bf16),
            pltpu.VMEM(temporal_in.shape[::-1], bf16),
            pltpu.VMEM((width, halves * group * piece), f32),
            pltpu.VMEM((width, 2 * lanes), bf16),
            pltpu.VMEM((3 * part, 2 * lanes), bf16),
            pltpu.VMEM((3 * part, halves * group * piece), f32),
            pltpu.VMEM((3 * part, group * piece), f32),
            pltpu.VMEM((group * piece + 4 * channels, width), bf16),
            pltpu.VMEM((3 * inner, rows), bf16),
            pltpu.VMEM((inner, rows), bf16),
            dma((12,)),
            dma((shards,)),
            dma((shards,)),
            dma((sections,)),
            dma((sections,)),
            dma((group,)),
            dma((group,)),
            dma((2, group)),
            dma((2, group)),
            dma((sections,)),
            dma((sections,)),
        ],
        compiler_params=pltpu.CompilerParams(
            collective_id=0, has_side_effects=True, vmem_limit_bytes=60 * 1024 * 1024
        ),
    )(
        slot_levels,
        queue_latents,
        fresh_noise,
        embed_weight,
        final,
        norm_gains,
        level_table,
        jnp.asarray(
            sincos(group * piece, width)
            .reshape(shards, sections, piece, width)
            .swapaxes(0, 1)
            .reshape(group * piece, width)
        ),
        spatial_in,
        spatial_out,
        temporal_in,
        temporal_out,
    )
    return pl.pallas_call(
        functools.partial(unpack, frames),
        out_shape=(jax.ShapeDtypeStruct(queue_latents.shape, f32),) * 2,
        in_specs=[vmem],
        out_specs=(vmem, vmem),
    )(pltpu.with_memory_space_constraint(landed, pltpu.VMEM))


def solution(mesh):
    own = P(("clip", "tm"), None, None, "space")
    return jax.shard_map(
        per_device,
        mesh=mesh,
        in_specs=(own, P("clip", None, None, "space"), P("clip")) + (P(),) * 8,
        out_specs=(own, own),
        check_vma=False,
    )
```
